32 devices in a mesh: replica: 2 (over y), sky: 4 (over z), freq: 4 (over x, core).
Axes of the slice: x: 2, y: 2, z: 4, core: 2. Of those that a mesh axis runs over, the one named last changes fastest.
Arguments:
- lightcone: bfloat16 [128, 32, 8, 128], P(('replica', 'freq'), None, 'sky'), parts along dimension 0, may hold values from -6 to 6
- cotangent: bfloat16 [128, 32, 8, 128], P(('replica', 'freq'), None, 'sky'), parts along dimension 0, may hold values from -6 to 6
- conv_weight: bfloat16 [32, 288], replicated, may hold values from -0.375 to 0.375
- in_proj: float32 [32, 16], replicated, may hold values from -1 to 1
- out_proj: float32 [32, 16], replicated, may hold values from -0.5 to 0.5
- skip_gain: float32 [32], replicated, may hold values from -4 to 4
- decay: float32 [64, 512], P('freq'), may hold values from 0.4 to 1
Outputs:
- d_lightcone: bfloat16 [128, 32, 8, 128], P(('replica', 'freq'), None, 'sky'), parts along dimension 0
- d_conv: float32 [64, 288], P('replica'), parts along dimension 0
- d_in_proj: float32 [64, 16], P('replica'), parts along dimension 0
- d_out_proj: float32 [64, 16], P('replica'), parts along dimension 0
- d_skip: float32 [64], P('replica'), parts along dimension 0
The draws below stay inside these ranges and needn't reach their ends.
There are 2 independent parts, one for each index of `replica`. The reference program is written for one: setup_inputs(seed, part) draws one part's arguments, and reference() takes and returns one part's arrays. A program takes and returns all parts, laid end to end along the dimension named above; an argument that names none is the same for every part. Nothing has to cross between parts.
All inputs are finite; a program needn't handle non-finite values.
Results may differ from the reference program's by a relative error of at most 0.0055.
Values may be sent and summed in bfloat16 or wider, within the bound.
A program may use at most 128 MiB of HBM per device.

```python
import jax
import jax.numpy as jnp
from jax import lax

C = 32
N = 16
W = 128
SPECTRAL_BINS = 64
H = 8


def draw_decay(key, part):
    subkeys = jax.random.split(key, 6)
    channels = C * N
    fast_mask = jax.random.uniform(subkeys[0], (channels,)) < 0.5
    span_len = jnp.exp(jax.random.uniform(subkeys[1], (channels,), minval=jnp.log(10.0), maxval=jnp.log(40.0)))
    kept_share = jax.random.uniform(subkeys[2], (channels,), minval=0.4, maxval=0.95)
    attenuation_speed = jnp.where(fast_mask, 1.0 / span_len, -jnp.log(kept_share) / SPECTRAL_BINS)
    stochastic_perturbation = jax.random.uniform(subkeys[3], (SPECTRAL_BINS, channels), minval=0.5, maxval=1.5)
    position_sequence = jax.random.randint(subkeys[4], (3,), 0, SPECTRAL_BINS)
    spike_occurrences = jnp.any(jnp.arange(SPECTRAL_BINS)[:, None] == position_sequence[None, :], axis=1)
    reduction_multiplier = jax.random.uniform(subkeys[5], (SPECTRAL_BINS, channels), minval=0.55, maxval=0.85)
    numeric_elements = jnp.exp(-attenuation_speed[None, :] * stochastic_perturbation) * jnp.where(spike_occurrences[:, None], reduction_multiplier, 1.0)
    return numeric_elements.astype(jnp.float32)


def steps_of(rng, dims, pieces, low, top_value):
    level, own = 1.0, jax.random.fold_in(rng, 6)
    for axis_at, shards_of in pieces:
        steps = jnp.exp(jax.random.uniform(jax.random.fold_in(own, axis_at), (shards_of,), jnp.float32, low / len(pieces), top_value / len(pieces)))
        level = level * jnp.repeat(steps, dims[axis_at] // shards_of).reshape([-1 if axis == axis_at else 1 for axis in range(len(dims))])
    return level


def gaussian(own_key, shape, spread, bound, shards=(), kind=jnp.bfloat16):
    factor_of = steps_of(own_key, shape, shards, -0.22, 0.18) if shards else 1.0
    values = jax.random.normal(own_key, shape, jnp.float32) * spread * factor_of
    return jnp.minimum(jnp.maximum(values, -bound), bound).astype(kind)


def setup_inputs(seed: int = 0, part: int = 0) -> dict:
    streams_of = jax.random.split(jax.random.key(seed), 8)
    part_splits = jax.random.split(jax.random.fold_in(streams_of[7], part), 8)
    lightcone = gaussian(part_splits[0], (SPECTRAL_BINS, C, H, W), 1.0, 6.0, ((0, 4), (2, 4)))
    cotangent = gaussian(part_splits[1], (SPECTRAL_BINS, C, H, W), 1.0, 6.0, ((0, 4), (2, 4)))
    conv_weight = gaussian(streams_of[2], (C, 9 * C), (9 * C) ** -0.5, 0.375)
    in_proj = gaussian(streams_of[3], (C, N), 0.2, 1.0, (), jnp.float32)
    out_proj = gaussian(streams_of[4], (C, N), 0.1, 0.5, (), jnp.float32)
    skip_gain = gaussian(streams_of[5], (C,), 1.0, 4.0, (), jnp.float32)
    decay = draw_decay(jax.random.fold_in(streams_of[7], 71), part)
    return dict(lightcone=lightcone, cotangent=cotangent, conv_weight=conv_weight, in_proj=in_proj, out_proj=out_proj, skip_gain=skip_gain, decay=decay)


def shifted_stack(numeric_elements):
    tap_list = []
    for row_off in (-1, 0, 1):
        for col_off in (-1, 0, 1):
            tap_list.append(jnp.roll(numeric_elements, (-row_off, -col_off), axis=(1, 2)))
    return jnp.concatenate(tap_list, axis=0)


def back_stack(numeric_elements):
    tap_list = []
    for row_off in (-1, 0, 1):
        for col_off in (-1, 0, 1):
            tap_list.append(jnp.roll(numeric_elements, (row_off, col_off), axis=(1, 2)))
    return jnp.concatenate(tap_list, axis=0)


def reference(lightcone, cotangent, conv_weight, in_proj, out_proj, skip_gain, decay):
    grad_scale = 1.0 / float(SPECTRAL_BINS * H * W) ** 0.5
    flip_weight = conv_weight.reshape(C, 9, C).transpose(2, 1, 0).reshape(C, 9 * C)

    def forward_conv(frame):
        stacked = shifted_stack(frame).reshape(9 * C, H * W)
        return jnp.dot(conv_weight, stacked, preferred_element_type=jnp.float32).astype(jnp.bfloat16)

    inputs = lax.map(forward_conv, lightcone)
    rates = decay.reshape(SPECTRAL_BINS, C, N)
    cot_flat = cotangent.reshape(SPECTRAL_BINS, C, H * W)

    def fwd_step(carry, slices):
        state, grad_out = carry
        rate_f, input_f, cot_f = slices
        state = rate_f[:, :, None] * state + in_proj[:, :, None] * input_f.astype(jnp.float32)[:, None, :]
        grad_out = grad_out + jnp.sum(cot_f.astype(jnp.float32)[:, None, :] * state, axis=2)
        return (state, grad_out), None

    start = (jnp.zeros((C, N, H * W), jnp.float32), jnp.zeros((C, N), jnp.float32))
    (last_state, grad_out), _ = lax.scan(fwd_step, start, (rates, inputs, cot_flat))

    def back_step(carry, slices):
        later, grad_in = carry
        rate_f, input_f, cot_f = slices
        cot_wide = cot_f.astype(jnp.float32)
        adjoint = out_proj[:, :, None] * cot_wide[:, None, :] + later
        grad_in = grad_in + jnp.sum(adjoint * input_f.astype(jnp.float32)[:, None, :], axis=2)
        d_input = (jnp.sum(in_proj[:, :, None] * adjoint, axis=1) + skip_gain[:, None] * cot_wide).astype(jnp.bfloat16)
        return (rate_f[:, :, None] * adjoint, grad_in), d_input

    (later_end, grad_in), d_inputs = lax.scan(back_step, start, (rates, inputs, cot_flat), reverse=True)
    d_skip = jnp.sum(cot_flat.astype(jnp.float32) * inputs.astype(jnp.float32), axis=(0, 2))

    def back_conv(carry, slices):
        frame, d_frame = slices
        d_grid = d_frame.reshape(C, H, W)
        d_light = jnp.dot(flip_weight, back_stack(d_grid).reshape(9 * C, H * W), preferred_element_type=jnp.float32).astype(jnp.bfloat16)
        stacked = shifted_stack(frame).reshape(9 * C, H * W)
        carry = carry + jnp.dot(d_frame, stacked.T, preferred_element_type=jnp.float32)
        return carry, d_light.reshape(C, H, W)

    grad_conv, d_lightcone = lax.scan(back_conv, jnp.zeros((C, 9 * C), jnp.float32), (lightcone, d_inputs))
    return (d_lightcone, grad_conv * grad_scale, grad_in * grad_scale, grad_out * grad_scale, d_skip * grad_scale)
```

```python
import functools

import jax
import jax.numpy as jnp
from jax import lax
from jax.experimental import pallas as pl
from jax.experimental.pallas import tpu as pltpu
from jax.sharding import PartitionSpec as P

MESH = pl.DeviceIdType.MESH
BF = jnp.bfloat16
F32 = jnp.float32


def dot(a, b):
    return jnp.dot(a, b, preferred_element_type=F32)


def dot_nt(a, b):
    return lax.dot_general(a, b, (((1,), (1,)), ((), ())), preferred_element_type=F32)


def iota(shape, dim):
    return lax.broadcasted_iota(jnp.int32, shape, dim)


def kernel(nf, ns, x_hbm, cot_hbm, w_hbm, in_hbm, out_hbm, skip_hbm, dec_hbm,
           dl_ref, pay_out,
           xr, cg, dg, inp, p4, cur, k4, m4, kb, dr, tacc, pay, rs, sk, own, aw, bw,
           halo_s, halo_r, dhalo_s, dhalo_r, dec_s, dec_r, cot_s, cot_r, fwd_s,
           rs_s, rs_r, sk_s, sk_r, ag_s, ag_r,
           x_ref, cot_ref, w_ref, in_ref, out_ref, skip_ref, load):
    F = x_ref.shape[0]
    me = lax.axis_index("freq")
    sky = lax.axis_index("sky")
    core = lax.rem(me, 2)
    chip = me // 2
    chips = nf // 2
    sibling = me + 1 - 2 * core
    nxt = lax.rem(sky + 1, ns)
    prv = lax.rem(sky + ns - 1, ns)
    rows = pay.shape[0] // nf

    loads = [
        pltpu.make_async_copy(src, dst, load.at[i])
        for i, (src, dst) in enumerate((
            (cot_hbm, cot_ref), (dec_hbm, dg.at[me]), (x_hbm, x_ref), (w_hbm, w_ref),
            (in_hbm, in_ref), (out_hbm, out_ref), (skip_hbm, skip_ref)))
    ]
    for one in loads:
        one.start()
    barrier = pltpu.get_barrier_semaphore()
    for d in range(1, nf):
        pl.semaphore_signal(barrier, inc=1, device_id={"freq": lax.rem(me + d, nf)}, device_id_type=MESH)
    for d in range(1, ns):
        pl.semaphore_signal(barrier, inc=1, device_id={"sky": lax.rem(sky + d, ns)}, device_id_type=MESH)

    pr, pc = iota((64, 64), 0), iota((64, 64), 1)
    perm = (pc == 2 * lax.rem(pr, 32) + pr // 32).astype(F32).astype(BF)
    loads[0].wait()
    for f in range(F):
        c2 = dot(perm, cot_ref[f]).astype(BF)
        cg[me, 0, f * 32:(f + 1) * 32, :] = c2[0:32]
        cg[me, 1, f * 32:(f + 1) * 32, :] = c2[32:64]
    loads[2].wait()
    for f in range(F):
        xr[f, 32:96, :] = dot(perm, x_ref[f]).astype(BF)
    for i in (1, 3, 4, 5, 6):
        loads[i].wait()
    pl.semaphore_wait(barrier, nf + ns - 2)

    def remote(src, dst, s, r, **where):
        return pltpu.make_async_remote_copy(
            src_ref=src, dst_ref=dst, send_sem=s, recv_sem=r, device_id=dict(where), device_id_type=MESH)

    def dec_copy(d):
        return remote(dg.at[me], dg.at[me], dec_s.at[d], dec_r.at[me], freq=jnp.maximum(me - d, 0))

    def cot_copy(d, h):
        target = jnp.maximum(chip - d, 0) * 2 + core
        return remote(cg.at[me, h], cg.at[me, h], cot_s.at[d, h], cot_r.at[me, h], freq=target)

    def sib_copy(h):
        return remote(cg.at[me, h], cg.at[me, h], cot_s.at[0, h], cot_r.at[me, h], freq=sibling)

    def slot_copy(slot, h, s):
        return remote(cg.at[slot, h], cg.at[slot, h], s, cot_r.at[slot, h], freq=sibling)

    def fwd_copy(d, h):
        slot = jnp.minimum(chip + d, chips - 1) * 2 + core
        return slot_copy(slot, h, fwd_s.at[d, h])

    up = remote(xr.at[:, 64:96], xr.at[:, 0:32], halo_s.at[0], halo_r.at[0], sky=nxt)
    down = remote(xr.at[:, 32:64], xr.at[:, 96:128], halo_s.at[1], halo_r.at[1], sky=prv)
    for d in range(1, nf):
        @pl.when(me >= d)
        def _():
            dec_copy(d).start()
    for h in range(2):
        for d in range(1, chips):
            @pl.when(chip >= d)
            def _():
                cot_copy(d, h).start()

        @pl.when(core == 1)
        def _():
            sib_copy(h).start()
    up.start()
    down.start()

    sr, sc = iota((128, 256), 0), iota((128, 256), 1)
    shift = jnp.logical_or(lax.rem(sr + 1, 128) == sc, lax.rem(sr + 127, 128) == sc - 128)
    shift = shift.astype(F32).astype(BF)
    er = (iota((128, 2048), 1) // 16 == iota((128, 2048), 0)).astype(F32).astype(BF)
    et = (iota((2048, 128), 0) // 16 == iota((2048, 128), 1)).astype(F32).astype(BF)
    fi = iota((F, 512), 0)
    same = lax.rem(iota((32, 512), 1), 32) == iota((32, 512), 0)
    r64, l64 = iota((64, 128), 0), iota((64, 128), 1)
    diag = lax.rem(r64, 16) == 4 * (r64 // 16) + l64 // 32

    tacc[...] = jnp.zeros_like(tacc)
    cur[...] = jnp.zeros_like(cur)

    spread = (lax.rem(iota((32, 2048), 1) // 16, 32) == iota((32, 2048), 0)).astype(F32)
    io = jnp.dot(in_ref[...] * out_ref[...], spread, precision=lax.Precision.HIGHEST, preferred_element_type=F32)
    io = jnp.sum(jnp.where(lax.rem(iota((16, 2048), 1), 16) == iota((16, 2048), 0), io, 0.0), axis=0, keepdims=True)
    skip4 = jnp.concatenate([skip_ref[...]] * 4, axis=1)

    def factors(d, carry):
        q = me + d

        @pl.when(d > 0)
        def _():
            remote(dg.at[q], dg.at[q], dec_s.at[0], dec_r.at[q], freq=sibling).wait_recv()

        v = cur[...]
        for g in range(F):
            v = jnp.where(fi == g - F * d, 1.0, v * dg[q, g:g + 1, :])
            G, j = g // 4, g % 4
            p4[d, G * 16:(G + 1) * 16, j * 512:(j + 1) * 512] = v
        cur[...] = v
        k = dot((p4[d] * io).astype(BF), et)
        k4[...] = k + jnp.where(jnp.logical_and(diag, d == 0), skip4, 0.0)
        for f in range(F):
            for G in range(4):
                row = jnp.broadcast_to(k4[G * 16 + f:G * 16 + f + 1, :], (32, 128))
                kb[d, f * 32:(f + 1) * 32, G * 128:(G + 1) * 128] = jnp.where(same[:, 0:128], row, 0.0).astype(BF)
        return carry

    lax.fori_loop(0, nf - me, factors, 0)

    kk, ll = iota((288, 384), 0), iota((288, 384), 1)
    for r in range(2):
        tap = lax.rem(ll, 128) // 32 - r
        pick = jnp.logical_and(kk == (tap * 3 + ll // 128) * 32 + lax.rem(ll, 32),
                               jnp.logical_and(tap >= 0, tap <= 2))
        aw[r * 32:(r + 1) * 32, :] = dot(w_ref[...], pick.astype(F32).astype(BF)).astype(BF)
    mm, kk = iota((64, 288), 0), iota((64, 288), 1)
    for k in range(3):
        for row in range(4):
            tap = lax.rem(mm, 2) + 2 - row
            pick = jnp.logical_and(kk == (tap * 3 + k) * 32 + mm // 2,
                                   jnp.logical_and(tap >= 0, tap <= 2))
            at = k * 128 + row * 32
            bw[:, at:at + 32] = dot_nt(pick.astype(F32).astype(BF), w_ref[...])

    dup = remote(dr.at[:, 64:96], dr.at[:, 0:32], dhalo_s.at[1], dhalo_r.at[1], sky=nxt)
    ddown = remote(dr.at[:, 32:64], dr.at[:, 96:128], dhalo_s.at[0], dhalo_r.at[0], sky=prv)

    def mix(h):
        def step(d, total):
            q = me + d

            @pl.when(jnp.logical_and(d > 0, lax.rem(q, 2) == 0))
            def _():
                slot_copy(q + core, h, fwd_s.at[0, h]).wait_recv()
                slot_copy(q + core, h, fwd_s.at[q // 2 - chip, h]).start()

            @pl.when(jnp.logical_and(d > 0, lax.rem(q, 2) != core))
            def _():
                slot_copy(q, h, fwd_s.at[0, h]).wait_recv()

            return total + dot(kb[d], cg[q, h])

        total = lax.fori_loop(0, nf - me, step, jnp.zeros((F * 32, 128), F32)).astype(BF)
        for f in range(F):
            dr[f, 32 + 32 * h:64 + 32 * h, :] = total[f * 32:(f + 1) * 32]

    mix(0)
    ddown.start()
    up.wait_recv()
    down.wait_recv()
    for f in range(F):
        x = xr[f]
        rolled = dot(x, shift).astype(BF)
        full = jnp.concatenate([rolled[:, 0:128], x, rolled[:, 128:256]], axis=0)
        got = dot(aw[...], full).astype(BF)
        inp[f * 32:(f + 1) * 32, 0:128] = got[0:32]
        inp[f * 32:(f + 1) * 32, 128:256] = got[32:64]
    mix(1)
    dup.start()

    def block(d, carry):
        q = me + d
        gram = dot_nt(inp[...], jnp.concatenate([cg[q, 0], cg[q, 1]], axis=1))
        for f in range(F):
            row = jnp.sum(jnp.where(same, gram[f * 32:(f + 1) * 32, :], 0.0), axis=0, keepdims=True)
            for G in range(4):
                m4[G * 16 + f:G * 16 + f + 1, :] = row[:, G * 128:(G + 1) * 128]

        @pl.when(d == 0)
        def _():
            pay[96:128, :] = jnp.zeros((32, 128), F32)
            pay[100:101, :] = jnp.sum(jnp.where(diag, m4[...], 0.0), axis=0, keepdims=True)

        wide = dot(m4[...].astype(BF), er) * p4[d]
        tacc[...] += jnp.sum(wide.reshape(8, 8, 2048), axis=0)
        return carry

    lax.fori_loop(0, nf - me, block, 0)

    grad = jnp.zeros((192, 128), F32)
    for f in range(F):
        mid = dr[f, 32:96, :]
        rolled = dot(mid, shift).astype(BF)
        full = jnp.concatenate([rolled[:, 128:256], mid, rolled[:, 0:128]], axis=0)
        grad = grad + dot_nt(full, xr[f])
    for k in range(3):
        top = grad[k * 64:k * 64 + 32, 0:96]
        low = grad[k * 64 + 32:k * 64 + 64, 32:128]
        pay[k * 32:(k + 1) * 32, 0:96] = top + low
        pay[k * 32:(k + 1) * 32, 96:128] = jnp.zeros((32, 32), F32)
    t = jnp.sum(tacc[...], axis=0, keepdims=True)
    t = t[:, 0:512] + t[:, 512:1024] + t[:, 1024:1536] + t[:, 1536:2048]
    for k in range(4):
        pay[96 + k:97 + k, :] = t[:, k * 128:(k + 1) * 128]

    def part(ref, i):
        return ref.at[pl.ds(pl.multiple_of(i * rows, 8), rows)]

    def rs_copy(d):
        to = lax.rem(me + d, nf)
        return remote(part(pay, to), rs.at[d], rs_s.at[d], rs_r.at[d], freq=to)

    def sk_copy(d):
        return remote(own, sk.at[d], sk_s.at[d], sk_r.at[d], sky=lax.rem(sky + d, ns))

    def ag_copy(d):
        return remote(part(pay_out, me), part(pay_out, me), ag_s.at[d], ag_r.at[me],
                      freq=lax.rem(me + d, nf))

    def ag_wait(d):
        q = lax.rem(me + nf - d, nf)
        remote(part(pay_out, q), part(pay_out, q), ag_s.at[0], ag_r.at[q], freq=q).wait_recv()

    for d in range(1, nf):
        rs_copy(d).start()
    total = pay[pl.ds(pl.multiple_of(me * rows, 8), rows), :]
    for d in range(1, nf):
        rs_copy(d).wait_recv()
        total = total + rs[d]
    own[...] = total
    for d in range(1, ns):
        sk_copy(d).start()
    dup.wait_recv()
    ddown.wait_recv()
    b = bw[...].astype(BF)
    for f in range(F):
        x = dr[f]
        rolled = dot(x, shift).astype(BF)
        full = jnp.concatenate([rolled[:, 128:256], x, rolled[:, 0:128]], axis=0)
        dl_ref[f] = dot(b, full).astype(BF)
    for d in range(1, ns):
        sk_copy(d).wait_recv()
        total = total + sk[d]
    pay_out[pl.ds(pl.multiple_of(me * rows, 8), rows), :] = total
    for d in range(1, nf):
        ag_copy(d).start()
    for d in range(1, nf):
        ag_wait(d)

    up.wait_send()
    down.wait_send()
    dup.wait_send()
    ddown.wait_send()
    for d in range(1, nf):
        rs_copy(d).wait_send()
        ag_copy(d).wait_send()

        @pl.when(me >= d)
        def _():
            dec_copy(d).wait_send()
    for d in range(1, ns):
        sk_copy(d).wait_send()
    for h in range(2):
        for d in range(1, chips):
            @pl.when(chip >= d)
            def _():
                cot_copy(d, h).wait_send()

            @pl.when(chip + d < chips)
            def _():
                fwd_copy(d, h).wait_send()

        @pl.when(core == 1)
        def _():
            sib_copy(h).wait_send()


def finish(scale, dl_ref, pay_ref, in_ref, out_ref, dl_hbm, conv_hbm, din_hbm, dout_hbm, skip_hbm,
           conv_out, din_out, dout_out, skip_out, sems):
    copies = [
        pltpu.make_async_copy(src, dst, sems.at[i])
        for i, (src, dst) in enumerate((
            (dl_ref, dl_hbm), (conv_out, conv_hbm), (din_out, din_hbm), (dout_out, dout_hbm), (skip_out, skip_hbm)))
    ]
    copies[0].start()
    for dr in range(3):
        for k in range(3):
            at = (dr * 3 + k) * 32
            conv_out[:, at:at + 32] = pay_ref[k * 32:(k + 1) * 32, dr * 32:(dr + 1) * 32] * scale
    copies[1].start()
    t = jnp.concatenate([pay_ref[96 + k:97 + k, :] for k in range(4)], axis=1) * scale
    t = jnp.where(lax.rem(iota((16, 512), 1), 16) == iota((16, 512), 0), t, 0.0)
    join = (iota((512, 32), 0) // 16 == iota((512, 32), 1)).astype(F32)
    t = jnp.dot(t, join, precision=lax.Precision.HIGHEST, preferred_element_type=F32)
    din_out[...] = t * out_ref[...]
    dout_out[...] = t * in_ref[...]
    s = pay_ref[100:101, :] * scale
    skip_out[...] = s[:, 0:32] + s[:, 32:64] + s[:, 64:96] + s[:, 96:128]
    for one in copies[2:]:
        one.start()
    for one in copies:
        one.wait()


def in_hbm(x):
    return pltpu.with_memory_space_constraint(x, pltpu.MemorySpace.HBM)


def per_device(lightcone, cotangent, conv_weight, in_proj, out_proj, skip_gain, decay):
    F, C, R, W = lightcone.shape
    N = in_proj.shape[1]
    nf, ns = lax.axis_size("freq"), lax.axis_size("sky")
    scale = 1.0 / float(F * nf * R * ns * W) ** 0.5
    rows = 128 // nf
    dma = pltpu.SemaphoreType.DMA
    vm = pl.BlockSpec(memory_space=pltpu.VMEM)
    hbm = pl.BlockSpec(memory_space=pltpu.MemorySpace.HBM)
    dl, pay = pl.pallas_call(
        functools.partial(kernel, nf, ns),
        out_shape=(
            jax.ShapeDtypeStruct((F, C * R, W), BF),
            jax.ShapeDtypeStruct((128, 128), F32),
        ),
        in_specs=[hbm] * 7,
        out_specs=(vm, vm),
        scratch_shapes=[
            pltpu.VMEM((F, 4 * C, W), BF),
            pltpu.VMEM((nf, R, F * C, W), BF),
            pltpu.VMEM((nf, F, C * N), F32),
            pltpu.VMEM((F * C, R * W), BF),
            pltpu.VMEM((nf, 4 * F, 4 * C * N), F32),
            pltpu.VMEM((F, C * N), F32),
            pltpu.VMEM((4 * F, 128), F32),
            pltpu.VMEM((4 * F, 128), F32),
            pltpu.VMEM((nf, F * C, F * C), BF),
            pltpu.VMEM((F, 4 * C, W), BF),
            pltpu.VMEM((8, 4 * C * N), F32),
            pltpu.VMEM((128, 128), F32),
            pltpu.VMEM((nf, rows, 128), F32),
            pltpu.VMEM((ns, rows, 128), F32),
            pltpu.VMEM((rows, 128), F32),
            pltpu.VMEM((2 * C, 12 * C), BF),
            pltpu.VMEM((2 * C, 12 * C), F32),
            dma((2,)), dma((2,)), dma((2,)), dma((2,)),
            dma((nf,)), dma((nf,)), dma((nf, 2)), dma((nf, 2)), dma((nf, 2)),
            dma((nf,)), dma((nf,)), dma((ns,)), dma((ns,)), dma((nf,)), dma((nf,)),
            pltpu.VMEM((F, C * R, W), BF),
            pltpu.VMEM((F, C * R, W), BF),
            pltpu.VMEM((C, 9 * C), BF),
            pltpu.VMEM((N, C), F32),
            pltpu.VMEM((N, C), F32),
            pltpu.VMEM((1, C), F32),
            dma((7,)),
        ],
        compiler_params=pltpu.CompilerParams(
            collective_id=0, has_side_effects=True, vmem_limit_bytes=(12 + 2 * nf) << 20),
    )(*map(in_hbm, (lightcone.reshape(F, C * R, W), cotangent.reshape(F, C * R, W), conv_weight,
                    in_proj.T, out_proj.T, skip_gain.reshape(1, C), decay)))
    dl, grad, din, dout, d_skip = pl.pallas_call(
        functools.partial(finish, scale),
        out_shape=(
            jax.ShapeDtypeStruct((F, C * R, W), BF),
            jax.ShapeDtypeStruct((C, 9 * C), F32),
            jax.ShapeDtypeStruct((N, C), F32),
            jax.ShapeDtypeStruct((N, C), F32),
            jax.ShapeDtypeStruct((1, C), F32),
        ),
        in_specs=[vm] * 4,
        out_specs=(hbm,) * 5,
        scratch_shapes=[
            pltpu.VMEM((C, 9 * C), F32), pltpu.VMEM((N, C), F32), pltpu.VMEM((N, C), F32),
            pltpu.VMEM((1, C), F32), dma((5,))],
        compiler_params=pltpu.CompilerParams(vmem_limit_bytes=8 << 20),
    )(dl, pay, in_proj.T, out_proj.T)
    return dl.reshape(F, C, R, W), grad, din.T, dout.T, d_skip.reshape(C)


def solution(mesh):
    return jax.shard_map(
        per_device,
        mesh=mesh,
        in_specs=(
            P(("replica", "freq"), None, "sky", None),
            P(("replica", "freq"), None, "sky", None),
            P(),
            P(),
            P(),
            P(),
            P("freq", None),
        ),
        out_specs=(
            P(("replica", "freq"), None, "sky", None),
            P("replica", None),
            P("replica", None),
            P("replica", None),
            P("replica"),
        ),
        check_vma=False,
    )
```

```python
import functools

import jax
import jax.numpy as jnp
from jax import lax
from jax.experimental import pallas as pl
from jax.experimental.pallas import tpu as pltpu
from jax.sharding import PartitionSpec as P

MESH = pl.DeviceIdType.MESH
BF = jnp.bfloat16
F32 = jnp.float32


def dot(a, b):
    return jnp.dot(a, b, preferred_element_type=F32)


def dot_nt(a, b):
    return lax.dot_general(a, b, (((1,), (1,)), ((), ())), preferred_element_type=F32)


def iota(shape, dim):
    return lax.broadcasted_iota(jnp.int32, shape, dim)


def kernel(nf, ns, x_hbm, cot_hbm, w_hbm, in_hbm, out_hbm, skip_hbm, dec_hbm,
           dl_ref, pay_out,
           xr, cg, dg, inp, p4, cur, k4, m4, kb, dr, tacc, pay, rs, aw, bw,
           halo_s, halo_r, dhalo_s, dhalo_r, dec_s, dec_r, cot_s, cot_r, fwd_s,
           rs_s, rs_r, ag_s, ag_r,
           x_ref, cot_ref, w_ref, in_ref, out_ref, skip_ref, load):
    F = x_ref.shape[0]
    me = lax.axis_index("freq")
    sky = lax.axis_index("sky")
    core = lax.rem(me, 2)
    chip = me // 2
    chips = nf // 2
    sibling = me + 1 - 2 * core
    nxt = lax.rem(sky + 1, ns)
    prv = lax.rem(sky + ns - 1, ns)
    rows = rs.shape[1]
    owners = pay.shape[0] // rows
    here = sky * nf + me
    owner = sky * chips + chip
    owns = jnp.logical_and(core == 1, owner < owners)

    loads = [
        pltpu.make_async_copy(src, dst, load.at[i])
        for i, (src, dst) in enumerate((
            (cot_hbm, cot_ref), (dec_hbm, dg.at[me]), (x_hbm, x_ref), (w_hbm, w_ref),
            (in_hbm, in_ref), (out_hbm, out_ref), (skip_hbm, skip_ref)))
    ]
    for one in loads:
        one.start()
    barrier = pltpu.get_barrier_semaphore()

    def greet(d, carry):
        other = lax.rem(here + d, nf * ns)
        pl.semaphore_signal(barrier, inc=1, device_id={"sky": other // nf, "freq": lax.rem(other, nf)},
                            device_id_type=MESH)
        return carry

    lax.fori_loop(1, nf * ns, greet, 0, unroll=nf * ns <= 16)

    pr, pc = iota((64, 64), 0), iota((64, 64), 1)
    perm = (pc == 2 * lax.rem(pr, 32) + pr // 32).astype(F32).astype(BF)
    loads[0].wait()
    for f in range(F):
        c2 = dot(perm, cot_ref[f]).astype(BF)
        cg[me, 0, f * 32:(f + 1) * 32, :] = c2[0:32]
        cg[me, 1, f * 32:(f + 1) * 32, :] = c2[32:64]
    loads[2].wait()
    for f in range(F):
        xr[f, 32:96, :] = dot(perm, x_ref[f]).astype(BF)
    for i in (1, 3, 4, 5, 6):
        loads[i].wait()
    pl.semaphore_wait(barrier, nf * ns - 1)

    def remote(src, dst, s, r, **where):
        return pltpu.make_async_remote_copy(
            src_ref=src, dst_ref=dst, send_sem=s, recv_sem=r, device_id=dict(where), device_id_type=MESH)

    def dec_copy(d):
        return remote(dg.at[me], dg.at[me], dec_s.at[d], dec_r.at[me], freq=jnp.maximum(me - d, 0))

    def cot_copy(d, h):
        target = jnp.maximum(chip - d, 0) * 2 + core
        return remote(cg.at[me, h], cg.at[me, h], cot_s.at[d, h], cot_r.at[me, h], freq=target)

    def sib_copy(h):
        return remote(cg.at[me, h], cg.at[me, h], cot_s.at[0, h], cot_r.at[me, h], freq=sibling)

    def slot_copy(slot, h, s):
        return remote(cg.at[slot, h], cg.at[slot, h], s, cot_r.at[slot, h], freq=sibling)

    def fwd_copy(d, h):
        slot = jnp.minimum(chip + d, chips - 1) * 2 + core
        return slot_copy(slot, h, fwd_s.at[d, h])

    up = remote(xr.at[:, 64:96], xr.at[:, 0:32], halo_s.at[0], halo_r.at[0], sky=nxt)
    down = remote(xr.at[:, 32:64], xr.at[:, 96:128], halo_s.at[1], halo_r.at[1], sky=prv)
    for d in range(1, nf):
        @pl.when(me >= d)
        def _():
            dec_copy(d).start()
    for h in range(2):
        for d in range(1, chips):
            @pl.when(chip >= d)
            def _():
                cot_copy(d, h).start()

        @pl.when(core == 1)
        def _():
            sib_copy(h).start()
    up.start()
    down.start()

    sr, sc = iota((128, 256), 0), iota((128, 256), 1)
    shift = jnp.logical_or(lax.rem(sr + 1, 128) == sc, lax.rem(sr + 127, 128) == sc - 128)
    shift = shift.astype(F32).astype(BF)
    er = (iota((128, 2048), 1) // 16 == iota((128, 2048), 0)).astype(F32).astype(BF)
    et = (iota((2048, 128), 0) // 16 == iota((2048, 128), 1)).astype(F32).astype(BF)
    fi = iota((F, 512), 0)
    same = lax.rem(iota((32, 512), 1), 32) == iota((32, 512), 0)
    r64, l64 = iota((64, 128), 0), iota((64, 128), 1)
    diag = lax.rem(r64, 16) == 4 * (r64 // 16) + l64 // 32

    tacc[...] = jnp.zeros_like(tacc)
    cur[...] = jnp.zeros_like(cur)

    spread = (lax.rem(iota((32, 2048), 1) // 16, 32) == iota((32, 2048), 0)).astype(F32)
    io = jnp.dot(in_ref[...] * out_ref[...], spread, precision=lax.Precision.HIGHEST, preferred_element_type=F32)
    io = jnp.sum(jnp.where(lax.rem(iota((16, 2048), 1), 16) == iota((16, 2048), 0), io, 0.0), axis=0, keepdims=True)
    skip4 = jnp.concatenate([skip_ref[...]] * 4, axis=1)

    def factors(d, carry):
        q = me + d

        @pl.when(d > 0)
        def _():
            remote(dg.at[q], dg.at[q], dec_s.at[0], dec_r.at[q], freq=sibling).wait_recv()

        v = cur[...]
        for g in range(F):
            v = jnp.where(fi == g - F * d, 1.0, v * dg[q, g:g + 1, :])
            G, j = g // 4, g % 4
            p4[d, G * 16:(G + 1) * 16, j * 512:(j + 1) * 512] = v
        cur[...] = v
        k = dot((p4[d] * io).astype(BF), et)
        k4[...] = k + jnp.where(jnp.logical_and(diag, d == 0), skip4, 0.0)
        for f in range(F):
            for G in range(4):
                row = jnp.broadcast_to(k4[G * 16 + f:G * 16 + f + 1, :], (32, 128))
                kb[d, f * 32:(f + 1) * 32, G * 128:(G + 1) * 128] = jnp.where(same[:, 0:128], row, 0.0).astype(BF)
        return carry

    lax.fori_loop(0, nf - me, factors, 0)

    kk, ll = iota((288, 384), 0), iota((288, 384), 1)
    for r in range(2):
        tap = lax.rem(ll, 128) // 32 - r
        pick = jnp.logical_and(kk == (tap * 3 + ll // 128) * 32 + lax.rem(ll, 32),
                               jnp.logical_and(tap >= 0, tap <= 2))
        aw[r * 32:(r + 1) * 32, :] = dot(w_ref[...], pick.astype(F32).astype(BF)).astype(BF)
    mm, kk = iota((64, 288), 0), iota((64, 288), 1)
    for k in range(3):
        for row in range(4):
            tap = lax.rem(mm, 2) + 2 - row
            pick = jnp.logical_and(kk == (tap * 3 + k) * 32 + mm // 2,
                                   jnp.logical_and(tap >= 0, tap <= 2))
            at = k * 128 + row * 32
            bw[:, at:at + 32] = dot_nt(pick.astype(F32).astype(BF), w_ref[...])

    dup = remote(dr.at[:, 64:96], dr.at[:, 0:32], dhalo_s.at[1], dhalo_r.at[1], sky=nxt)
    ddown = remote(dr.at[:, 32:64], dr.at[:, 96:128], dhalo_s.at[0], dhalo_r.at[0], sky=prv)

    def mix(h):
        def step(d, total):
            q = me + d

            @pl.when(jnp.logical_and(d > 0, lax.rem(q, 2) == 0))
            def _():
                slot_copy(q + core, h, fwd_s.at[0, h]).wait_recv()
                slot_copy(q + core, h, fwd_s.at[q // 2 - chip, h]).start()

            @pl.when(jnp.logical_and(d > 0, lax.rem(q, 2) != core))
            def _():
                slot_copy(q, h, fwd_s.at[0, h]).wait_recv()

            return total + dot(kb[d], cg[q, h])

        total = lax.fori_loop(0, nf - me, step, jnp.zeros((F * 32, 128), F32)).astype(BF)
        for f in range(F):
            dr[f, 32 + 32 * h:64 + 32 * h, :] = total[f * 32:(f + 1) * 32]

    mix(0)
    ddown.start()
    up.wait_recv()
    down.wait_recv()
    for f in range(F):
        x = xr[f]
        rolled = dot(x, shift).astype(BF)
        full = jnp.concatenate([rolled[:, 0:128], x, rolled[:, 128:256]], axis=0)
        got = dot(aw[...], full).astype(BF)
        inp[f * 32:(f + 1) * 32, 0:128] = got[0:32]
        inp[f * 32:(f + 1) * 32, 128:256] = got[32:64]
    mix(1)
    dup.start()

    def block(d, carry):
        q = me + d
        gram = dot_nt(inp[...], jnp.concatenate([cg[q, 0], cg[q, 1]], axis=1))
        for f in range(F):
            row = jnp.sum(jnp.where(same, gram[f * 32:(f + 1) * 32, :], 0.0), axis=0, keepdims=True)
            for G in range(4):
                m4[G * 16 + f:G * 16 + f + 1, :] = row[:, G * 128:(G + 1) * 128]

        @pl.when(d == 0)
        def _():
            pay[96:128, :] = jnp.zeros((32, 128), F32)
            pay[100:101, :] = jnp.sum(jnp.where(diag, m4[...], 0.0), axis=0, keepdims=True)

        wide = dot(m4[...].astype(BF), er) * p4[d]
        tacc[...] += jnp.sum(wide.reshape(8, 8, 2048), axis=0)
        return carry

    lax.fori_loop(0, nf - me, block, 0)

    grad = jnp.zeros((192, 128), F32)
    for f in range(F):
        mid = dr[f, 32:96, :]
        rolled = dot(mid, shift).astype(BF)
        full = jnp.concatenate([rolled[:, 128:256], mid, rolled[:, 0:128]], axis=0)
        grad = grad + dot_nt(full, xr[f])
    for k in range(3):
        top = grad[k * 64:k * 64 + 32, 0:96]
        low = grad[k * 64 + 32:k * 64 + 64, 32:128]
        pay[k * 32:(k + 1) * 32, 0:96] = top + low
        pay[k * 32:(k + 1) * 32, 96:128] = jnp.zeros((32, 32), F32)
    t = jnp.sum(tacc[...], axis=0, keepdims=True)
    t = t[:, 0:512] + t[:, 512:1024] + t[:, 1024:1536] + t[:, 1536:2048]
    for k in range(4):
        pay[96 + k:97 + k, :] = t[:, k * 128:(k + 1) * 128]

    def part(ref, i):
        return ref.at[pl.ds(pl.multiple_of(i * rows, 8), rows)]

    def each_owner(do):
        def step(d, carry):
            i = lax.rem(owner + d, owners)

            @pl.when(jnp.logical_not(jnp.logical_and(owns, i == owner)))
            def _():
                do(remote(part(pay, i), rs.at[here], rs_s.at[0], rs_r.at[0],
                          sky=i // chips, freq=lax.rem(i, chips) * 2 + 1))

            return carry

        lax.fori_loop(0, owners, step, 0, unroll=owners <= 8)

    def each_other(do):
        def step(d, carry):
            other = lax.rem(here + d, nf * ns)
            do(remote(part(pay_out, owner), part(pay_out, owner), ag_s.at[0], ag_r.at[0],
                      sky=other // nf, freq=lax.rem(other, nf)))
            return carry

        lax.fori_loop(1, nf * ns, step, 0, unroll=nf * ns <= 16)

    each_owner(lambda one: one.start())
    dup.wait_recv()
    ddown.wait_recv()
    b = bw[...].astype(BF)
    for f in range(F):
        x = dr[f]
        rolled = dot(x, shift).astype(BF)
        full = jnp.concatenate([rolled[:, 128:256], x, rolled[:, 0:128]], axis=0)
        dl_ref[f] = dot(b, full).astype(BF)

    @pl.when(owns)
    def _():
        rs[here] = pay[pl.ds(pl.multiple_of(owner * rows, 8), rows), :]
        some = rs.at[0:nf * ns - 1]
        pltpu.make_async_copy(some, some, rs_r.at[0]).wait()
        pay_out[pl.ds(pl.multiple_of(owner * rows, 8), rows), :] = jnp.sum(rs[...], axis=0)
        each_other(lambda one: one.start())
        rest = pay_out.at[0:128 - rows]
        pltpu.make_async_copy(rest, rest, ag_r.at[0]).wait()

    @pl.when(jnp.logical_not(owns))
    def _():
        pltpu.make_async_copy(pay_out, pay_out, ag_r.at[0]).wait()

    up.wait_send()
    down.wait_send()
    dup.wait_send()
    ddown.wait_send()
    each_owner(lambda one: one.wait_send())

    @pl.when(owns)
    def _():
        each_other(lambda one: one.wait_send())

    for d in range(1, nf):
        @pl.when(me >= d)
        def _():
            dec_copy(d).wait_send()
    for h in range(2):
        for d in range(1, chips):
            @pl.when(chip >= d)
            def _():
                cot_copy(d, h).wait_send()

            @pl.when(chip + d < chips)
            def _():
                fwd_copy(d, h).wait_send()

        @pl.when(core == 1)
        def _():
            sib_copy(h).wait_send()


def finish(scale, dl_ref, pay_ref, in_ref, out_ref, dl_hbm, conv_hbm, din_hbm, dout_hbm, skip_hbm,
           conv_out, din_out, dout_out, skip_out, sems):
    copies = [
        pltpu.make_async_copy(src, dst, sems.at[i])
        for i, (src, dst) in enumerate((
            (dl_ref, dl_hbm), (conv_out, conv_hbm), (din_out, din_hbm), (dout_out, dout_hbm), (skip_out, skip_hbm)))
    ]
    copies[0].start()
    for dr in range(3):
        for k in range(3):
            at = (dr * 3 + k) * 32
            conv_out[:, at:at + 32] = pay_ref[k * 32:(k + 1) * 32, dr * 32:(dr + 1) * 32] * scale
    copies[1].start()
    t = jnp.concatenate([pay_ref[96 + k:97 + k, :] for k in range(4)], axis=1) * scale
    t = jnp.where(lax.rem(iota((16, 512), 1), 16) == iota((16, 512), 0), t, 0.0)
    join = (iota((512, 32), 0) // 16 == iota((512, 32), 1)).astype(F32)
    t = jnp.dot(t, join, precision=lax.Precision.HIGHEST, preferred_element_type=F32)
    din_out[...] = t * out_ref[...]
    dout_out[...] = t * in_ref[...]
    s = pay_ref[100:101, :] * scale
    skip_out[...] = s[:, 0:32] + s[:, 32:64] + s[:, 64:96] + s[:, 96:128]
    for one in copies[2:]:
        one.start()
    for one in copies:
        one.wait()


def in_hbm(x):
    return pltpu.with_memory_space_constraint(x, pltpu.MemorySpace.HBM)


def per_device(lightcone, cotangent, conv_weight, in_proj, out_proj, skip_gain, decay):
    F, C, R, W = lightcone.shape
    N = in_proj.shape[1]
    nf, ns = lax.axis_size("freq"), lax.axis_size("sky")
    scale = 1.0 / float(F * nf * R * ns * W) ** 0.5
    owners = min(nf // 2 * ns, 16)
    dma = pltpu.SemaphoreType.DMA
    vm = pl.BlockSpec(memory_space=pltpu.VMEM)
    hbm = pl.BlockSpec(memory_space=pltpu.MemorySpace.HBM)
    dl, pay = pl.pallas_call(
        functools.partial(kernel, nf, ns),
        out_shape=(
            jax.ShapeDtypeStruct((F, C * R, W), BF),
            jax.ShapeDtypeStruct((128, 128), F32),
        ),
        in_specs=[hbm] * 7,
        out_specs=(vm, vm),
        scratch_shapes=[
            pltpu.VMEM((F, 4 * C, W), BF),
            pltpu.VMEM((nf, R, F * C, W), BF),
            pltpu.VMEM((nf, F, C * N), F32),
            pltpu.VMEM((F * C, R * W), BF),
            pltpu.VMEM((nf, 4 * F, 4 * C * N), F32),
            pltpu.VMEM((F, C * N), F32),
            pltpu.VMEM((4 * F, 128), F32),
            pltpu.VMEM((4 * F, 128), F32),
            pltpu.VMEM((nf, F * C, F * C), BF),
            pltpu.VMEM((F, 4 * C, W), BF),
            pltpu.VMEM((8, 4 * C * N), F32),
            pltpu.VMEM((128, 128), F32),
            pltpu.VMEM((nf * ns, 128 // owners, 128), F32),
            pltpu.VMEM((2 * C, 12 * C), BF),
            pltpu.VMEM((2 * C, 12 * C), F32),
            dma((2,)), dma((2,)), dma((2,)), dma((2,)),
            dma((nf,)), dma((nf,)), dma((nf, 2)), dma((nf, 2)), dma((nf, 2)),
            dma((1,)), dma((1,)), dma((1,)), dma((1,)),
            pltpu.VMEM((F, C * R, W), BF),
            pltpu.VMEM((F, C * R, W), BF),
            pltpu.VMEM((C, 9 * C), BF),
            pltpu.VMEM((N, C), F32),
            pltpu.VMEM((N, C), F32),
            pltpu.VMEM((1, C), F32),
            dma((7,)),
        ],
        compiler_params=pltpu.CompilerParams(
            collective_id=0, has_side_effects=True, vmem_limit_bytes=(12 + 2 * nf) << 20),
    )(*map(in_hbm, (lightcone.reshape(F, C * R, W), cotangent.reshape(F, C * R, W), conv_weight,
                    in_proj.T, out_proj.T, skip_gain.reshape(1, C), decay)))
    dl, grad, din, dout, d_skip = pl.pallas_call(
        functools.partial(finish, scale),
        out_shape=(
            jax.ShapeDtypeStruct((F, C * R, W), BF),
            jax.ShapeDtypeStruct((C, 9 * C), F32),
            jax.ShapeDtypeStruct((N, C), F32),
            jax.ShapeDtypeStruct((N, C), F32),
            jax.ShapeDtypeStruct((1, C), F32),
        ),
        in_specs=[vm] * 4,
        out_specs=(hbm,) * 5,
        scratch_shapes=[
            pltpu.VMEM((C, 9 * C), F32), pltpu.VMEM((N, C), F32), pltpu.VMEM((N, C), F32),
            pltpu.VMEM((1, C), F32), dma((5,))],
        compiler_params=pltpu.CompilerParams(vmem_limit_bytes=8 << 20),
    )(dl, pay, in_proj.T, out_proj.T)
    return dl.reshape(F, C, R, W), grad, din.T, dout.T, d_skip.reshape(C)


def solution(mesh):
    return jax.shard_map(
        per_device,
        mesh=mesh,
        in_specs=(
            P(("replica", "freq"), None, "sky", None),
            P(("replica", "freq"), None, "sky", None),
            P(),
            P(),
            P(),
            P(),
            P("freq", None),
        ),
        out_specs=(
            P(("replica", "freq"), None, "sky", None),
            P("replica", None),
            P("replica", None),
            P("replica", None),
            P("replica"),
        ),
        check_vma=False,
    )
```

```python
import functools

import jax
import jax.numpy as jnp
from jax import lax
from jax.experimental import pallas as pl
from jax.experimental.pallas import tpu as pltpu
from jax.sharding import PartitionSpec as P

MESH = pl.DeviceIdType.MESH
BF = jnp.bfloat16
F32 = jnp.float32


def dot(a, b):
    return jnp.dot(a, b, preferred_element_type=F32)


def dot_nt(a, b):
    return lax.dot_general(a, b, (((1,), (1,)), ((), ())), preferred_element_type=F32)


def iota(shape, dim):
    return lax.broadcasted_iota(jnp.int32, shape, dim)


def kernel(nf, ns, x_hbm, cot_hbm, w_hbm, in_hbm, out_hbm, skip_hbm, dec_hbm,
           dl_ref, pay_out,
           xr, cg, dg, inp, p3, k4, pe, qs, kb, nb, mb, own_d, adj, adj_bf, dr, pay, rs, aw, bw,
           halo_s, halo_r, dhalo_s, dhalo_r, dec_s, dec_r, cot_s, cot_r, fwd_s,
           rs_s, rs_r, ag_s, ag_r,
           x_ref, cot_ref, w_ref, in_ref, out_ref, skip_ref, load):
    F = x_ref.shape[0]
    half = F * 16
    me = lax.axis_index("freq")
    sky = lax.axis_index("sky")
    core = lax.rem(me, 2)
    chip = me // 2
    chips = nf // 2
    sibling = me + 1 - 2 * core
    nxt = lax.rem(sky + 1, ns)
    prv = lax.rem(sky + ns - 1, ns)
    rows = rs.shape[1]
    owners = pay.shape[0] // rows
    here = sky * nf + me
    owner = sky * chips + chip
    owns = jnp.logical_and(core == 1, owner < owners)

    loads = [
        pltpu.make_async_copy(src, dst, load.at[i])
        for i, (src, dst) in enumerate((
            (cot_hbm, cot_ref), (dec_hbm, dg.at[me]), (x_hbm, x_ref), (w_hbm, w_ref),
            (in_hbm, in_ref), (out_hbm, out_ref), (skip_hbm, skip_ref)))
    ]
    for one in loads:
        one.start()
    barrier = pltpu.get_barrier_semaphore()

    def greet(d, carry):
        other = lax.rem(here + d, nf * ns)
        pl.semaphore_signal(barrier, inc=1, device_id={"sky": other // nf, "freq": lax.rem(other, nf)},
                            device_id_type=MESH)
        return carry

    lax.fori_loop(1, nf * ns, greet, 0, unroll=nf * ns <= 16)

    pr, pc = iota((64, 64), 0), iota((64, 64), 1)
    perm = (pc == 2 * lax.rem(pr, 32) + pr // 32).astype(F32).astype(BF)
    loads[0].wait()
    for f in range(F):
        c2 = dot(perm, cot_ref[f]).astype(BF)
        for h in range(2):
            for hi in range(2):
                at = hi * half + f * 16
                cg[me, h, at:at + 16, :] = c2[h * 32 + hi * 16:h * 32 + hi * 16 + 16]
    loads[2].wait()
    for f in range(F):
        xr[f, 32:96, :] = dot(perm, x_ref[f]).astype(BF)
    for i in (1, 3, 4, 5, 6):
        loads[i].wait()
    pl.semaphore_wait(barrier, nf * ns - 1)

    def remote(src, dst, s, r, **where):
        return pltpu.make_async_remote_copy(
            src_ref=src, dst_ref=dst, send_sem=s, recv_sem=r, device_id=dict(where), device_id_type=MESH)

    def dec_copy(d):
        return remote(dg.at[me], dg.at[me], dec_s.at[d], dec_r.at[me], freq=jnp.maximum(me - d, 0))

    def cot_copy(d, h):
        target = jnp.maximum(chip - d, 0) * 2 + core
        return remote(cg.at[me, h], cg.at[me, h], cot_s.at[d, h], cot_r.at[me, h], freq=target)

    def sib_copy(h):
        return remote(cg.at[me, h], cg.at[me, h], cot_s.at[0, h], cot_r.at[me, h], freq=sibling)

    def slot_copy(slot, h, s):
        return remote(cg.at[slot, h], cg.at[slot, h], s, cot_r.at[slot, h], freq=sibling)

    def fwd_copy(d, h):
        slot = jnp.minimum(chip + d, chips - 1) * 2 + core
        return slot_copy(slot, h, fwd_s.at[d, h])

    up = remote(xr.at[:, 64:96], xr.at[:, 0:32], halo_s.at[0], halo_r.at[0], sky=nxt)
    down = remote(xr.at[:, 32:64], xr.at[:, 96:128], halo_s.at[1], halo_r.at[1], sky=prv)
    for d in range(1, nf):
        @pl.when(me >= d)
        def _():
            dec_copy(d).start()
    for h in range(2):
        for d in range(1, chips):
            @pl.when(chip >= d)
            def _():
                cot_copy(d, h).start()

        @pl.when(core == 1)
        def _():
            sib_copy(h).start()
    up.start()
    down.start()

    sr, sc = iota((128, 256), 0), iota((128, 256), 1)
    shift = jnp.logical_or(lax.rem(sr + 1, 128) == sc, lax.rem(sr + 127, 128) == sc - 128)
    shift = shift.astype(F32).astype(BF)

    spread = (iota((32, 512), 1) // 16 == iota((32, 512), 0)).astype(F32)
    io = jnp.dot(in_ref[...] * out_ref[...], spread, precision=lax.Precision.HIGHEST, preferred_element_type=F32)
    io = jnp.sum(jnp.where(lax.rem(iota((16, 512), 1), 16) == iota((16, 512), 0), io, 0.0), axis=0, keepdims=True)
    tr, tc = iota((32, 256), 0), iota((32, 256), 1)
    skips = jnp.where(tr == tc // 128 * 16 + lax.rem(tc, 16), 1.0, 0.0)
    skips = jnp.dot(skip_ref[...], skips, precision=lax.Precision.HIGHEST, preferred_element_type=F32)
    tr, tc = iota((512, 256), 0), iota((512, 256), 1)
    tile = (tr // 16 == tc // 128 * 16 + lax.rem(tc, 16)).astype(F32).astype(BF)

    fi = iota((F, 512), 0)
    v = jnp.zeros((F, 512), F32)
    for g in range(F):
        v = jnp.where(fi == g, 1.0, v * dg[me, g:g + 1, :])
        p3[g * F:(g + 1) * F, :] = v
    pe[...] = v * io
    kk = dot((p3[...] * io).astype(BF), tile)
    row16, lane16 = iota((F, 256), 0), lax.rem(iota((F, 256), 1), 128) // 16
    for G in range(2):
        k = jnp.where(row16 == lane16 + 8 * G, skips, 0.0)
        for j in range(8):
            at = (8 * G + j) * F
            k = k + jnp.where(lane16 == j, kk[at:at + F], 0.0)
        k4[G * F:(G + 1) * F, :] = k
    low_row = lax.rem(iota((16, 128), 1), 16) == iota((16, 128), 0)
    low_col = iota((16, 256), 1) // 16 == iota((16, 256), 0)
    for hi in range(2):
        for f in range(F):
            for G in range(2):
                row = jnp.broadcast_to(k4[G * F + f:G * F + f + 1, hi * 128:(hi + 1) * 128], (16, 128))
                kb[hi, f * 16:(f + 1) * 16, G * 128:(G + 1) * 128] = jnp.where(low_row, row, 0.0).astype(BF)
            row = jnp.broadcast_to(pe[f:f + 1, hi * 256:(hi + 1) * 256], (16, 256))
            nb[hi, f * 16:(f + 1) * 16, :] = jnp.where(low_col, row, 0.0).astype(BF)

    expand = low_col.astype(F32).astype(BF)
    kept = iota((256, 256), 0) // 16 == lax.rem(iota((256, 256), 1), 16)

    def later(q, run):
        remote(dg.at[q], dg.at[q], dec_s.at[0], dec_r.at[q], freq=sibling).wait_recv()
        for g in range(F):
            run = run * dg[q, g:g + 1, :]
            qs[g:g + 1, :] = run
        for hi in range(2):
            m = lax.dot_general(qs[:, hi * 256:(hi + 1) * 256].astype(BF), expand, (((0,), (0,)), ((), ())),
                                preferred_element_type=F32)
            mb[q, hi] = jnp.where(kept, m, 0.0).astype(BF)
        return run

    def cells(q, hi):
        at = slice(hi * half, (hi + 1) * half)
        return jnp.concatenate([cg[q, 0, at], cg[q, 1, at]], axis=1)

    for hi in range(2):
        own_d[hi] = dot(kb[hi], cells(me, hi))

    kk, ll = iota((288, 384), 0), iota((288, 384), 1)
    for r in range(2):
        tap = lax.rem(ll, 128) // 32 - r
        pick = jnp.logical_and(kk == (tap * 3 + ll // 128) * 32 + lax.rem(ll, 32),
                               jnp.logical_and(tap >= 0, tap <= 2))
        aw[r * 32:(r + 1) * 32, :] = dot(w_ref[...], pick.astype(F32).astype(BF)).astype(BF)
    mm, kk = iota((64, 288), 0), iota((64, 288), 1)
    for k in range(3):
        for row in range(4):
            tap = lax.rem(mm, 2) + 2 - row
            pick = jnp.logical_and(kk == (tap * 3 + k) * 32 + mm // 2,
                                   jnp.logical_and(tap >= 0, tap <= 2))
            at = k * 128 + row * 32
            bw[:, at:at + 32] = dot_nt(pick.astype(F32).astype(BF), w_ref[...])

    dup = remote(dr.at[:, 64:96], dr.at[:, 0:32], dhalo_s.at[1], dhalo_r.at[1], sky=nxt)
    ddown = remote(dr.at[:, 32:64], dr.at[:, 96:128], dhalo_s.at[0], dhalo_r.at[0], sky=prv)

    lax.fori_loop(me + 1, nf, later, jnp.ones((1, 512), F32))

    @pl.when(core == 0)
    def _():
        q = jnp.minimum(me + 1, nf - 1)
        for h in range(2):
            slot_copy(q, h, fwd_s.at[0, h]).wait_recv()
        for hi in range(2):
            adj[hi] = dot(mb[q, hi], cells(q, hi))

    @pl.when(core == 1)
    def _():
        adj[...] = jnp.zeros_like(adj)

    def forward(h):
        def step(k, carry):
            slot_copy(2 * k + core, h, fwd_s.at[0, h]).wait_recv()
            slot_copy(2 * k + core, h, fwd_s.at[k - chip, h]).start()
            return carry

        lax.fori_loop(chip + 1, chips, step, 0)

    def mix(h):
        wide = slice(h * 128, (h + 1) * 128)

        def step(k, carry):
            slot_copy(2 * k + 1 - core, h, fwd_s.at[0, h]).wait_recv()
            for hi in range(2):
                at = slice(hi * half, (hi + 1) * half)
                adj[hi, :, wide] += dot(mb[2 * k, hi], cg[2 * k, h, at]) + dot(mb[2 * k + 1, hi], cg[2 * k + 1, h, at])
            return carry

        lax.fori_loop(chip + 1, chips, step, 0)
        for hi in range(2):
            a = adj[hi, :, wide].astype(BF)
            adj_bf[hi, :, wide] = a
            d = (own_d[hi, :, wide] + dot(nb[hi], a)).astype(BF)
            at = 32 + 32 * h + 16 * hi
            for f in range(F):
                dr[f, at:at + 16, :] = d[f * 16:(f + 1) * 16]

    forward(0)
    mix(0)
    ddown.start()
    forward(1)
    up.wait_recv()
    down.wait_recv()
    for f in range(F):
        x = xr[f]
        rolled = dot(x, shift).astype(BF)
        full = jnp.concatenate([rolled[:, 0:128], x, rolled[:, 128:256]], axis=0)
        got = dot(aw[...], full).astype(BF)
        for r in range(2):
            for hi in range(2):
                inp[hi, f * 16:(f + 1) * 16, r * 128:(r + 1) * 128] = got[r * 32 + hi * 16:r * 32 + hi * 16 + 16]

    r256, l256 = iota((256, 256), 0), iota((256, 256), 1)
    same = lax.rem(r256, 16) == lax.rem(l256, 16)
    widen = (lax.rem(r256, 16) == l256 // 16).astype(F32).astype(BF)
    now = r256 // 16 == lax.rem(r256, 16)
    block_of = l256[0:16] // 16
    sums = []
    for hi in range(2):
        gram = jnp.where(same, dot_nt(inp[hi], cells(me, hi)), 0.0).astype(BF)
        rows_f = dot(expand, gram)
        stack = jnp.concatenate([jnp.where(block_of == g, rows_f, 0.0) for g in range(F)], axis=0).astype(BF)
        pairs = dot(stack, widen)
        sums.append(jnp.sum((pairs * p3[:, hi * 256:(hi + 1) * 256]).reshape(F * F // 8, 8, 256), axis=0))
        skip = jnp.sum(jnp.where(now, pairs, 0.0), axis=0, keepdims=True)
        for k in range(2):
            pay[100 + 2 * hi + k:101 + 2 * hi + k, :] = skip[:, k * 128:(k + 1) * 128]
    mix(1)
    dup.start()
    for hi in range(2):
        gram = dot_nt(inp[hi], adj_bf[hi])
        total = sums[hi]
        for f in range(F):
            rows_f = jnp.where(low_col, gram[f * 16:(f + 1) * 16], 0.0)
            at = (F - 1) * F + f
            total = total + (rows_f[0:8] + rows_f[8:16]) * p3[at:at + 1, hi * 256:(hi + 1) * 256]
        t = jnp.sum(total, axis=0, keepdims=True)
        for k in range(2):
            pay[96 + 2 * hi + k:97 + 2 * hi + k, :] = t[:, k * 128:(k + 1) * 128]

    grad = jnp.zeros((192, 128), F32)
    for f in range(F):
        mid = dr[f, 32:96, :]
        rolled = dot(mid, shift).astype(BF)
        full = jnp.concatenate([rolled[:, 128:256], mid, rolled[:, 0:128]], axis=0)
        grad = grad + dot_nt(full, xr[f])
    for k in range(3):
        top = grad[k * 64:k * 64 + 32, 0:96]
        low = grad[k * 64 + 32:k * 64 + 64, 32:128]
        pay[k * 32:(k + 1) * 32, 0:96] = top + low
        pay[k * 32:(k + 1) * 32, 96:128] = jnp.zeros((32, 32), F32)
    pay[104:128, :] = jnp.zeros((24, 128), F32)

    def part(ref, i):
        return ref.at[pl.ds(pl.multiple_of(i * rows, 8), rows)]

    def each_owner(do):
        def step(d, carry):
            i = lax.rem(owner + d, owners)

            @pl.when(jnp.logical_not(jnp.logical_and(owns, i == owner)))
            def _():
                do(remote(part(pay, i), rs.at[here], rs_s.at[0], rs_r.at[0],
                          sky=i // chips, freq=lax.rem(i, chips) * 2 + 1))

            return carry

        lax.fori_loop(0, owners, step, 0, unroll=owners <= 8)

    def each_other(do):
        def step(d, carry):
            other = lax.rem(here + d, nf * ns)
            do(remote(part(pay_out, owner), part(pay_out, owner), ag_s.at[0], ag_r.at[0],
                      sky=other // nf, freq=lax.rem(other, nf)))
            return carry

        lax.fori_loop(1, nf * ns, step, 0, unroll=nf * ns <= 16)

    each_owner(lambda one: one.start())
    @pl.when(owns)
    def _():
        rs[here] = pay[pl.ds(pl.multiple_of(owner * rows, 8), rows), :]
        some = rs.at[0:nf * ns - 1]
        pltpu.make_async_copy(some, some, rs_r.at[0]).wait()
        pay_out[pl.ds(pl.multiple_of(owner * rows, 8), rows), :] = jnp.sum(rs[...], axis=0)
        each_other(lambda one: one.start())

    dup.wait_recv()
    ddown.wait_recv()
    b = bw[...].astype(BF)
    for f in range(F):
        x = dr[f]
        rolled = dot(x, shift).astype(BF)
        full = jnp.concatenate([rolled[:, 128:256], x, rolled[:, 0:128]], axis=0)
        dl_ref[f] = dot(b, full).astype(BF)

    @pl.when(owns)
    def _():
        rest = pay_out.at[0:128 - rows]
        pltpu.make_async_copy(rest, rest, ag_r.at[0]).wait()

    @pl.when(jnp.logical_not(owns))
    def _():
        pltpu.make_async_copy(pay_out, pay_out, ag_r.at[0]).wait()

    up.wait_send()
    down.wait_send()
    dup.wait_send()
    ddown.wait_send()
    each_owner(lambda one: one.wait_send())

    @pl.when(owns)
    def _():
        each_other(lambda one: one.wait_send())

    for d in range(1, nf):
        @pl.when(me >= d)
        def _():
            dec_copy(d).wait_send()
    for h in range(2):
        for d in range(1, chips):
            @pl.when(chip >= d)
            def _():
                cot_copy(d, h).wait_send()

            @pl.when(chip + d < chips)
            def _():
                fwd_copy(d, h).wait_send()

        @pl.when(core == 1)
        def _():
            sib_copy(h).wait_send()


def finish(scale, dl_ref, pay_ref, in_ref, out_ref, dl_hbm, conv_hbm, din_hbm, dout_hbm, skip_hbm,
           conv_out, din_out, dout_out, skip_out, sems):
    copies = [
        pltpu.make_async_copy(src, dst, sems.at[i])
        for i, (src, dst) in enumerate((
            (dl_ref, dl_hbm), (conv_out, conv_hbm), (din_out, din_hbm), (dout_out, dout_hbm), (skip_out, skip_hbm)))
    ]
    copies[0].start()
    for dr in range(3):
        for k in range(3):
            at = (dr * 3 + k) * 32
            conv_out[:, at:at + 32] = pay_ref[k * 32:(k + 1) * 32, dr * 32:(dr + 1) * 32] * scale
    copies[1].start()
    t = jnp.concatenate([pay_ref[96 + k:97 + k, :] for k in range(4)], axis=1) * scale
    t = jnp.where(lax.rem(iota((16, 512), 1), 16) == iota((16, 512), 0), t, 0.0)
    join = (iota((512, 32), 0) // 16 == iota((512, 32), 1)).astype(F32)
    t = jnp.dot(t, join, precision=lax.Precision.HIGHEST, preferred_element_type=F32)
    din_out[...] = t * out_ref[...]
    dout_out[...] = t * in_ref[...]
    s = jnp.concatenate([pay_ref[100 + k:101 + k, :] for k in range(4)], axis=1) * scale
    s = jnp.where(lax.rem(iota((1, 512), 1), 16) == 0, s, 0.0)
    skip_out[...] = jnp.dot(s, join, precision=lax.Precision.HIGHEST, preferred_element_type=F32)
    for one in copies[2:]:
        one.start()
    for one in copies:
        one.wait()


def in_hbm(x):
    return pltpu.with_memory_space_constraint(x, pltpu.MemorySpace.HBM)


def per_device(lightcone, cotangent, conv_weight, in_proj, out_proj, skip_gain, decay):
    F, C, R, W = lightcone.shape
    N = in_proj.shape[1]
    nf, ns = lax.axis_size("freq"), lax.axis_size("sky")
    scale = 1.0 / float(F * nf * R * ns * W) ** 0.5
    owners = min(nf // 2 * ns, 16)
    dma = pltpu.SemaphoreType.DMA
    vm = pl.BlockSpec(memory_space=pltpu.VMEM)
    hbm = pl.BlockSpec(memory_space=pltpu.MemorySpace.HBM)
    dl, pay = pl.pallas_call(
        functools.partial(kernel, nf, ns),
        out_shape=(
            jax.ShapeDtypeStruct((F, C * R, W), BF),
            jax.ShapeDtypeStruct((128, 128), F32),
        ),
        in_specs=[hbm] * 7,
        out_specs=(vm, vm),
        scratch_shapes=[
            pltpu.VMEM((F, 4 * C, W), BF),
            pltpu.VMEM((nf, R, F * C, W), BF),
            pltpu.VMEM((nf, F, C * N), F32),
            pltpu.VMEM((2, F * 16, R * W), BF),
            pltpu.VMEM((F * F, C * N), F32),
            pltpu.VMEM((2 * F, 256), F32),
            pltpu.VMEM((F, C * N), F32),
            pltpu.VMEM((F, C * N), F32),
            pltpu.VMEM((2, F * 16, F * 16), BF),
            pltpu.VMEM((2, F * 16, 16 * N), BF),
            pltpu.VMEM((nf, 2, 16 * N, F * 16), BF),
            pltpu.VMEM((2, F * 16, R * W), F32),
            pltpu.VMEM((2, 16 * N, R * W), F32),
            pltpu.VMEM((2, 16 * N, R * W), BF),
            pltpu.VMEM((F, 4 * C, W), BF),
            pltpu.VMEM((128, 128), F32),
            pltpu.VMEM((nf * ns, 128 // owners, 128), F32),
            pltpu.VMEM((2 * C, 12 * C), BF),
            pltpu.VMEM((2 * C, 12 * C), F32),
            dma((2,)), dma((2,)), dma((2,)), dma((2,)),
            dma((nf,)), dma((nf,)), dma((nf, 2)), dma((nf, 2)), dma((nf, 2)),
            dma((1,)), dma((1,)), dma((1,)), dma((1,)),
            pltpu.VMEM((F, C * R, W), BF),
            pltpu.VMEM((F, C * R, W), BF),
            pltpu.VMEM((C, 9 * C), BF),
            pltpu.VMEM((N, C), F32),
            pltpu.VMEM((N, C), F32),
            pltpu.VMEM((1, C), F32),
            dma((7,)),
        ],
        compiler_params=pltpu.CompilerParams(
            collective_id=0, has_side_effects=True, vmem_limit_bytes=(12 + 2 * nf) << 20),
    )(*map(in_hbm, (lightcone.reshape(F, C * R, W), cotangent.reshape(F, C * R, W), conv_weight,
                    in_proj.T, out_proj.T, skip_gain.reshape(1, C), decay)))
    dl, grad, din, dout, d_skip = pl.pallas_call(
        functools.partial(finish, scale),
        out_shape=(
            jax.ShapeDtypeStruct((F, C * R, W), BF),
            jax.ShapeDtypeStruct((C, 9 * C), F32),
            jax.ShapeDtypeStruct((N, C), F32),
            jax.ShapeDtypeStruct((N, C), F32),
            jax.ShapeDtypeStruct((1, C), F32),
        ),
        in_specs=[vm] * 4,
        out_specs=(hbm,) * 5,
        scratch_shapes=[
            pltpu.VMEM((C, 9 * C), F32), pltpu.VMEM((N, C), F32), pltpu.VMEM((N, C), F32),
            pltpu.VMEM((1, C), F32), dma((5,))],
        compiler_params=pltpu.CompilerParams(vmem_limit_bytes=8 << 20),
    )(dl, pay, in_proj.T, out_proj.T)
    return dl.reshape(F, C, R, W), grad, din.T, dout.T, d_skip.reshape(C)


def solution(mesh):
    return jax.shard_map(
        per_device,
        mesh=mesh,
        in_specs=(
            P(("replica", "freq"), None, "sky", None),
            P(("replica", "freq"), None, "sky", None),
            P(),
            P(),
            P(),
            P(),
            P("freq", None),
        ),
        out_specs=(
            P(("replica", "freq"), None, "sky", None),
            P("replica", None),
            P("replica", None),
            P("replica", None),
            P("replica"),
        ),
        check_vma=False,
    )
```

```python
import functools

import jax
import jax.numpy as jnp
from jax import lax
from jax.experimental import pallas as pl
from jax.experimental.pallas import tpu as pltpu
from jax.sharding import PartitionSpec as P

MESH = pl.DeviceIdType.MESH
BF = jnp.bfloat16
F32 = jnp.float32


def dot(a, b):
    return jnp.dot(a, b, preferred_element_type=F32)


def dot_nt(a, b):
    return lax.dot_general(a, b, (((1,), (1,)), ((), ())), preferred_element_type=F32)


def iota(shape, dim):
    return lax.broadcasted_iota(jnp.int32, shape, dim)


def kernel(nf, ns, x_hbm, cot_hbm, w_hbm, in_hbm, out_hbm, skip_hbm, dec_hbm,
           dl_ref, pay_out,
           xr, cg, dg, inp, p3, k4, pe, qs, kb, nb, mb, own_d, adj, adj_bf, dr, pay, pay_bf, rs, aw, bw,
           halo_s, halo_r, dhalo_s, dhalo_r, dec_s, dec_r, cot_s, cot_r, fwd_s,
           rs_s, rs_r, ag_s, ag_r,
           x_ref, cot_ref, w_ref, in_ref, out_ref, skip_ref, load):
    F = x_ref.shape[0]
    half = F * 16
    me = lax.axis_index("freq")
    sky = lax.axis_index("sky")
    core = lax.rem(me, 2)
    chip = me // 2
    chips = nf // 2
    sibling = me + 1 - 2 * core
    nxt = lax.rem(sky + 1, ns)
    prv = lax.rem(sky + ns - 1, ns)
    rows = rs.shape[1]
    owners = pay.shape[0] // rows
    here = sky * nf + me
    owner = sky * chips + chip
    owns = jnp.logical_and(core == 1, owner < owners)

    loads = [
        pltpu.make_async_copy(src, dst, load.at[i])
        for i, (src, dst) in enumerate((
            (cot_hbm, cot_ref), (dec_hbm, dg.at[me]), (x_hbm, x_ref), (w_hbm, w_ref),
            (in_hbm, in_ref), (out_hbm, out_ref), (skip_hbm, skip_ref)))
    ]
    for one in loads:
        one.start()
    barrier = pltpu.get_barrier_semaphore()

    def greet(d, carry):
        other = lax.rem(here + d, nf * ns)
        pl.semaphore_signal(barrier, inc=1, device_id={"sky": other // nf, "freq": lax.rem(other, nf)},
                            device_id_type=MESH)
        return carry

    lax.fori_loop(1, nf * ns, greet, 0, unroll=nf * ns <= 16)

    pr, pc = iota((64, 64), 0), iota((64, 64), 1)
    perm = (pc == 2 * lax.rem(pr, 32) + pr // 32).astype(F32).astype(BF)
    loads[0].wait()
    for f in range(F):
        c2 = dot(perm, cot_ref[f]).astype(BF)
        for h in range(2):
            for hi in range(2):
                at = hi * half + f * 16
                cg[me, h, at:at + 16, :] = c2[h * 32 + hi * 16:h * 32 + hi * 16 + 16]
    loads[2].wait()
    for f in range(F):
        xr[f, 32:96, :] = dot(perm, x_ref[f]).astype(BF)
    for i in (1, 3, 4, 5, 6):
        loads[i].wait()
    pl.semaphore_wait(barrier, nf * ns - 1)

    def remote(src, dst, s, r, **where):
        return pltpu.make_async_remote_copy(
            src_ref=src, dst_ref=dst, send_sem=s, recv_sem=r, device_id=dict(where), device_id_type=MESH)

    def dec_copy(d):
        return remote(dg.at[me], dg.at[me], dec_s.at[d], dec_r.at[me], freq=jnp.maximum(me - d, 0))

    def cot_copy(d, h):
        target = jnp.maximum(chip - d, 0) * 2 + core
        return remote(cg.at[me, h], cg.at[me, h], cot_s.at[d, h], cot_r.at[me, h], freq=target)

    def sib_copy(h):
        return remote(cg.at[me, h], cg.at[me, h], cot_s.at[0, h], cot_r.at[me, h], freq=sibling)

    def slot_copy(slot, h, s):
        return remote(cg.at[slot, h], cg.at[slot, h], s, cot_r.at[slot, h], freq=sibling)

    def fwd_copy(d, h):
        slot = jnp.minimum(chip + d, chips - 1) * 2 + core
        return slot_copy(slot, h, fwd_s.at[d, h])

    up = remote(xr.at[:, 64:96], xr.at[:, 0:32], halo_s.at[0], halo_r.at[0], sky=nxt)
    down = remote(xr.at[:, 32:64], xr.at[:, 96:128], halo_s.at[1], halo_r.at[1], sky=prv)
    for d in range(1, nf):
        @pl.when(me >= d)
        def _():
            dec_copy(d).start()
    for h in range(2):
        for d in range(1, chips):
            @pl.when(chip >= d)
            def _():
                cot_copy(d, h).start()

        @pl.when(core == 1)
        def _():
            sib_copy(h).start()
    up.start()
    down.start()

    sr, sc = iota((128, 256), 0), iota((128, 256), 1)
    shift = jnp.logical_or(lax.rem(sr + 1, 128) == sc, lax.rem(sr + 127, 128) == sc - 128)
    shift = shift.astype(F32).astype(BF)

    spread = (iota((32, 512), 1) // 16 == iota((32, 512), 0)).astype(F32)
    io = jnp.dot(in_ref[...] * out_ref[...], spread, precision=lax.Precision.HIGHEST, preferred_element_type=F32)
    io = jnp.sum(jnp.where(lax.rem(iota((16, 512), 1), 16) == iota((16, 512), 0), io, 0.0), axis=0, keepdims=True)
    tr, tc = iota((32, 256), 0), iota((32, 256), 1)
    skips = jnp.where(tr == tc // 128 * 16 + lax.rem(tc, 16), 1.0, 0.0)
    skips = jnp.dot(skip_ref[...], skips, precision=lax.Precision.HIGHEST, preferred_element_type=F32)
    tr, tc = iota((512, 256), 0), iota((512, 256), 1)
    tile = (tr // 16 == tc // 128 * 16 + lax.rem(tc, 16)).astype(F32).astype(BF)

    fi = iota((F, 512), 0)
    v = jnp.zeros((F, 512), F32)
    for g in range(F):
        v = jnp.where(fi == g, 1.0, v * dg[me, g:g + 1, :])
        p3[g * F:(g + 1) * F, :] = v
    pe[...] = v * io
    kk = dot((p3[...] * io).astype(BF), tile)
    row16, lane16 = iota((F, 256), 0), lax.rem(iota((F, 256), 1), 128) // 16
    for G in range(2):
        k = jnp.where(row16 == lane16 + 8 * G, skips, 0.0)
        for j in range(8):
            at = (8 * G + j) * F
            k = k + jnp.where(lane16 == j, kk[at:at + F], 0.0)
        k4[G * F:(G + 1) * F, :] = k
    low_row = lax.rem(iota((16, 128), 1), 16) == iota((16, 128), 0)
    low_col = iota((16, 256), 1) // 16 == iota((16, 256), 0)
    for hi in range(2):
        for f in range(F):
            for G in range(2):
                row = jnp.broadcast_to(k4[G * F + f:G * F + f + 1, hi * 128:(hi + 1) * 128], (16, 128))
                kb[hi, f * 16:(f + 1) * 16, G * 128:(G + 1) * 128] = jnp.where(low_row, row, 0.0).astype(BF)
            row = jnp.broadcast_to(pe[f:f + 1, hi * 256:(hi + 1) * 256], (16, 256))
            nb[hi, f * 16:(f + 1) * 16, :] = jnp.where(low_col, row, 0.0).astype(BF)

    expand = low_col.astype(F32).astype(BF)
    kept = iota((256, 256), 0) // 16 == lax.rem(iota((256, 256), 1), 16)

    def later(q, run):
        remote(dg.at[q], dg.at[q], dec_s.at[0], dec_r.at[q], freq=sibling).wait_recv()
        for g in range(F):
            run = run * dg[q, g:g + 1, :]
            qs[g:g + 1, :] = run
        for hi in range(2):
            m = lax.dot_general(qs[:, hi * 256:(hi + 1) * 256].astype(BF), expand, (((0,), (0,)), ((), ())),
                                preferred_element_type=F32)
            mb[q, hi] = jnp.where(kept, m, 0.0).astype(BF)
        return run

    def cells(q, hi):
        at = slice(hi * half, (hi + 1) * half)
        return jnp.concatenate([cg[q, 0, at], cg[q, 1, at]], axis=1)

    for hi in range(2):
        own_d[hi] = dot(kb[hi], cells(me, hi))

    kk, ll = iota((288, 384), 0), iota((288, 384), 1)
    for r in range(2):
        tap = lax.rem(ll, 128) // 32 - r
        pick = jnp.logical_and(kk == (tap * 3 + ll // 128) * 32 + lax.rem(ll, 32),
                               jnp.logical_and(tap >= 0, tap <= 2))
        aw[r * 32:(r + 1) * 32, :] = dot(w_ref[...], pick.astype(F32).astype(BF)).astype(BF)
    mm, kk = iota((64, 288), 0), iota((64, 288), 1)
    for k in range(3):
        for row in range(4):
            tap = lax.rem(mm, 2) + 2 - row
            pick = jnp.logical_and(kk == (tap * 3 + k) * 32 + mm // 2,
                                   jnp.logical_and(tap >= 0, tap <= 2))
            at = k * 128 + row * 32
            bw[:, at:at + 32] = dot_nt(pick.astype(F32).astype(BF), w_ref[...])

    dup = remote(dr.at[:, 64:96], dr.at[:, 0:32], dhalo_s.at[1], dhalo_r.at[1], sky=nxt)
    ddown = remote(dr.at[:, 32:64], dr.at[:, 96:128], dhalo_s.at[0], dhalo_r.at[0], sky=prv)

    lax.fori_loop(me + 1, nf, later, jnp.ones((1, 512), F32))

    @pl.when(core == 0)
    def _():
        q = jnp.minimum(me + 1, nf - 1)
        for h in range(2):
            slot_copy(q, h, fwd_s.at[0, h]).wait_recv()
        for hi in range(2):
            adj[hi] = dot(mb[q, hi], cells(q, hi))

    @pl.when(core == 1)
    def _():
        adj[...] = jnp.zeros_like(adj)

    def forward(h):
        def step(k, carry):
            slot_copy(2 * k + core, h, fwd_s.at[0, h]).wait_recv()
            slot_copy(2 * k + core, h, fwd_s.at[k - chip, h]).start()
            return carry

        lax.fori_loop(chip + 1, chips, step, 0)

    def mix(h):
        wide = slice(h * 128, (h + 1) * 128)

        def step(k, carry):
            slot_copy(2 * k + 1 - core, h, fwd_s.at[0, h]).wait_recv()
            for hi in range(2):
                at = slice(hi * half, (hi + 1) * half)
                adj[hi, :, wide] += dot(mb[2 * k, hi], cg[2 * k, h, at]) + dot(mb[2 * k + 1, hi], cg[2 * k + 1, h, at])
            return carry

        lax.fori_loop(chip + 1, chips, step, 0)
        for hi in range(2):
            a = adj[hi, :, wide].astype(BF)
            adj_bf[hi, :, wide] = a
            d = (own_d[hi, :, wide] + dot(nb[hi], a)).astype(BF)
            at = 32 + 32 * h + 16 * hi
            for f in range(F):
                dr[f, at:at + 16, :] = d[f * 16:(f + 1) * 16]

    forward(0)
    mix(0)
    ddown.start()
    forward(1)
    up.wait_recv()
    down.wait_recv()
    for f in range(F):
        x = xr[f]
        rolled = dot(x, shift).astype(BF)
        full = jnp.concatenate([rolled[:, 0:128], x, rolled[:, 128:256]], axis=0)
        got = dot(aw[...], full).astype(BF)
        for r in range(2):
            for hi in range(2):
                inp[hi, f * 16:(f + 1) * 16, r * 128:(r + 1) * 128] = got[r * 32 + hi * 16:r * 32 + hi * 16 + 16]

    r256, l256 = iota((256, 256), 0), iota((256, 256), 1)
    same = lax.rem(r256, 16) == lax.rem(l256, 16)
    widen = (lax.rem(r256, 16) == l256 // 16).astype(F32).astype(BF)
    now = r256 // 16 == lax.rem(r256, 16)
    block_of = l256[0:16] // 16
    sums = []
    for hi in range(2):
        gram = jnp.where(same, dot_nt(inp[hi], cells(me, hi)), 0.0).astype(BF)
        rows_f = dot(expand, gram)
        stack = jnp.concatenate([jnp.where(block_of == g, rows_f, 0.0) for g in range(F)], axis=0).astype(BF)
        pairs = dot(stack, widen)
        sums.append(jnp.sum((pairs * p3[:, hi * 256:(hi + 1) * 256]).reshape(F * F // 8, 8, 256), axis=0))
        skip = jnp.sum(jnp.where(now, pairs, 0.0), axis=0, keepdims=True)
        for k in range(2):
            pay[100 + 2 * hi + k:101 + 2 * hi + k, :] = skip[:, k * 128:(k + 1) * 128]
    mix(1)
    for hi in range(2):
        gram = dot_nt(inp[hi], adj_bf[hi])
        total = sums[hi]
        for f in range(F):
            rows_f = jnp.where(low_col, gram[f * 16:(f + 1) * 16], 0.0)
            at = (F - 1) * F + f
            total = total + (rows_f[0:8] + rows_f[8:16]) * p3[at:at + 1, hi * 256:(hi + 1) * 256]
        t = jnp.sum(total, axis=0, keepdims=True)
        for k in range(2):
            pay[96 + 2 * hi + k:97 + 2 * hi + k, :] = t[:, k * 128:(k + 1) * 128]

    grad = jnp.zeros((192, 128), F32)
    for f in range(F):
        mid = dr[f, 32:96, :]
        rolled = dot(mid, shift).astype(BF)
        full = jnp.concatenate([rolled[:, 128:256], mid, rolled[:, 0:128]], axis=0)
        grad = grad + dot_nt(full, xr[f])
    for k in range(3):
        top = grad[k * 64:k * 64 + 32, 0:96]
        low = grad[k * 64 + 32:k * 64 + 64, 32:128]
        pay[k * 32:(k + 1) * 32, 0:96] = top + low
        pay[k * 32:(k + 1) * 32, 96:128] = jnp.zeros((32, 32), F32)
    pay[104:128, :] = jnp.zeros((24, 128), F32)

    def part(ref, i):
        return ref.at[pl.ds(pl.multiple_of(i * rows, 16), rows)]

    def each_owner(do):
        def step(d, carry):
            i = lax.rem(owner + d, owners)

            @pl.when(jnp.logical_not(jnp.logical_and(owns, i == owner)))
            def _():
                do(remote(part(pay_bf, i), rs.at[here], rs_s.at[0], rs_r.at[0],
                          sky=i // chips, freq=lax.rem(i, chips) * 2 + 1))

            return carry

        lax.fori_loop(0, owners, step, 0, unroll=owners <= 8)

    def each_other(do):
        def step(d, carry):
            other = lax.rem(here + d, nf * ns)
            do(remote(part(pay_out, owner), part(pay_out, owner), ag_s.at[0], ag_r.at[0],
                      sky=other // nf, freq=lax.rem(other, nf)))
            return carry

        lax.fori_loop(1, nf * ns, step, 0, unroll=nf * ns <= 16)

    pay_bf[...] = pay[...].astype(BF)
    each_owner(lambda one: one.start())
    dup.start()
    @pl.when(owns)
    def _():
        at = pl.ds(pl.multiple_of(owner * rows, 16), rows)
        rs[here] = pay_bf[at, :]
        some = rs.at[0:nf * ns - 1]
        pltpu.make_async_copy(some, some, rs_r.at[0]).wait()
        pay_out[at, :] = jnp.sum(rs[...].astype(F32), axis=0).astype(BF)
        each_other(lambda one: one.start())

    dup.wait_recv()
    ddown.wait_recv()
    b = bw[...].astype(BF)
    for f in range(F):
        x = dr[f]
        rolled = dot(x, shift).astype(BF)
        full = jnp.concatenate([rolled[:, 128:256], x, rolled[:, 0:128]], axis=0)
        dl_ref[f] = dot(b, full).astype(BF)

    @pl.when(owns)
    def _():
        rest = pay_out.at[0:128 - rows]
        pltpu.make_async_copy(rest, rest, ag_r.at[0]).wait()

    @pl.when(jnp.logical_not(owns))
    def _():
        pltpu.make_async_copy(pay_out, pay_out, ag_r.at[0]).wait()

    up.wait_send()
    down.wait_send()
    dup.wait_send()
    ddown.wait_send()
    each_owner(lambda one: one.wait_send())

    @pl.when(owns)
    def _():
        each_other(lambda one: one.wait_send())

    for d in range(1, nf):
        @pl.when(me >= d)
        def _():
            dec_copy(d).wait_send()
    for h in range(2):
        for d in range(1, chips):
            @pl.when(chip >= d)
            def _():
                cot_copy(d, h).wait_send()

            @pl.when(chip + d < chips)
            def _():
                fwd_copy(d, h).wait_send()

        @pl.when(core == 1)
        def _():
            sib_copy(h).wait_send()


def finish(scale, dl_ref, pay_ref, in_ref, out_ref, dl_hbm, conv_hbm, din_hbm, dout_hbm, skip_hbm,
           conv_out, din_out, dout_out, skip_out, pay, sems):
    copies = [
        pltpu.make_async_copy(src, dst, sems.at[i])
        for i, (src, dst) in enumerate((
            (dl_ref, dl_hbm), (conv_out, conv_hbm), (din_out, din_hbm), (dout_out, dout_hbm), (skip_out, skip_hbm)))
    ]
    copies[0].start()
    pay[...] = pay_ref[...].astype(F32)
    for dr in range(3):
        for k in range(3):
            at = (dr * 3 + k) * 32
            conv_out[:, at:at + 32] = pay[k * 32:(k + 1) * 32, dr * 32:(dr + 1) * 32] * scale
    copies[1].start()
    t = jnp.concatenate([pay[96 + k:97 + k, :] for k in range(4)], axis=1) * scale
    t = jnp.where(lax.rem(iota((16, 512), 1), 16) == iota((16, 512), 0), t, 0.0)
    join = (iota((512, 32), 0) // 16 == iota((512, 32), 1)).astype(F32)
    t = jnp.dot(t, join, precision=lax.Precision.HIGHEST, preferred_element_type=F32)
    din_out[...] = t * out_ref[...]
    dout_out[...] = t * in_ref[...]
    s = jnp.concatenate([pay[100 + k:101 + k, :] for k in range(4)], axis=1) * scale
    s = jnp.where(lax.rem(iota((1, 512), 1), 16) == 0, s, 0.0)
    skip_out[...] = jnp.dot(s, join, precision=lax.Precision.HIGHEST, preferred_element_type=F32)
    for one in copies[2:]:
        one.start()
    for one in copies:
        one.wait()


def in_hbm(x):
    return pltpu.with_memory_space_constraint(x, pltpu.MemorySpace.HBM)


def per_device(lightcone, cotangent, conv_weight, in_proj, out_proj, skip_gain, decay):
    F, C, R, W = lightcone.shape
    N = in_proj.shape[1]
    nf, ns = lax.axis_size("freq"), lax.axis_size("sky")
    scale = 1.0 / float(F * nf * R * ns * W) ** 0.5
    owners = min(nf // 2 * ns, 8)
    dma = pltpu.SemaphoreType.DMA
    vm = pl.BlockSpec(memory_space=pltpu.VMEM)
    hbm = pl.BlockSpec(memory_space=pltpu.MemorySpace.HBM)
    dl, pay = pl.pallas_call(
        functools.partial(kernel, nf, ns),
        out_shape=(
            jax.ShapeDtypeStruct((F, C * R, W), BF),
            jax.ShapeDtypeStruct((128, 128), BF),
        ),
        in_specs=[hbm] * 7,
        out_specs=(vm, vm),
        scratch_shapes=[
            pltpu.VMEM((F, 4 * C, W), BF),
            pltpu.VMEM((nf, R, F * C, W), BF),
            pltpu.VMEM((nf, F, C * N), F32),
            pltpu.VMEM((2, F * 16, R * W), BF),
            pltpu.VMEM((F * F, C * N), F32),
            pltpu.VMEM((2 * F, 256), F32),
            pltpu.VMEM((F, C * N), F32),
            pltpu.VMEM((F, C * N), F32),
            pltpu.VMEM((2, F * 16, F * 16), BF),
            pltpu.VMEM((2, F * 16, 16 * N), BF),
            pltpu.VMEM((nf, 2, 16 * N, F * 16), BF),
            pltpu.VMEM((2, F * 16, R * W), F32),
            pltpu.VMEM((2, 16 * N, R * W), F32),
            pltpu.VMEM((2, 16 * N, R * W), BF),
            pltpu.VMEM((F, 4 * C, W), BF),
            pltpu.VMEM((128, 128), F32),
            pltpu.VMEM((128, 128), BF),
            pltpu.VMEM((nf * ns, 128 // owners, 128), BF),
            pltpu.VMEM((2 * C, 12 * C), BF),
            pltpu.VMEM((2 * C, 12 * C), F32),
            dma((2,)), dma((2,)), dma((2,)), dma((2,)),
            dma((nf,)), dma((nf,)), dma((nf, 2)), dma((nf, 2)), dma((nf, 2)),
            dma((1,)), dma((1,)), dma((1,)), dma((1,)),
            pltpu.VMEM((F, C * R, W), BF),
            pltpu.VMEM((F, C * R, W), BF),
            pltpu.VMEM((C, 9 * C), BF),
            pltpu.VMEM((N, C), F32),
            pltpu.VMEM((N, C), F32),
            pltpu.VMEM((1, C), F32),
            dma((7,)),
        ],
        compiler_params=pltpu.CompilerParams(
            collective_id=0, has_side_effects=True, vmem_limit_bytes=(12 + 2 * nf) << 20),
    )(*map(in_hbm, (lightcone.reshape(F, C * R, W), cotangent.reshape(F, C * R, W), conv_weight,
                    in_proj.T, out_proj.T, skip_gain.reshape(1, C), decay)))
    dl, grad, din, dout, d_skip = pl.pallas_call(
        functools.partial(finish, scale),
        out_shape=(
            jax.ShapeDtypeStruct((F, C * R, W), BF),
            jax.ShapeDtypeStruct((C, 9 * C), F32),
            jax.ShapeDtypeStruct((N, C), F32),
            jax.ShapeDtypeStruct((N, C), F32),
            jax.ShapeDtypeStruct((1, C), F32),
        ),
        in_specs=[vm] * 4,
        out_specs=(hbm,) * 5,
        scratch_shapes=[
            pltpu.VMEM((C, 9 * C), F32), pltpu.VMEM((N, C), F32), pltpu.VMEM((N, C), F32),
            pltpu.VMEM((1, C), F32), pltpu.VMEM((128, 128), F32), dma((5,))],
        compiler_params=pltpu.CompilerParams(vmem_limit_bytes=8 << 20),
    )(dl, pay, in_proj.T, out_proj.T)
    return dl.reshape(F, C, R, W), grad, din.T, dout.T, d_skip.reshape(C)


def solution(mesh):
    return jax.shard_map(
        per_device,
        mesh=mesh,
        in_specs=(
            P(("replica", "freq"), None, "sky", None),
            P(("replica", "freq"), None, "sky", None),
            P(),
            P(),
            P(),
            P(),
            P("freq", None),
        ),
        out_specs=(
            P(("replica", "freq"), None, "sky", None),
            P("replica", None),
            P("replica", None),
            P("replica", None),
            P("replica"),
        ),
        check_vma=False,
    )
```

```python
import functools

import jax
import jax.numpy as jnp
from jax import lax
from jax.experimental import pallas as pl
from jax.experimental.pallas import tpu as pltpu
from jax.sharding import PartitionSpec as P

MESH = pl.DeviceIdType.MESH
BF = jnp.bfloat16
F32 = jnp.float32


def dot(a, b):
    return jnp.dot(a, b, preferred_element_type=F32)


def dot_nt(a, b):
    return lax.dot_general(a, b, (((1,), (1,)), ((), ())), preferred_element_type=F32)


def iota(shape, dim):
    return lax.broadcasted_iota(jnp.int32, shape, dim)


def kernel(nf, ns, x_hbm, cot_hbm, w_hbm, in_hbm, out_hbm, skip_hbm, dec_hbm,
           dl_ref, pay_out,
           xr, cg, dg, inp, p3, k4, pe, qs, kb, nb, mb, dm, own_d, adj, adj_bf, ab, ab_out, dr, pay, pay_bf, rs, aw, bw,
           halo_s, halo_r, dhalo_s, dhalo_r, dec_s, dec_r, cot_s, cot_r, ab_s, ab_r,
           rs_s, rs_r, ag_s, ag_r,
           x_ref, cot_ref, w_ref, in_ref, out_ref, skip_ref, load):
    F = x_ref.shape[0]
    half = F * 16
    me = lax.axis_index("freq")
    sky = lax.axis_index("sky")
    core = lax.rem(me, 2)
    chip = me // 2
    chips = nf // 2
    sibling = me + 1 - 2 * core
    nxt = lax.rem(sky + 1, ns)
    prv = lax.rem(sky + ns - 1, ns)
    rows = rs.shape[1]
    owners = pay.shape[0] // rows
    here = sky * nf + me
    owner = sky * chips + chip
    owns = jnp.logical_and(core == 1, owner < owners)

    loads = [
        pltpu.make_async_copy(src, dst, load.at[i])
        for i, (src, dst) in enumerate((
            (cot_hbm, cot_ref), (dec_hbm, dg.at[core]), (x_hbm, x_ref), (w_hbm, w_ref),
            (in_hbm, in_ref), (out_hbm, out_ref), (skip_hbm, skip_ref)))
    ]
    for one in loads:
        one.start()
    barrier = pltpu.get_barrier_semaphore()

    def greet(d, carry):
        other = lax.rem(here + d, nf * ns)
        pl.semaphore_signal(barrier, inc=1, device_id={"sky": other // nf, "freq": lax.rem(other, nf)},
                            device_id_type=MESH)
        return carry

    lax.fori_loop(1, nf * ns, greet, 0, unroll=nf * ns <= 16)

    pr, pc = iota((64, 64), 0), iota((64, 64), 1)
    perm = (pc == 2 * lax.rem(pr, 32) + pr // 32).astype(F32).astype(BF)
    loads[0].wait()
    for f in range(F):
        c2 = dot(perm, cot_ref[f]).astype(BF)
        for h in range(2):
            for hi in range(2):
                at = hi * half + f * 16
                cg[core, h, at:at + 16, :] = c2[h * 32 + hi * 16:h * 32 + hi * 16 + 16]
    loads[1].wait()
    pl.semaphore_wait(barrier, nf * ns - 1)

    def remote(src, dst, s, r, **where):
        return pltpu.make_async_remote_copy(
            src_ref=src, dst_ref=dst, send_sem=s, recv_sem=r, device_id=dict(where), device_id_type=MESH)

    first, last = chip == 0, chip == chips - 1

    def dec_copy(slot):
        return remote(dg.at[slot], dg.at[slot], dec_s.at[0], dec_r.at[0], freq=sibling)

    def cot_copy(slot, h):
        return remote(cg.at[slot, h], cg.at[slot, h], cot_s.at[h], cot_r.at[h], freq=sibling)

    def adj_copy():
        return remote(ab_out, ab.at[core], ab_s.at[0], ab_r.at[core], freq=jnp.maximum(me - 2, 0))

    def fwd_copy(slot):
        return remote(ab.at[slot], ab.at[slot], ab_s.at[1], ab_r.at[slot], freq=sibling)

    up = remote(xr.at[:, 64:96], xr.at[:, 0:32], halo_s.at[0], halo_r.at[0], sky=nxt)
    down = remote(xr.at[:, 32:64], xr.at[:, 96:128], halo_s.at[1], halo_r.at[1], sky=prv)
    dec_copy(core).start()

    @pl.when(core == 1)
    def _():
        cot_copy(core, 0).start()
        cot_copy(core, 1).start()

    @pl.when(jnp.logical_and(core == 0, jnp.logical_not(first)))
    def _():
        cot_copy(core, 1).start()

    loads[2].wait()
    for f in range(F):
        xr[f, 32:96, :] = dot(perm, x_ref[f]).astype(BF)
    up.start()
    down.start()
    for i in (3, 4, 5, 6):
        loads[i].wait()

    sr, sc = iota((128, 256), 0), iota((128, 256), 1)
    shift = jnp.logical_or(lax.rem(sr + 1, 128) == sc, lax.rem(sr + 127, 128) == sc - 128)
    shift = shift.astype(F32).astype(BF)

    low_row = lax.rem(iota((16, 128), 1), 16) == iota((16, 128), 0)
    low_col = iota((16, 256), 1) // 16 == iota((16, 256), 0)
    expand = low_col.astype(F32).astype(BF)
    r256, l256 = iota((256, 256), 0), iota((256, 256), 1)
    kept = r256 // 16 == lax.rem(l256, 16)

    def group(hi):
        return slice(hi * half, (hi + 1) * half)

    def decayed(to, slot, run):
        for g in range(F):
            run = run * dg[slot, g:g + 1, :]
            qs[g:g + 1, :] = run
        for hi in range(2):
            m = lax.dot_general(qs[:, hi * 256:(hi + 1) * 256].astype(BF), expand, (((0,), (0,)), ((), ())),
                                preferred_element_type=F32)
            mb[to, hi] = jnp.where(kept, m, 0.0).astype(BF)
        return run

    def diagonal(to, run):
        for hi in range(2):
            dm[to, hi] = jnp.where(r256 == l256, run[:, hi * 256:(hi + 1) * 256], 0.0).astype(BF)

    def take():
        fwd_copy(core).wait_recv()
        fwd_copy(core).start()

    dec_copy(1 - core).wait_recv()

    @pl.when(jnp.logical_not(first))
    def _():
        run = decayed(1, 0, jnp.ones((1, 512), F32))
        run = decayed(2, 1, run)
        cot_copy(1 - core, core).wait_recv()
        for hi in range(2):
            adj[0, hi] = dot(mb[1, hi], cg[0, core, group(hi)]) + dot(mb[2, hi], cg[1, core, group(hi)])

        @pl.when(jnp.logical_not(last))
        def _():
            diagonal(1, run)
            take()
            for hi in range(2):
                adj[0, hi] += dot(dm[1, hi], ab[core, hi])

        ab_out[...] = adj[0].astype(BF)
        adj_copy().start()

    @pl.when(last)
    def _():
        ab[...] = jnp.zeros_like(ab)

    spread = (iota((32, 512), 1) // 16 == iota((32, 512), 0)).astype(F32)
    io = jnp.dot(in_ref[...] * out_ref[...], spread, precision=lax.Precision.HIGHEST, preferred_element_type=F32)
    io = jnp.sum(jnp.where(lax.rem(iota((16, 512), 1), 16) == iota((16, 512), 0), io, 0.0), axis=0, keepdims=True)
    tr, tc = iota((32, 256), 0), iota((32, 256), 1)
    skips = jnp.where(tr == tc // 128 * 16 + lax.rem(tc, 16), 1.0, 0.0)
    skips = jnp.dot(skip_ref[...], skips, precision=lax.Precision.HIGHEST, preferred_element_type=F32)
    tr, tc = iota((512, 256), 0), iota((512, 256), 1)
    tile = (tr // 16 == tc // 128 * 16 + lax.rem(tc, 16)).astype(F32).astype(BF)

    fi = iota((F, 512), 0)
    v = jnp.zeros((F, 512), F32)
    for g in range(F):
        v = jnp.where(fi == g, 1.0, v * dg[core, g:g + 1, :])
        p3[g * F:(g + 1) * F, :] = v
    pe[...] = v * io
    kk = dot((p3[...] * io).astype(BF), tile)
    row16, lane16 = iota((F, 256), 0), lax.rem(iota((F, 256), 1), 128) // 16
    for G in range(2):
        k = jnp.where(row16 == lane16 + 8 * G, skips, 0.0)
        for j in range(8):
            at = (8 * G + j) * F
            k = k + jnp.where(lane16 == j, kk[at:at + F], 0.0)
        k4[G * F:(G + 1) * F, :] = k
    for hi in range(2):
        for f in range(F):
            for G in range(2):
                row = jnp.broadcast_to(k4[G * F + f:G * F + f + 1, hi * 128:(hi + 1) * 128], (16, 128))
                kb[hi, f * 16:(f + 1) * 16, G * 128:(G + 1) * 128] = jnp.where(low_row, row, 0.0).astype(BF)
            row = jnp.broadcast_to(pe[f:f + 1, hi * 256:(hi + 1) * 256], (16, 256))
            nb[hi, f * 16:(f + 1) * 16, :] = jnp.where(low_col, row, 0.0).astype(BF)

    def cells(slot, hi):
        return jnp.concatenate([cg[slot, 0, group(hi)], cg[slot, 1, group(hi)]], axis=1)

    for hi in range(2):
        d = dot(kb[hi], cells(core, hi))
        own_d[0, hi] = d[:, 0:128]
        own_d[1, hi] = d[:, 128:256]

    @pl.when(core == 0)
    def _():
        diagonal(0, decayed(0, 1, jnp.ones((1, 512), F32)))
        pl.when(first)(cot_copy(1, 0).wait_recv)
        cot_copy(1, 1).wait_recv()
        for hi in range(2):
            a = dot(mb[0, hi], cells(1, hi))
            adj[0, hi] = a[:, 0:128]
            adj[1, hi] = a[:, 128:256]

    kk, ll = iota((288, 384), 0), iota((288, 384), 1)
    for r in range(2):
        tap = lax.rem(ll, 128) // 32 - r
        pick = jnp.logical_and(kk == (tap * 3 + ll // 128) * 32 + lax.rem(ll, 32),
                               jnp.logical_and(tap >= 0, tap <= 2))
        aw[r * 32:(r + 1) * 32, :] = dot(w_ref[...], pick.astype(F32).astype(BF)).astype(BF)
    mm, kk = iota((64, 288), 0), iota((64, 288), 1)
    for k in range(3):
        for row in range(4):
            tap = lax.rem(mm, 2) + 2 - row
            pick = jnp.logical_and(kk == (tap * 3 + k) * 32 + mm // 2,
                                   jnp.logical_and(tap >= 0, tap <= 2))
            at = k * 128 + row * 32
            bw[:, at:at + 32] = dot_nt(pick.astype(F32).astype(BF), w_ref[...])

    dup = remote(dr.at[:, 64:96], dr.at[:, 0:32], dhalo_s.at[1], dhalo_r.at[1], sky=nxt)
    ddown = remote(dr.at[:, 32:64], dr.at[:, 96:128], dhalo_s.at[0], dhalo_r.at[0], sky=prv)

    def mix(h):
        @pl.when(core == 0)
        def _():
            for hi in range(2):
                adj_bf[h, hi] = (adj[h, hi] + dot(dm[0, hi], ab[h, hi])).astype(BF)

        @pl.when(core == 1)
        def _():
            adj_bf[h] = ab[h]

        for hi in range(2):
            d = (own_d[h, hi] + dot(nb[hi], adj_bf[h, hi])).astype(BF)
            at = pl.multiple_of(32 + 32 * h + 16 * hi, 16)
            for f in range(F):
                dr[f, pl.ds(at, 16), :] = d[f * 16:(f + 1) * 16]

    pl.when(first)(take)
    mix(core)
    pl.when(core == 0)(ddown.start)
    pl.when(core == 1)(dup.start)
    up.wait_recv()
    down.wait_recv()
    for f in range(F):
        x = xr[f]
        rolled = dot(x, shift).astype(BF)
        full = jnp.concatenate([rolled[:, 0:128], x, rolled[:, 128:256]], axis=0)
        got = dot(aw[...], full).astype(BF)
        for r in range(2):
            for hi in range(2):
                inp[hi, f * 16:(f + 1) * 16, r * 128:(r + 1) * 128] = got[r * 32 + hi * 16:r * 32 + hi * 16 + 16]

    same = lax.rem(r256, 16) == lax.rem(l256, 16)
    widen = (lax.rem(r256, 16) == l256 // 16).astype(F32).astype(BF)
    now = r256 // 16 == lax.rem(r256, 16)
    block_of = l256[0:16] // 16
    sums = []
    for hi in range(2):
        gram = jnp.where(same, dot_nt(inp[hi], cells(core, hi)), 0.0).astype(BF)
        rows_f = dot(expand, gram)
        stack = jnp.concatenate([jnp.where(block_of == g, rows_f, 0.0) for g in range(F)], axis=0).astype(BF)
        pairs = dot(stack, widen)
        sums.append(jnp.sum((pairs * p3[:, hi * 256:(hi + 1) * 256]).reshape(F * F // 8, 8, 256), axis=0))
        skip = jnp.sum(jnp.where(now, pairs, 0.0), axis=0, keepdims=True)
        for k in range(2):
            pay[100 + 2 * hi + k:101 + 2 * hi + k, :] = skip[:, k * 128:(k + 1) * 128]
    pl.when(jnp.logical_not(last))(fwd_copy(1 - core).wait_recv)
    mix(1 - core)
    for hi in range(2):
        gram = dot_nt(inp[hi], jnp.concatenate([adj_bf[0, hi], adj_bf[1, hi]], axis=1))
        total = sums[hi]
        for f in range(F):
            rows_f = jnp.where(low_col, gram[f * 16:(f + 1) * 16], 0.0)
            at = (F - 1) * F + f
            total = total + (rows_f[0:8] + rows_f[8:16]) * p3[at:at + 1, hi * 256:(hi + 1) * 256]
        t = jnp.sum(total, axis=0, keepdims=True)
        for k in range(2):
            pay[96 + 2 * hi + k:97 + 2 * hi + k, :] = t[:, k * 128:(k + 1) * 128]

    grad = jnp.zeros((192, 128), F32)
    for f in range(F):
        mid = dr[f, 32:96, :]
        rolled = dot(mid, shift).astype(BF)
        full = jnp.concatenate([rolled[:, 128:256], mid, rolled[:, 0:128]], axis=0)
        grad = grad + dot_nt(full, xr[f])
    for k in range(3):
        top = grad[k * 64:k * 64 + 32, 0:96]
        low = grad[k * 64 + 32:k * 64 + 64, 32:128]
        pay[k * 32:(k + 1) * 32, 0:96] = top + low
        pay[k * 32:(k + 1) * 32, 96:128] = jnp.zeros((32, 32), F32)

    def part(ref, i):
        return ref.at[pl.ds(pl.multiple_of(i * rows, 16), rows)]

    def each_owner(do):
        def step(d, carry):
            i = lax.rem(owner + d, owners)

            @pl.when(jnp.logical_not(jnp.logical_and(owns, i == owner)))
            def _():
                do(remote(part(pay_bf, i), rs.at[here], rs_s.at[0], rs_r.at[0],
                          sky=i // chips, freq=lax.rem(i, chips) * 2 + 1))

            return carry

        lax.fori_loop(0, owners, step, 0, unroll=owners <= 8)

    def each_other(do):
        def step(d, carry):
            other = lax.rem(here + d, nf * ns)
            do(remote(part(pay_out, owner), part(pay_out, owner), ag_s.at[0], ag_r.at[0],
                      sky=other // nf, freq=lax.rem(other, nf)))
            return carry

        lax.fori_loop(1, nf * ns, step, 0, unroll=nf * ns <= 16)

    pay_bf[0:96, :] = pay[0:96, :].astype(BF)
    small = pay[96:104, :]
    high = small.astype(BF).astype(F32)
    pay_bf[96:112, :] = jnp.concatenate([high, small - high], axis=0).astype(BF)
    pay_bf[112:128, :] = jnp.zeros((16, 128), BF)
    each_owner(lambda one: one.start())
    pl.when(core == 0)(dup.start)
    pl.when(core == 1)(ddown.start)
    @pl.when(owns)
    def _():
        at = pl.ds(pl.multiple_of(owner * rows, 16), rows)
        rs[here] = pay_bf[at, :]
        some = rs.at[0:nf * ns - 1]
        pltpu.make_async_copy(some, some, rs_r.at[0]).wait()
        total = jnp.sum(rs[...].astype(F32), axis=0)
        small = total[0:8] + total[8:16]
        high = small.astype(BF).astype(F32)
        pair = jnp.concatenate([high, small - high], axis=0)
        pay_out[at, :] = jnp.where(owner * rows == 96, pair, total).astype(BF)
        each_other(lambda one: one.start())

    dup.wait_recv()
    ddown.wait_recv()
    b = bw[...].astype(BF)
    for f in range(F):
        x = dr[f]
        rolled = dot(x, shift).astype(BF)
        full = jnp.concatenate([rolled[:, 128:256], x, rolled[:, 0:128]], axis=0)
        dl_ref[f] = dot(b, full).astype(BF)

    @pl.when(owns)
    def _():
        rest = pay_out.at[0:128 - rows]
        pltpu.make_async_copy(rest, rest, ag_r.at[0]).wait()

    @pl.when(jnp.logical_not(owns))
    def _():
        pltpu.make_async_copy(pay_out, pay_out, ag_r.at[0]).wait()

    up.wait_send()
    down.wait_send()
    dup.wait_send()
    ddown.wait_send()
    each_owner(lambda one: one.wait_send())

    @pl.when(owns)
    def _():
        each_other(lambda one: one.wait_send())

    dec_copy(core).wait_send()

    @pl.when(core == 1)
    def _():
        cot_copy(core, 0).wait_send()
        cot_copy(core, 1).wait_send()

    @pl.when(jnp.logical_and(core == 0, jnp.logical_not(first)))
    def _():
        cot_copy(core, 1).wait_send()

    pl.when(jnp.logical_not(first))(adj_copy().wait_send)
    pl.when(jnp.logical_not(last))(fwd_copy(core).wait_send)


def finish(scale, dl_ref, pay_ref, in_ref, out_ref, dl_hbm, conv_hbm, din_hbm, dout_hbm, skip_hbm,
           conv_out, din_out, dout_out, skip_out, pay, sems):
    copies = [
        pltpu.make_async_copy(src, dst, sems.at[i])
        for i, (src, dst) in enumerate((
            (dl_ref, dl_hbm), (conv_out, conv_hbm), (din_out, din_hbm), (dout_out, dout_hbm), (skip_out, skip_hbm)))
    ]
    copies[0].start()
    pay[...] = pay_ref[...].astype(F32)
    pay[96:104, :] += pay[104:112, :]
    for dr in range(3):
        for k in range(3):
            at = (dr * 3 + k) * 32
            conv_out[:, at:at + 32] = pay[k * 32:(k + 1) * 32, dr * 32:(dr + 1) * 32] * scale
    copies[1].start()
    t = jnp.concatenate([pay[96 + k:97 + k, :] for k in range(4)], axis=1) * scale
    t = jnp.where(lax.rem(iota((16, 512), 1), 16) == iota((16, 512), 0), t, 0.0)
    join = (iota((512, 32), 0) // 16 == iota((512, 32), 1)).astype(F32)
    t = jnp.dot(t, join, precision=lax.Precision.HIGHEST, preferred_element_type=F32)
    din_out[...] = t * out_ref[...]
    dout_out[...] = t * in_ref[...]
    s = jnp.concatenate([pay[100 + k:101 + k, :] for k in range(4)], axis=1) * scale
    s = jnp.where(lax.rem(iota((1, 512), 1), 16) == 0, s, 0.0)
    skip_out[...] = jnp.dot(s, join, precision=lax.Precision.HIGHEST, preferred_element_type=F32)
    for one in copies[2:]:
        one.start()
    for one in copies:
        one.wait()


def in_hbm(x):
    return pltpu.with_memory_space_constraint(x, pltpu.MemorySpace.HBM)


def per_device(lightcone, cotangent, conv_weight, in_proj, out_proj, skip_gain, decay):
    F, C, R, W = lightcone.shape
    N = in_proj.shape[1]
    nf, ns = lax.axis_size("freq"), lax.axis_size("sky")
    scale = 1.0 / float(F * nf * R * ns * W) ** 0.5
    owners = min(nf // 2 * ns, 8)
    dma = pltpu.SemaphoreType.DMA
    vm = pl.BlockSpec(memory_space=pltpu.VMEM)
    hbm = pl.BlockSpec(memory_space=pltpu.MemorySpace.HBM)
    dl, pay = pl.pallas_call(
        functools.partial(kernel, nf, ns),
        out_shape=(
            jax.ShapeDtypeStruct((F, C * R, W), BF),
            jax.ShapeDtypeStruct((128, 128), BF),
        ),
        in_specs=[hbm] * 7,
        out_specs=(vm, vm),
        scratch_shapes=[
            pltpu.VMEM((F, 4 * C, W), BF),
            pltpu.VMEM((2, R, F * C, W), BF),
            pltpu.VMEM((2, F, C * N), F32),
            pltpu.VMEM((2, F * 16, R * W), BF),
            pltpu.VMEM((F * F, C * N), F32),
            pltpu.VMEM((2 * F, 256), F32),
            pltpu.VMEM((F, C * N), F32),
            pltpu.VMEM((F, C * N), F32),
            pltpu.VMEM((2, F * 16, F * 16), BF),
            pltpu.VMEM((2, F * 16, 16 * N), BF),
            pltpu.VMEM((3, 2, 16 * N, F * 16), BF),
            pltpu.VMEM((2, 2, 16 * N, 16 * N), BF),
            pltpu.VMEM((R, 2, F * 16, W), F32),
            pltpu.VMEM((R, 2, 16 * N, W), F32),
            pltpu.VMEM((R, 2, 16 * N, W), BF),
            pltpu.VMEM((R, 2, 16 * N, W), BF),
            pltpu.VMEM((2, 16 * N, W), BF),
            pltpu.VMEM((F, 4 * C, W), BF),
            pltpu.VMEM((128, 128), F32),
            pltpu.VMEM((128, 128), BF),
            pltpu.VMEM((nf * ns, 128 // owners, 128), BF),
            pltpu.VMEM((2 * C, 12 * C), BF),
            pltpu.VMEM((2 * C, 12 * C), F32),
            dma((2,)), dma((2,)), dma((2,)), dma((2,)),
            dma((1,)), dma((1,)), dma((2,)), dma((2,)), dma((2,)), dma((2,)),
            dma((1,)), dma((1,)), dma((1,)), dma((1,)),
            pltpu.VMEM((F, C * R, W), BF),
            pltpu.VMEM((F, C * R, W), BF),
            pltpu.VMEM((C, 9 * C), BF),
            pltpu.VMEM((N, C), F32),
            pltpu.VMEM((N, C), F32),
            pltpu.VMEM((1, C), F32),
            dma((7,)),
        ],
        compiler_params=pltpu.CompilerParams(
            collective_id=0, has_side_effects=True, vmem_limit_bytes=16 << 20),
    )(*map(in_hbm, (lightcone.reshape(F, C * R, W), cotangent.reshape(F, C * R, W), conv_weight,
                    in_proj.T, out_proj.T, skip_gain.reshape(1, C), decay)))
    dl, grad, din, dout, d_skip = pl.pallas_call(
        functools.partial(finish, scale),
        out_shape=(
            jax.ShapeDtypeStruct((F, C * R, W), BF),
            jax.ShapeDtypeStruct((C, 9 * C), F32),
            jax.ShapeDtypeStruct((N, C), F32),
            jax.ShapeDtypeStruct((N, C), F32),
            jax.ShapeDtypeStruct((1, C), F32),
        ),
        in_specs=[vm] * 4,
        out_specs=(hbm,) * 5,
        scratch_shapes=[
            pltpu.VMEM((C, 9 * C), F32), pltpu.VMEM((N, C), F32), pltpu.VMEM((N, C), F32),
            pltpu.VMEM((1, C), F32), pltpu.VMEM((128, 128), F32), dma((5,))],
        compiler_params=pltpu.CompilerParams(vmem_limit_bytes=8 << 20),
    )(dl, pay, in_proj.T, out_proj.T)
    return dl.reshape(F, C, R, W), grad, din.T, dout.T, d_skip.reshape(C)


def solution(mesh):
    return jax.shard_map(
        per_device,
        mesh=mesh,
        in_specs=(
            P(("replica", "freq"), None, "sky", None),
            P(("replica", "freq"), None, "sky", None),
            P(),
            P(),
            P(),
            P(),
            P("freq", None),
        ),
        out_specs=(
            P(("replica", "freq"), None, "sky", None),
            P("replica", None),
            P("replica", None),
            P("replica", None),
            P("replica"),
        ),
        check_vma=False,
    )
```

```python
import functools

import jax
import jax.numpy as jnp
from jax import lax
from jax.experimental import pallas as pl
from jax.experimental.pallas import tpu as pltpu
from jax.sharding import PartitionSpec as P

MESH = pl.DeviceIdType.MESH
BF = jnp.bfloat16
F32 = jnp.float32


def dot(a, b):
    return jnp.dot(a, b, preferred_element_type=F32)


def dot_nt(a, b):
    return lax.dot_general(a, b, (((1,), (1,)), ((), ())), preferred_element_type=F32)


def iota(shape, dim):
    return lax.broadcasted_iota(jnp.int32, shape, dim)


def kernel(nf, ns, x_hbm, cot_hbm, w_hbm, in_hbm, out_hbm, skip_hbm, dec_hbm,
           dl_ref, pay_out,
           xr, cg, dg, inp, p3, k4, pe, qs, kb, nb, mb, dm, own_d, adj, adj_bf, ab, ab_out, dr, pay, pay_bf, rs, aw, bw,
           halo_s, halo_r, dhalo_s, dhalo_r, dec_s, dec_r, cot_s, cot_r, ab_s, ab_r,
           rs_s, rs_r, ag_s, ag_r,
           x_ref, cot_ref, w_ref, in_ref, out_ref, skip_ref, load):
    F = x_ref.shape[0]
    half = F * 16
    me = lax.axis_index("freq")
    sky = lax.axis_index("sky")
    core = lax.rem(me, 2)
    chip = me // 2
    chips = nf // 2
    sibling = me + 1 - 2 * core
    nxt = lax.rem(sky + 1, ns)
    prv = lax.rem(sky + ns - 1, ns)
    rows = rs.shape[1]
    owners = pay.shape[0] // rows
    here = sky * nf + me
    owner = sky * chips + chip
    owns = jnp.logical_and(core == 1, owner < owners)

    loads = [
        pltpu.make_async_copy(src, dst, load.at[i])
        for i, (src, dst) in enumerate((
            (cot_hbm, cot_ref), (dec_hbm, dg.at[core]), (x_hbm, x_ref), (w_hbm, w_ref),
            (in_hbm, in_ref), (out_hbm, out_ref), (skip_hbm, skip_ref)))
    ]
    for one in loads:
        one.start()
    barrier = pltpu.get_barrier_semaphore()

    def greet(d, carry):
        other = lax.rem(here + d, nf * ns)
        pl.semaphore_signal(barrier, inc=1, device_id={"sky": other // nf, "freq": lax.rem(other, nf)},
                            device_id_type=MESH)
        return carry

    lax.fori_loop(1, nf * ns, greet, 0, unroll=nf * ns <= 16)

    pr, pc = iota((64, 64), 0), iota((64, 64), 1)
    perm = (pc == 2 * lax.rem(pr, 32) + pr // 32).astype(F32).astype(BF)
    loads[0].wait()
    for f in range(F):
        c2 = dot(perm, cot_ref[f]).astype(BF)
        for h in range(2):
            for hi in range(2):
                at = hi * half + f * 16
                cg[core, h, at:at + 16, :] = c2[h * 32 + hi * 16:h * 32 + hi * 16 + 16]
    loads[1].wait()
    pl.semaphore_wait(barrier, nf * ns - 1)

    def remote(src, dst, s, r, **where):
        return pltpu.make_async_remote_copy(
            src_ref=src, dst_ref=dst, send_sem=s, recv_sem=r, device_id=dict(where), device_id_type=MESH)

    first, last = chip == 0, chip == chips - 1

    def dec_copy(slot):
        return remote(dg.at[slot], dg.at[slot], dec_s.at[0], dec_r.at[0], freq=sibling)

    def cot_copy(slot, h):
        return remote(cg.at[slot, h], cg.at[slot, h], cot_s.at[h], cot_r.at[h], freq=sibling)

    def adj_copy():
        return remote(ab_out, ab.at[core], ab_s.at[0], ab_r.at[core], freq=jnp.maximum(me - 2, 0))

    def fwd_copy(slot):
        return remote(ab.at[slot], ab.at[slot], ab_s.at[1], ab_r.at[slot], freq=sibling)

    up = remote(xr.at[:, 64:96], xr.at[:, 0:32], halo_s.at[0], halo_r.at[0], sky=nxt)
    down = remote(xr.at[:, 32:64], xr.at[:, 96:128], halo_s.at[1], halo_r.at[1], sky=prv)
    dec_copy(core).start()

    @pl.when(core == 1)
    def _():
        cot_copy(core, 0).start()
        cot_copy(core, 1).start()

    @pl.when(jnp.logical_and(core == 0, jnp.logical_not(first)))
    def _():
        cot_copy(core, 1).start()

    loads[2].wait()
    for f in range(F):
        xr[f, 32:96, :] = dot(perm, x_ref[f]).astype(BF)
    up.start()
    down.start()
    for i in (3, 4, 5, 6):
        loads[i].wait()

    W = x_ref.shape[2]

    low_row = lax.rem(iota((16, 128), 1), 16) == iota((16, 128), 0)
    low_col = iota((16, 256), 1) // 16 == iota((16, 256), 0)
    expand = low_col.astype(F32).astype(BF)
    r256, l256 = iota((256, 256), 0), iota((256, 256), 1)
    kept = r256 // 16 == lax.rem(l256, 16)

    def group(hi):
        return slice(hi * half, (hi + 1) * half)

    def decayed(to, slot, run):
        for g in range(F):
            run = run * dg[slot, g:g + 1, :]
            qs[g:g + 1, :] = run
        for hi in range(2):
            m = lax.dot_general(qs[:, hi * 256:(hi + 1) * 256].astype(BF), expand, (((0,), (0,)), ((), ())),
                                preferred_element_type=F32)
            mb[to, hi] = jnp.where(kept, m, 0.0).astype(BF)
        return run

    def diagonal(to, run):
        for hi in range(2):
            dm[to, hi] = jnp.where(r256 == l256, run[:, hi * 256:(hi + 1) * 256], 0.0).astype(BF)

    def take():
        fwd_copy(core).wait_recv()
        fwd_copy(core).start()

    dec_copy(1 - core).wait_recv()

    @pl.when(jnp.logical_not(first))
    def _():
        run = decayed(1, 0, jnp.ones((1, 512), F32))
        run = decayed(2, 1, run)
        cot_copy(1 - core, core).wait_recv()
        for hi in range(2):
            adj[0, hi] = dot(mb[1, hi], cg[0, core, group(hi)]) + dot(mb[2, hi], cg[1, core, group(hi)])

        @pl.when(jnp.logical_not(last))
        def _():
            diagonal(1, run)
            take()
            for hi in range(2):
                adj[0, hi] += dot(dm[1, hi], ab[core, hi])

        ab_out[...] = adj[0].astype(BF)
        adj_copy().start()

    @pl.when(last)
    def _():
        ab[...] = jnp.zeros_like(ab)

    spread = (iota((32, 512), 1) // 16 == iota((32, 512), 0)).astype(F32)
    io = jnp.dot(in_ref[...] * out_ref[...], spread, precision=lax.Precision.HIGHEST, preferred_element_type=F32)
    io = jnp.sum(jnp.where(lax.rem(iota((16, 512), 1), 16) == iota((16, 512), 0), io, 0.0), axis=0, keepdims=True)
    tr, tc = iota((32, 256), 0), iota((32, 256), 1)
    skips = jnp.where(tr == tc // 128 * 16 + lax.rem(tc, 16), 1.0, 0.0)
    skips = jnp.dot(skip_ref[...], skips, precision=lax.Precision.HIGHEST, preferred_element_type=F32)
    tr, tc = iota((512, 256), 0), iota((512, 256), 1)
    tile = (tr // 16 == tc // 128 * 16 + lax.rem(tc, 16)).astype(F32).astype(BF)

    fi = iota((F, 512), 0)
    v = jnp.zeros((F, 512), F32)
    for g in range(F):
        v = jnp.where(fi == g, 1.0, v * dg[core, g:g + 1, :])
        p3[g * F:(g + 1) * F, :] = v
    pe[...] = v * io
    kk = dot((p3[...] * io).astype(BF), tile)
    row16, lane16 = iota((F, 256), 0), lax.rem(iota((F, 256), 1), 128) // 16
    for G in range(2):
        k = jnp.where(row16 == lane16 + 8 * G, skips, 0.0)
        for j in range(8):
            at = (8 * G + j) * F
            k = k + jnp.where(lane16 == j, kk[at:at + F], 0.0)
        k4[G * F:(G + 1) * F, :] = k
    for hi in range(2):
        for f in range(F):
            for G in range(2):
                row = jnp.broadcast_to(k4[G * F + f:G * F + f + 1, hi * 128:(hi + 1) * 128], (16, 128))
                kb[hi, f * 16:(f + 1) * 16, G * 128:(G + 1) * 128] = jnp.where(low_row, row, 0.0).astype(BF)
            row = jnp.broadcast_to(pe[f:f + 1, hi * 256:(hi + 1) * 256], (16, 256))
            nb[hi, f * 16:(f + 1) * 16, :] = jnp.where(low_col, row, 0.0).astype(BF)

    def cells(slot, hi):
        return jnp.concatenate([cg[slot, 0, group(hi)], cg[slot, 1, group(hi)]], axis=1)

    for hi in range(2):
        d = dot(kb[hi], cells(core, hi))
        own_d[0, hi] = d[:, 0:128]
        own_d[1, hi] = d[:, 128:256]

    @pl.when(core == 0)
    def _():
        diagonal(0, decayed(0, 1, jnp.ones((1, 512), F32)))
        pl.when(first)(cot_copy(1, 0).wait_recv)
        cot_copy(1, 1).wait_recv()
        for hi in range(2):
            a = dot(mb[0, hi], cells(1, hi))
            adj[0, hi] = a[:, 0:128]
            adj[1, hi] = a[:, 128:256]

    kk, ll = iota((288, 384), 0), iota((288, 384), 1)
    for r in range(2):
        tap = lax.rem(ll, 128) // 32 - r
        pick = jnp.logical_and(kk == (tap * 3 + ll // 128) * 32 + lax.rem(ll, 32),
                               jnp.logical_and(tap >= 0, tap <= 2))
        aw[r * 32:(r + 1) * 32, :] = dot(w_ref[...], pick.astype(F32).astype(BF)).astype(BF)
    mm, kk = iota((64, 288), 0), iota((64, 288), 1)
    for k in range(3):
        for row in range(4):
            tap = lax.rem(mm, 2) + 2 - row
            pick = jnp.logical_and(kk == (tap * 3 + k) * 32 + mm // 2,
                                   jnp.logical_and(tap >= 0, tap <= 2))
            at = k * 128 + row * 32
            bw[:, at:at + 32] = dot_nt(pick.astype(F32).astype(BF), w_ref[...])

    dup = remote(dr.at[:, 64:96], dr.at[:, 0:32], dhalo_s.at[1], dhalo_r.at[1], sky=nxt)
    ddown = remote(dr.at[:, 32:64], dr.at[:, 96:128], dhalo_s.at[0], dhalo_r.at[0], sky=prv)

    def mix(h):
        @pl.when(core == 0)
        def _():
            for hi in range(2):
                adj_bf[h, hi] = (adj[h, hi] + dot(dm[0, hi], ab[h, hi])).astype(BF)

        @pl.when(core == 1)
        def _():
            adj_bf[h] = ab[h]

        for hi in range(2):
            d = (own_d[h, hi] + dot(nb[hi], adj_bf[h, hi])).astype(BF)
            at = pl.multiple_of(32 + 32 * h + 16 * hi, 16)
            for f in range(F):
                dr[f, pl.ds(at, 16), :] = d[f * 16:(f + 1) * 16]

    pl.when(first)(take)
    mix(core)
    pl.when(core == 0)(ddown.start)
    pl.when(core == 1)(dup.start)
    up.wait_recv()
    down.wait_recv()
    for f in range(F):
        x = xr[f]
        full = jnp.concatenate([pltpu.roll(x, 1, 1), x, pltpu.roll(x, W - 1, 1)], axis=0)
        got = dot(aw[...], full).astype(BF)
        for r in range(2):
            for hi in range(2):
                inp[hi, f * 16:(f + 1) * 16, r * 128:(r + 1) * 128] = got[r * 32 + hi * 16:r * 32 + hi * 16 + 16]

    same = lax.rem(r256, 16) == lax.rem(l256, 16)
    widen = (lax.rem(r256, 16) == l256 // 16).astype(F32).astype(BF)
    now = r256 // 16 == lax.rem(r256, 16)
    block_of = l256[0:16] // 16
    sums = []
    for hi in range(2):
        gram = jnp.where(same, dot_nt(inp[hi], cells(core, hi)), 0.0).astype(BF)
        rows_f = dot(expand, gram)
        stack = jnp.concatenate([jnp.where(block_of == g, rows_f, 0.0) for g in range(F)], axis=0).astype(BF)
        pairs = dot(stack, widen)
        sums.append(jnp.sum((pairs * p3[:, hi * 256:(hi + 1) * 256]).reshape(F * F // 8, 8, 256), axis=0))
        skip = jnp.sum(jnp.where(now, pairs, 0.0), axis=0, keepdims=True)
        for k in range(2):
            pay[100 + 2 * hi + k:101 + 2 * hi + k, :] = skip[:, k * 128:(k + 1) * 128]
    pl.when(jnp.logical_not(last))(fwd_copy(1 - core).wait_recv)
    mix(1 - core)
    for hi in range(2):
        gram = dot_nt(inp[hi], jnp.concatenate([adj_bf[0, hi], adj_bf[1, hi]], axis=1))
        total = sums[hi]
        for f in range(F):
            rows_f = jnp.where(low_col, gram[f * 16:(f + 1) * 16], 0.0)
            at = (F - 1) * F + f
            total = total + (rows_f[0:8] + rows_f[8:16]) * p3[at:at + 1, hi * 256:(hi + 1) * 256]
        t = jnp.sum(total, axis=0, keepdims=True)
        for k in range(2):
            pay[96 + 2 * hi + k:97 + 2 * hi + k, :] = t[:, k * 128:(k + 1) * 128]

    grad = jnp.zeros((192, 128), F32)
    for f in range(F):
        mid = dr[f, 32:96, :]
        full = jnp.concatenate([pltpu.roll(mid, W - 1, 1), mid, pltpu.roll(mid, 1, 1)], axis=0)
        grad = grad + dot_nt(full, xr[f])
    for k in range(3):
        top = grad[k * 64:k * 64 + 32, 0:96]
        low = grad[k * 64 + 32:k * 64 + 64, 32:128]
        pay[k * 32:(k + 1) * 32, 0:96] = top + low
        pay[k * 32:(k + 1) * 32, 96:128] = jnp.zeros((32, 32), F32)

    def part(ref, i):
        return ref.at[pl.ds(pl.multiple_of(i * rows, 16), rows)]

    def each_owner(do):
        def step(d, carry):
            i = lax.rem(owner + d, owners)

            @pl.when(jnp.logical_not(jnp.logical_and(owns, i == owner)))
            def _():
                do(remote(part(pay_bf, i), rs.at[here], rs_s.at[0], rs_r.at[0],
                          sky=i // chips, freq=lax.rem(i, chips) * 2 + 1))

            return carry

        lax.fori_loop(0, owners, step, 0, unroll=owners <= 8)

    def each_other(do):
        def step(d, carry):
            other = lax.rem(here + d, nf * ns)
            do(remote(part(pay_out, owner), part(pay_out, owner), ag_s.at[0], ag_r.at[0],
                      sky=other // nf, freq=lax.rem(other, nf)))
            return carry

        lax.fori_loop(1, nf * ns, step, 0, unroll=nf * ns <= 16)

    pay_bf[0:96, :] = pay[0:96, :].astype(BF)
    small = pay[96:104, :]
    high = small.astype(BF).astype(F32)
    pay_bf[96:112, :] = jnp.concatenate([high, small - high], axis=0).astype(BF)
    pay_bf[112:128, :] = jnp.zeros((16, 128), BF)
    each_owner(lambda one: one.start())
    pl.when(core == 0)(dup.start)
    pl.when(core == 1)(ddown.start)
    @pl.when(owns)
    def _():
        at = pl.ds(pl.multiple_of(owner * rows, 16), rows)
        rs[here] = pay_bf[at, :]
        some = rs.at[0:nf * ns - 1]
        pltpu.make_async_copy(some, some, rs_r.at[0]).wait()
        total = jnp.sum(rs[...].astype(F32), axis=0)
        small = total[0:8] + total[8:16]
        high = small.astype(BF).astype(F32)
        pair = jnp.concatenate([high, small - high], axis=0)
        pay_out[at, :] = jnp.where(owner * rows == 96, pair, total).astype(BF)
        each_other(lambda one: one.start())

    dup.wait_recv()
    ddown.wait_recv()
    b = bw[...].astype(BF)
    for f in range(F):
        x = dr[f]
        full = jnp.concatenate([pltpu.roll(x, W - 1, 1), x, pltpu.roll(x, 1, 1)], axis=0)
        dl_ref[f] = dot(b, full).astype(BF)

    up.wait_send()
    down.wait_send()
    dup.wait_send()
    ddown.wait_send()
    dec_copy(core).wait_send()

    @pl.when(core == 1)
    def _():
        cot_copy(core, 0).wait_send()
        cot_copy(core, 1).wait_send()

    @pl.when(jnp.logical_and(core == 0, jnp.logical_not(first)))
    def _():
        cot_copy(core, 1).wait_send()

    pl.when(jnp.logical_not(first))(adj_copy().wait_send)
    pl.when(jnp.logical_not(last))(fwd_copy(core).wait_send)

    @pl.when(owns)
    def _():
        sent = pay_bf.at[0:128 - rows]
        pltpu.make_async_copy(sent, sent, rs_s.at[0]).wait()

    @pl.when(jnp.logical_not(owns))
    def _():
        pltpu.make_async_copy(pay_bf, pay_bf, rs_s.at[0]).wait()

    @pl.when(owns)
    def _():
        rest = pay_out.at[0:128 - rows]
        pltpu.make_async_copy(rest, rest, ag_r.at[0]).wait()

    @pl.when(jnp.logical_not(owns))
    def _():
        pltpu.make_async_copy(pay_out, pay_out, ag_r.at[0]).wait()

    @pl.when(owns)
    def _():
        sent = rs.at[0:nf * ns - 1]
        pltpu.make_async_copy(sent, sent, ag_s.at[0]).wait()


def finish(scale, dl_ref, pay_ref, in_ref, out_ref, dl_hbm, conv_hbm, din_hbm, dout_hbm, skip_hbm,
           conv_out, din_out, dout_out, skip_out, pay, sems):
    copies = [
        pltpu.make_async_copy(src, dst, sems.at[i])
        for i, (src, dst) in enumerate((
            (dl_ref, dl_hbm), (conv_out, conv_hbm), (din_out, din_hbm), (dout_out, dout_hbm), (skip_out, skip_hbm)))
    ]
    copies[0].start()
    pay[...] = pay_ref[...].astype(F32)
    pay[96:104, :] += pay[104:112, :]
    for dr in range(3):
        for k in range(3):
            at = (dr * 3 + k) * 32
            conv_out[:, at:at + 32] = pay[k * 32:(k + 1) * 32, dr * 32:(dr + 1) * 32] * scale
    copies[1].start()
    t = jnp.concatenate([pay[96 + k:97 + k, :] for k in range(4)], axis=1) * scale
    t = jnp.where(lax.rem(iota((16, 512), 1), 16) == iota((16, 512), 0), t, 0.0)
    join = (iota((512, 32), 0) // 16 == iota((512, 32), 1)).astype(F32)
    t = jnp.dot(t, join, precision=lax.Precision.HIGHEST, preferred_element_type=F32)
    din_out[...] = t * out_ref[...]
    dout_out[...] = t * in_ref[...]
    s = jnp.concatenate([pay[100 + k:101 + k, :] for k in range(4)], axis=1) * scale
    s = jnp.where(lax.rem(iota((1, 512), 1), 16) == 0, s, 0.0)
    skip_out[...] = jnp.dot(s, join, precision=lax.Precision.HIGHEST, preferred_element_type=F32)
    for one in copies[2:]:
        one.start()
    for one in copies:
        one.wait()


def in_hbm(x):
    return pltpu.with_memory_space_constraint(x, pltpu.MemorySpace.HBM)


def per_device(lightcone, cotangent, conv_weight, in_proj, out_proj, skip_gain, decay):
    F, C, R, W = lightcone.shape
    N = in_proj.shape[1]
    nf, ns = lax.axis_size("freq"), lax.axis_size("sky")
    scale = 1.0 / float(F * nf * R * ns * W) ** 0.5
    owners = min(nf // 2 * ns, 8)
    dma = pltpu.SemaphoreType.DMA
    vm = pl.BlockSpec(memory_space=pltpu.VMEM)
    hbm = pl.BlockSpec(memory_space=pltpu.MemorySpace.HBM)
    dl, pay = pl.pallas_call(
        functools.partial(kernel, nf, ns),
        out_shape=(
            jax.ShapeDtypeStruct((F, C * R, W), BF),
            jax.ShapeDtypeStruct((128, 128), BF),
        ),
        in_specs=[hbm] * 7,
        out_specs=(vm, vm),
        scratch_shapes=[
            pltpu.VMEM((F, 4 * C, W), BF),
            pltpu.VMEM((2, R, F * C, W), BF),
            pltpu.VMEM((2, F, C * N), F32),
            pltpu.VMEM((2, F * 16, R * W), BF),
            pltpu.VMEM((F * F, C * N), F32),
            pltpu.VMEM((2 * F, 256), F32),
            pltpu.VMEM((F, C * N), F32),
            pltpu.VMEM((F, C * N), F32),
            pltpu.VMEM((2, F * 16, F * 16), BF),
            pltpu.VMEM((2, F * 16, 16 * N), BF),
            pltpu.VMEM((3, 2, 16 * N, F * 16), BF),
            pltpu.VMEM((2, 2, 16 * N, 16 * N), BF),
            pltpu.VMEM((R, 2, F * 16, W), F32),
            pltpu.VMEM((R, 2, 16 * N, W), F32),
            pltpu.VMEM((R, 2, 16 * N, W), BF),
            pltpu.VMEM((R, 2, 16 * N, W), BF),
            pltpu.VMEM((2, 16 * N, W), BF),
            pltpu.VMEM((F, 4 * C, W), BF),
            pltpu.VMEM((128, 128), F32),
            pltpu.VMEM((128, 128), BF),
            pltpu.VMEM((nf * ns, 128 // owners, 128), BF),
            pltpu.VMEM((2 * C, 12 * C), BF),
            pltpu.VMEM((2 * C, 12 * C), F32),
            dma((2,)), dma((2,)), dma((2,)), dma((2,)),
            dma((1,)), dma((1,)), dma((2,)), dma((2,)), dma((2,)), dma((2,)),
            dma((1,)), dma((1,)), dma((1,)), dma((1,)),
            pltpu.VMEM((F, C * R, W), BF),
            pltpu.VMEM((F, C * R, W), BF),
            pltpu.VMEM((C, 9 * C), BF),
            pltpu.VMEM((N, C), F32),
            pltpu.VMEM((N, C), F32),
            pltpu.VMEM((1, C), F32),
            dma((7,)),
        ],
        compiler_params=pltpu.CompilerParams(
            collective_id=0, has_side_effects=True, vmem_limit_bytes=16 << 20),
    )(*map(in_hbm, (lightcone.reshape(F, C * R, W), cotangent.reshape(F, C * R, W), conv_weight,
                    in_proj.T, out_proj.T, skip_gain.reshape(1, C), decay)))
    dl, grad, din, dout, d_skip = pl.pallas_call(
        functools.partial(finish, scale),
        out_shape=(
            jax.ShapeDtypeStruct((F, C * R, W), BF),
            jax.ShapeDtypeStruct((C, 9 * C), F32),
            jax.ShapeDtypeStruct((N, C), F32),
            jax.ShapeDtypeStruct((N, C), F32),
            jax.ShapeDtypeStruct((1, C), F32),
        ),
        in_specs=[vm] * 4,
        out_specs=(hbm,) * 5,
        scratch_shapes=[
            pltpu.VMEM((C, 9 * C), F32), pltpu.VMEM((N, C), F32), pltpu.VMEM((N, C), F32),
            pltpu.VMEM((1, C), F32), pltpu.VMEM((128, 128), F32), dma((5,))],
        compiler_params=pltpu.CompilerParams(vmem_limit_bytes=8 << 20),
    )(dl, pay, in_proj.T, out_proj.T)
    return dl.reshape(F, C, R, W), grad, din.T, dout.T, d_skip.reshape(C)


def solution(mesh):
    return jax.shard_map(
        per_device,
        mesh=mesh,
        in_specs=(
            P(("replica", "freq"), None, "sky", None),
            P(("replica", "freq"), None, "sky", None),
            P(),
            P(),
            P(),
            P(),
            P("freq", None),
        ),
        out_specs=(
            P(("replica", "freq"), None, "sky", None),
            P("replica", None),
            P("replica", None),
            P("replica", None),
            P("replica"),
        ),
        check_vma=False,
    )
```

```python
import functools

import jax
import jax.numpy as jnp
from jax import lax
from jax.experimental import pallas as pl
from jax.experimental.pallas import tpu as pltpu
from jax.sharding import PartitionSpec as P

MESH = pl.DeviceIdType.MESH
BF = jnp.bfloat16
F32 = jnp.float32


def dot(a, b):
    return jnp.dot(a, b, preferred_element_type=F32)


def dot_nt(a, b):
    return lax.dot_general(a, b, (((1,), (1,)), ((), ())), preferred_element_type=F32)


def iota(shape, dim):
    return lax.broadcasted_iota(jnp.int32, shape, dim)


def kernel(nf, ns, x_hbm, cot_hbm, w_hbm, in_hbm, out_hbm, skip_hbm, dec_hbm,
           dl_ref, pay_out,
           xr, cg, dg, inp, p3, k4, pe, qs, kb, nb, mb, dm, own_d, adj, adj_bf, ab, ab_out, dr, pay, pay_bf, rs, aw, bw,
           halo_s, halo_r, dhalo_s, dhalo_r, dec_s, dec_r, cot_s, cot_r, ab_s, ab_r,
           rs_s, rs_r, ag_s, ag_r, relay,
           x_ref, cot_ref, w_ref, in_ref, out_ref, skip_ref, load):
    F = x_ref.shape[0]
    half = F * 16
    me = lax.axis_index("freq")
    sky = lax.axis_index("sky")
    core = lax.rem(me, 2)
    chip = me // 2
    chips = nf // 2
    sibling = me + 1 - 2 * core
    nxt = lax.rem(sky + 1, ns)
    prv = lax.rem(sky + ns - 1, ns)
    rows = rs.shape[1]
    owners = pay.shape[0] // rows
    here = sky * nf + me
    owner = sky * chips + chip
    owns = jnp.logical_and(core == 1, owner < owners)

    loads = [
        pltpu.make_async_copy(src, dst, load.at[i])
        for i, (src, dst) in enumerate((
            (cot_hbm, cot_ref), (dec_hbm, dg.at[core]), (x_hbm, x_ref), (w_hbm, w_ref),
            (in_hbm, in_ref), (out_hbm, out_ref), (skip_hbm, skip_ref)))
    ]
    for one in loads:
        one.start()
    barrier = pltpu.get_barrier_semaphore()
    for d in range(1, nf):
        pl.semaphore_signal(barrier, inc=1, device_id={"freq": lax.rem(me + d, nf)}, device_id_type=MESH)
    for to in (nxt, prv):
        pl.semaphore_signal(barrier, inc=1, device_id={"sky": to}, device_id_type=MESH)

    def pass_on(stage):
        for to in (nxt, prv):
            pl.semaphore_signal(relay.at[stage], inc=1, device_id={"sky": to}, device_id_type=MESH)

    stages = ns // 2

    pr, pc = iota((64, 64), 0), iota((64, 64), 1)
    perm = (pc == 2 * lax.rem(pr, 32) + pr // 32).astype(F32).astype(BF)
    loads[0].wait()
    for f in range(F):
        c2 = dot(perm, cot_ref[f]).astype(BF)
        for h in range(2):
            for hi in range(2):
                at = hi * half + f * 16
                cg[core, h, at:at + 16, :] = c2[h * 32 + hi * 16:h * 32 + hi * 16 + 16]
    loads[1].wait()
    pl.semaphore_wait(barrier, nf - 1 + 2)

    def remote(src, dst, s, r, **where):
        return pltpu.make_async_remote_copy(
            src_ref=src, dst_ref=dst, send_sem=s, recv_sem=r, device_id=dict(where), device_id_type=MESH)

    first, last = chip == 0, chip == chips - 1

    def dec_copy(slot):
        return remote(dg.at[slot], dg.at[slot], dec_s.at[0], dec_r.at[0], freq=sibling)

    def cot_copy(slot, h):
        return remote(cg.at[slot, h], cg.at[slot, h], cot_s.at[h], cot_r.at[h], freq=sibling)

    def adj_copy():
        return remote(ab_out, ab.at[core], ab_s.at[0], ab_r.at[core], freq=jnp.maximum(me - 2, 0))

    def fwd_copy(slot):
        return remote(ab.at[slot], ab.at[slot], ab_s.at[1], ab_r.at[slot], freq=sibling)

    up = remote(xr.at[:, 64:96], xr.at[:, 0:32], halo_s.at[0], halo_r.at[0], sky=nxt)
    down = remote(xr.at[:, 32:64], xr.at[:, 96:128], halo_s.at[1], halo_r.at[1], sky=prv)
    dec_copy(core).start()

    @pl.when(core == 1)
    def _():
        cot_copy(core, 0).start()
        cot_copy(core, 1).start()

    @pl.when(jnp.logical_and(core == 0, jnp.logical_not(first)))
    def _():
        cot_copy(core, 1).start()

    pass_on(0)
    loads[2].wait()
    for f in range(F):
        xr[f, 32:96, :] = dot(perm, x_ref[f]).astype(BF)
    up.start()
    down.start()
    for i in (3, 4, 5, 6):
        loads[i].wait()

    W = x_ref.shape[2]

    low_row = lax.rem(iota((16, 128), 1), 16) == iota((16, 128), 0)
    low_col = iota((16, 256), 1) // 16 == iota((16, 256), 0)
    expand = low_col.astype(F32).astype(BF)
    r256, l256 = iota((256, 256), 0), iota((256, 256), 1)
    kept = r256 // 16 == lax.rem(l256, 16)

    def group(hi):
        return slice(hi * half, (hi + 1) * half)

    def decayed(to, slot, run):
        for g in range(F):
            run = run * dg[slot, g:g + 1, :]
            qs[g:g + 1, :] = run
        for hi in range(2):
            m = lax.dot_general(qs[:, hi * 256:(hi + 1) * 256].astype(BF), expand, (((0,), (0,)), ((), ())),
                                preferred_element_type=F32)
            mb[to, hi] = jnp.where(kept, m, 0.0).astype(BF)
        return run

    def diagonal(to, run):
        for hi in range(2):
            dm[to, hi] = jnp.where(r256 == l256, run[:, hi * 256:(hi + 1) * 256], 0.0).astype(BF)

    def take():
        fwd_copy(core).wait_recv()
        fwd_copy(core).start()

    dec_copy(1 - core).wait_recv()

    @pl.when(jnp.logical_not(first))
    def _():
        run = decayed(1, 0, jnp.ones((1, 512), F32))
        run = decayed(2, 1, run)
        cot_copy(1 - core, core).wait_recv()
        for hi in range(2):
            adj[0, hi] = dot(mb[1, hi], cg[0, core, group(hi)]) + dot(mb[2, hi], cg[1, core, group(hi)])

        @pl.when(jnp.logical_not(last))
        def _():
            diagonal(1, run)
            take()
            for hi in range(2):
                adj[0, hi] += dot(dm[1, hi], ab[core, hi])

        ab_out[...] = adj[0].astype(BF)
        adj_copy().start()

    @pl.when(last)
    def _():
        ab[...] = jnp.zeros_like(ab)

    spread = (iota((32, 512), 1) // 16 == iota((32, 512), 0)).astype(F32)
    io = jnp.dot(in_ref[...] * out_ref[...], spread, precision=lax.Precision.HIGHEST, preferred_element_type=F32)
    io = jnp.sum(jnp.where(lax.rem(iota((16, 512), 1), 16) == iota((16, 512), 0), io, 0.0), axis=0, keepdims=True)
    tr, tc = iota((32, 256), 0), iota((32, 256), 1)
    skips = jnp.where(tr == tc // 128 * 16 + lax.rem(tc, 16), 1.0, 0.0)
    skips = jnp.dot(skip_ref[...], skips, precision=lax.Precision.HIGHEST, preferred_element_type=F32)
    tr, tc = iota((512, 256), 0), iota((512, 256), 1)
    tile = (tr // 16 == tc // 128 * 16 + lax.rem(tc, 16)).astype(F32).astype(BF)

    fi = iota((F, 512), 0)
    v = jnp.zeros((F, 512), F32)
    for g in range(F):
        v = jnp.where(fi == g, 1.0, v * dg[core, g:g + 1, :])
        p3[g * F:(g + 1) * F, :] = v
    pe[...] = v * io
    kk = dot((p3[...] * io).astype(BF), tile)
    row16, lane16 = iota((F, 256), 0), lax.rem(iota((F, 256), 1), 128) // 16
    for G in range(2):
        k = jnp.where(row16 == lane16 + 8 * G, skips, 0.0)
        for j in range(8):
            at = (8 * G + j) * F
            k = k + jnp.where(lane16 == j, kk[at:at + F], 0.0)
        k4[G * F:(G + 1) * F, :] = k
    for hi in range(2):
        for f in range(F):
            for G in range(2):
                row = jnp.broadcast_to(k4[G * F + f:G * F + f + 1, hi * 128:(hi + 1) * 128], (16, 128))
                kb[hi, f * 16:(f + 1) * 16, G * 128:(G + 1) * 128] = jnp.where(low_row, row, 0.0).astype(BF)
            row = jnp.broadcast_to(pe[f:f + 1, hi * 256:(hi + 1) * 256], (16, 256))
            nb[hi, f * 16:(f + 1) * 16, :] = jnp.where(low_col, row, 0.0).astype(BF)

    def cells(slot, hi):
        return jnp.concatenate([cg[slot, 0, group(hi)], cg[slot, 1, group(hi)]], axis=1)

    for hi in range(2):
        d = dot(kb[hi], cells(core, hi))
        own_d[0, hi] = d[:, 0:128]
        own_d[1, hi] = d[:, 128:256]

    @pl.when(core == 0)
    def _():
        diagonal(0, decayed(0, 1, jnp.ones((1, 512), F32)))
        pl.when(first)(cot_copy(1, 0).wait_recv)
        cot_copy(1, 1).wait_recv()
        for hi in range(2):
            a = dot(mb[0, hi], cells(1, hi))
            adj[0, hi] = a[:, 0:128]
            adj[1, hi] = a[:, 128:256]

    kk, ll = iota((288, 384), 0), iota((288, 384), 1)
    for r in range(2):
        tap = lax.rem(ll, 128) // 32 - r
        pick = jnp.logical_and(kk == (tap * 3 + ll // 128) * 32 + lax.rem(ll, 32),
                               jnp.logical_and(tap >= 0, tap <= 2))
        aw[r * 32:(r + 1) * 32, :] = dot(w_ref[...], pick.astype(F32).astype(BF)).astype(BF)
    mm, kk = iota((64, 288), 0), iota((64, 288), 1)
    for k in range(3):
        for row in range(4):
            tap = lax.rem(mm, 2) + 2 - row
            pick = jnp.logical_and(kk == (tap * 3 + k) * 32 + mm // 2,
                                   jnp.logical_and(tap >= 0, tap <= 2))
            at = k * 128 + row * 32
            bw[:, at:at + 32] = dot_nt(pick.astype(F32).astype(BF), w_ref[...])

    dup = remote(dr.at[:, 64:96], dr.at[:, 0:32], dhalo_s.at[1], dhalo_r.at[1], sky=nxt)
    ddown = remote(dr.at[:, 32:64], dr.at[:, 96:128], dhalo_s.at[0], dhalo_r.at[0], sky=prv)

    def mix(h):
        @pl.when(core == 0)
        def _():
            for hi in range(2):
                adj_bf[h, hi] = (adj[h, hi] + dot(dm[0, hi], ab[h, hi])).astype(BF)

        @pl.when(core == 1)
        def _():
            adj_bf[h] = ab[h]

        for hi in range(2):
            d = (own_d[h, hi] + dot(nb[hi], adj_bf[h, hi])).astype(BF)
            at = pl.multiple_of(32 + 32 * h + 16 * hi, 16)
            for f in range(F):
                dr[f, pl.ds(at, 16), :] = d[f * 16:(f + 1) * 16]

    for stage in range(1, stages):
        pl.semaphore_wait(relay.at[stage - 1], 2)
        pass_on(stage)

    pl.when(first)(take)
    mix(core)
    pl.when(core == 0)(ddown.start)
    pl.when(core == 1)(dup.start)
    up.wait_recv()
    down.wait_recv()
    for f in range(F):
        x = xr[f]
        full = jnp.concatenate([pltpu.roll(x, 1, 1), x, pltpu.roll(x, W - 1, 1)], axis=0)
        got = dot(aw[...], full).astype(BF)
        for r in range(2):
            for hi in range(2):
                inp[hi, f * 16:(f + 1) * 16, r * 128:(r + 1) * 128] = got[r * 32 + hi * 16:r * 32 + hi * 16 + 16]

    same = lax.rem(r256, 16) == lax.rem(l256, 16)
    widen = (lax.rem(r256, 16) == l256 // 16).astype(F32).astype(BF)
    now = r256 // 16 == lax.rem(r256, 16)
    block_of = l256[0:16] // 16
    sums = []
    for hi in range(2):
        gram = jnp.where(same, dot_nt(inp[hi], cells(core, hi)), 0.0).astype(BF)
        rows_f = dot(expand, gram)
        stack = jnp.concatenate([jnp.where(block_of == g, rows_f, 0.0) for g in range(F)], axis=0).astype(BF)
        pairs = dot(stack, widen)
        sums.append(jnp.sum((pairs * p3[:, hi * 256:(hi + 1) * 256]).reshape(F * F // 8, 8, 256), axis=0))
        skip = jnp.sum(jnp.where(now, pairs, 0.0), axis=0, keepdims=True)
        for k in range(2):
            pay[100 + 2 * hi + k:101 + 2 * hi + k, :] = skip[:, k * 128:(k + 1) * 128]
    pl.when(jnp.logical_not(last))(fwd_copy(1 - core).wait_recv)
    mix(1 - core)
    for hi in range(2):
        gram = dot_nt(inp[hi], jnp.concatenate([adj_bf[0, hi], adj_bf[1, hi]], axis=1))
        total = sums[hi]
        for f in range(F):
            rows_f = jnp.where(low_col, gram[f * 16:(f + 1) * 16], 0.0)
            at = (F - 1) * F + f
            total = total + (rows_f[0:8] + rows_f[8:16]) * p3[at:at + 1, hi * 256:(hi + 1) * 256]
        t = jnp.sum(total, axis=0, keepdims=True)
        for k in range(2):
            pay[96 + 2 * hi + k:97 + 2 * hi + k, :] = t[:, k * 128:(k + 1) * 128]

    grad = jnp.zeros((192, 128), F32)
    for f in range(F):
        mid = dr[f, 32:96, :]
        full = jnp.concatenate([pltpu.roll(mid, W - 1, 1), mid, pltpu.roll(mid, 1, 1)], axis=0)
        grad = grad + dot_nt(full, xr[f])
    for k in range(3):
        top = grad[k * 64:k * 64 + 32, 0:96]
        low = grad[k * 64 + 32:k * 64 + 64, 32:128]
        pay[k * 32:(k + 1) * 32, 0:96] = top + low
        pay[k * 32:(k + 1) * 32, 96:128] = jnp.zeros((32, 32), F32)

    def part(ref, i):
        return ref.at[pl.ds(pl.multiple_of(i * rows, 16), rows)]

    def each_owner(do):
        def step(d, carry):
            i = lax.rem(owner + d, owners)

            @pl.when(jnp.logical_not(jnp.logical_and(owns, i == owner)))
            def _():
                do(remote(part(pay_bf, i), rs.at[here], rs_s.at[0], rs_r.at[0],
                          sky=i // chips, freq=lax.rem(i, chips) * 2 + 1))

            return carry

        lax.fori_loop(0, owners, step, 0, unroll=owners <= 8)

    def each_other(do):
        def step(d, carry):
            other = lax.rem(here + d, nf * ns)
            do(remote(part(pay_out, owner), part(pay_out, owner), ag_s.at[0], ag_r.at[0],
                      sky=other // nf, freq=lax.rem(other, nf)))
            return carry

        lax.fori_loop(1, nf * ns, step, 0, unroll=nf * ns <= 16)

    pay_bf[0:96, :] = pay[0:96, :].astype(BF)
    small = pay[96:104, :]
    high = small.astype(BF).astype(F32)
    pay_bf[96:112, :] = jnp.concatenate([high, small - high], axis=0).astype(BF)
    pay_bf[112:128, :] = jnp.zeros((16, 128), BF)
    pl.semaphore_wait(relay.at[stages - 1], 2)
    each_owner(lambda one: one.start())
    pl.when(core == 0)(dup.start)
    pl.when(core == 1)(ddown.start)
    @pl.when(owns)
    def _():
        at = pl.ds(pl.multiple_of(owner * rows, 16), rows)
        rs[here] = pay_bf[at, :]
        some = rs.at[0:nf * ns - 1]
        pltpu.make_async_copy(some, some, rs_r.at[0]).wait()
        total = jnp.sum(rs[...].astype(F32), axis=0)
        small = total[0:8] + total[8:16]
        high = small.astype(BF).astype(F32)
        pair = jnp.concatenate([high, small - high], axis=0)
        pay_out[at, :] = jnp.where(owner * rows == 96, pair, total).astype(BF)
        each_other(lambda one: one.start())

    dup.wait_recv()
    ddown.wait_recv()
    b = bw[...].astype(BF)
    for f in range(F):
        x = dr[f]
        full = jnp.concatenate([pltpu.roll(x, W - 1, 1), x, pltpu.roll(x, 1, 1)], axis=0)
        dl_ref[f] = dot(b, full).astype(BF)

    up.wait_send()
    down.wait_send()
    dup.wait_send()
    ddown.wait_send()
    dec_copy(core).wait_send()

    @pl.when(core == 1)
    def _():
        cot_copy(core, 0).wait_send()
        cot_copy(core, 1).wait_send()

    @pl.when(jnp.logical_and(core == 0, jnp.logical_not(first)))
    def _():
        cot_copy(core, 1).wait_send()

    pl.when(jnp.logical_not(first))(adj_copy().wait_send)
    pl.when(jnp.logical_not(last))(fwd_copy(core).wait_send)

    @pl.when(owns)
    def _():
        sent = pay_bf.at[0:128 - rows]
        pltpu.make_async_copy(sent, sent, rs_s.at[0]).wait()

    @pl.when(jnp.logical_not(owns))
    def _():
        pltpu.make_async_copy(pay_bf, pay_bf, rs_s.at[0]).wait()

    @pl.when(owns)
    def _():
        rest = pay_out.at[0:128 - rows]
        pltpu.make_async_copy(rest, rest, ag_r.at[0]).wait()

    @pl.when(jnp.logical_not(owns))
    def _():
        pltpu.make_async_copy(pay_out, pay_out, ag_r.at[0]).wait()

    @pl.when(owns)
    def _():
        sent = rs.at[0:nf * ns - 1]
        pltpu.make_async_copy(sent, sent, ag_s.at[0]).wait()


def finish(scale, dl_ref, pay_ref, in_ref, out_ref, dl_hbm, conv_hbm, din_hbm, dout_hbm, skip_hbm,
           conv_out, din_out, dout_out, skip_out, pay, sems):
    copies = [
        pltpu.make_async_copy(src, dst, sems.at[i])
        for i, (src, dst) in enumerate((
            (dl_ref, dl_hbm), (conv_out, conv_hbm), (din_out, din_hbm), (dout_out, dout_hbm), (skip_out, skip_hbm)))
    ]
    copies[0].start()
    pay[...] = pay_ref[...].astype(F32)
    pay[96:104, :] += pay[104:112, :]
    for dr in range(3):
        for k in range(3):
            at = (dr * 3 + k) * 32
            conv_out[:, at:at + 32] = pay[k * 32:(k + 1) * 32, dr * 32:(dr + 1) * 32] * scale
    copies[1].start()
    t = jnp.concatenate([pay[96 + k:97 + k, :] for k in range(4)], axis=1) * scale
    t = jnp.where(lax.rem(iota((16, 512), 1), 16) == iota((16, 512), 0), t, 0.0)
    join = (iota((512, 32), 0) // 16 == iota((512, 32), 1)).astype(F32)
    t = jnp.dot(t, join, precision=lax.Precision.HIGHEST, preferred_element_type=F32)
    din_out[...] = t * out_ref[...]
    dout_out[...] = t * in_ref[...]
    s = jnp.concatenate([pay[100 + k:101 + k, :] for k in range(4)], axis=1) * scale
    s = jnp.where(lax.rem(iota((1, 512), 1), 16) == 0, s, 0.0)
    skip_out[...] = jnp.dot(s, join, precision=lax.Precision.HIGHEST, preferred_element_type=F32)
    for one in copies[2:]:
        one.start()
    for one in copies:
        one.wait()


def in_hbm(x):
    return pltpu.with_memory_space_constraint(x, pltpu.MemorySpace.HBM)


def per_device(lightcone, cotangent, conv_weight, in_proj, out_proj, skip_gain, decay):
    F, C, R, W = lightcone.shape
    N = in_proj.shape[1]
    nf, ns = lax.axis_size("freq"), lax.axis_size("sky")
    scale = 1.0 / float(F * nf * R * ns * W) ** 0.5
    owners = min(nf // 2 * ns, 8)
    dma = pltpu.SemaphoreType.DMA
    vm = pl.BlockSpec(memory_space=pltpu.VMEM)
    hbm = pl.BlockSpec(memory_space=pltpu.MemorySpace.HBM)
    dl, pay = pl.pallas_call(
        functools.partial(kernel, nf, ns),
        out_shape=(
            jax.ShapeDtypeStruct((F, C * R, W), BF),
            jax.ShapeDtypeStruct((128, 128), BF),
        ),
        in_specs=[hbm] * 7,
        out_specs=(vm, vm),
        scratch_shapes=[
            pltpu.VMEM((F, 4 * C, W), BF),
            pltpu.VMEM((2, R, F * C, W), BF),
            pltpu.VMEM((2, F, C * N), F32),
            pltpu.VMEM((2, F * 16, R * W), BF),
            pltpu.VMEM((F * F, C * N), F32),
            pltpu.VMEM((2 * F, 256), F32),
            pltpu.VMEM((F, C * N), F32),
            pltpu.VMEM((F, C * N), F32),
            pltpu.VMEM((2, F * 16, F * 16), BF),
            pltpu.VMEM((2, F * 16, 16 * N), BF),
            pltpu.VMEM((3, 2, 16 * N, F * 16), BF),
            pltpu.VMEM((2, 2, 16 * N, 16 * N), BF),
            pltpu.VMEM((R, 2, F * 16, W), F32),
            pltpu.VMEM((R, 2, 16 * N, W), F32),
            pltpu.VMEM((R, 2, 16 * N, W), BF),
            pltpu.VMEM((R, 2, 16 * N, W), BF),
            pltpu.VMEM((2, 16 * N, W), BF),
            pltpu.VMEM((F, 4 * C, W), BF),
            pltpu.VMEM((128, 128), F32),
            pltpu.VMEM((128, 128), BF),
            pltpu.VMEM((nf * ns, 128 // owners, 128), BF),
            pltpu.VMEM((2 * C, 12 * C), BF),
            pltpu.VMEM((2 * C, 12 * C), F32),
            dma((2,)), dma((2,)), dma((2,)), dma((2,)),
            dma((1,)), dma((1,)), dma((2,)), dma((2,)), dma((2,)), dma((2,)),
            dma((1,)), dma((1,)), dma((1,)), dma((1,)),
            pltpu.SemaphoreType.REGULAR((ns // 2,)),
            pltpu.VMEM((F, C * R, W), BF),
            pltpu.VMEM((F, C * R, W), BF),
            pltpu.VMEM((C, 9 * C), BF),
            pltpu.VMEM((N, C), F32),
            pltpu.VMEM((N, C), F32),
            pltpu.VMEM((1, C), F32),
            dma((7,)),
        ],
        compiler_params=pltpu.CompilerParams(
            collective_id=0, has_side_effects=True, vmem_limit_bytes=16 << 20),
    )(*map(in_hbm, (lightcone.reshape(F, C * R, W), cotangent.reshape(F, C * R, W), conv_weight,
                    in_proj.T, out_proj.T, skip_gain.reshape(1, C), decay)))
    dl, grad, din, dout, d_skip = pl.pallas_call(
        functools.partial(finish, scale),
        out_shape=(
            jax.ShapeDtypeStruct((F, C * R, W), BF),
            jax.ShapeDtypeStruct((C, 9 * C), F32),
            jax.ShapeDtypeStruct((N, C), F32),
            jax.ShapeDtypeStruct((N, C), F32),
            jax.ShapeDtypeStruct((1, C), F32),
        ),
        in_specs=[vm] * 4,
        out_specs=(hbm,) * 5,
        scratch_shapes=[
            pltpu.VMEM((C, 9 * C), F32), pltpu.VMEM((N, C), F32), pltpu.VMEM((N, C), F32),
            pltpu.VMEM((1, C), F32), pltpu.VMEM((128, 128), F32), dma((5,))],
        compiler_params=pltpu.CompilerParams(vmem_limit_bytes=8 << 20),
    )(dl, pay, in_proj.T, out_proj.T)
    return dl.reshape(F, C, R, W), grad, din.T, dout.T, d_skip.reshape(C)


def solution(mesh):
    return jax.shard_map(
        per_device,
        mesh=mesh,
        in_specs=(
            P(("replica", "freq"), None, "sky", None),
            P(("replica", "freq"), None, "sky", None),
            P(),
            P(),
            P(),
            P(),
            P("freq", None),
        ),
        out_specs=(
            P(("replica", "freq"), None, "sky", None),
            P("replica", None),
            P("replica", None),
            P("replica", None),
            P("replica"),
        ),
        check_vma=False,
    )
```

```python
import functools

import jax
import jax.numpy as jnp
from jax import lax
from jax.experimental import pallas as pl
from jax.experimental.pallas import tpu as pltpu
from jax.sharding import PartitionSpec as P

MESH = pl.DeviceIdType.MESH
BF = jnp.bfloat16
F32 = jnp.float32


def dot(a, b):
    return jnp.dot(a, b, preferred_element_type=F32)


def dot_nt(a, b):
    return lax.dot_general(a, b, (((1,), (1,)), ((), ())), preferred_element_type=F32)


def iota(shape, dim):
    return lax.broadcasted_iota(jnp.int32, shape, dim)


def kernel(nf, ns, x_hbm, cot_hbm, w_hbm, in_hbm, out_hbm, skip_hbm, dec_hbm,
           dl_ref, pay_out,
           xr, cg, dg, inp, p3, k4, pe, qs, kb, nb, mb, dm, own_d, adj, adj_bf, ab, ab_out, dr, pay, pay_bf, rs, aw, bw,
           halo_s, halo_r, dhalo_s, dhalo_r, dec_s, dec_r, cot_s, cot_r, ab_s, ab_r,
           rs_s, rs_r, ag_s, ag_r, relay,
           x_ref, cot_ref, w_ref, in_ref, out_ref, skip_ref, load):
    F = x_ref.shape[0]
    half = F * 16
    me = lax.axis_index("freq")
    sky = lax.axis_index("sky")
    core = lax.rem(me, 2)
    chip = me // 2
    chips = nf // 2
    sibling = me + 1 - 2 * core
    nxt = lax.rem(sky + 1, ns)
    prv = lax.rem(sky + ns - 1, ns)
    rows = rs.shape[1]
    owners = pay.shape[0] // rows
    here = sky * nf + me
    owner = sky * chips + chip
    owns = jnp.logical_and(core == 1, owner < owners)

    loads = [
        pltpu.make_async_copy(src, dst, load.at[i])
        for i, (src, dst) in enumerate((
            (cot_hbm, cot_ref), (dec_hbm, dg.at[core]), (x_hbm, x_ref), (w_hbm, w_ref),
            (in_hbm, in_ref), (out_hbm, out_ref), (skip_hbm, skip_ref)))
    ]
    for i in (2, 1, 0, 3, 4, 5, 6):
        loads[i].start()
    barrier = pltpu.get_barrier_semaphore()
    for d in range(1, nf):
        pl.semaphore_signal(barrier, inc=1, device_id={"freq": lax.rem(me + d, nf)}, device_id_type=MESH)
    for to in (nxt, prv):
        pl.semaphore_signal(barrier, inc=1, device_id={"sky": to}, device_id_type=MESH)

    def pass_on(stage):
        for to in (nxt, prv):
            pl.semaphore_signal(relay.at[stage], inc=1, device_id={"sky": to}, device_id_type=MESH)

    stages = ns // 2

    pr, pc = iota((64, 64), 0), iota((64, 64), 1)
    perm = (pc == 2 * lax.rem(pr, 32) + pr // 32).astype(F32).astype(BF)
    loads[2].wait()
    for f in range(F):
        xr[f, 32:96, :] = dot(perm, x_ref[f]).astype(BF)
    pl.semaphore_wait(barrier, nf - 1 + 2)

    def remote(src, dst, s, r, **where):
        return pltpu.make_async_remote_copy(
            src_ref=src, dst_ref=dst, send_sem=s, recv_sem=r, device_id=dict(where), device_id_type=MESH)

    first, last = chip == 0, chip == chips - 1

    def dec_copy(slot):
        return remote(dg.at[slot], dg.at[slot], dec_s.at[0], dec_r.at[0], freq=sibling)

    def cot_copy(slot, h):
        return remote(cg.at[slot, h], cg.at[slot, h], cot_s.at[h], cot_r.at[h], freq=sibling)

    def adj_copy():
        return remote(ab_out, ab.at[core], ab_s.at[0], ab_r.at[core], freq=jnp.maximum(me - 2, 0))

    def fwd_copy(slot):
        return remote(ab.at[slot], ab.at[slot], ab_s.at[1], ab_r.at[slot], freq=sibling)

    up = remote(xr.at[:, 64:96], xr.at[:, 0:32], halo_s.at[0], halo_r.at[0], sky=nxt)
    down = remote(xr.at[:, 32:64], xr.at[:, 96:128], halo_s.at[1], halo_r.at[1], sky=prv)
    up.start()
    down.start()
    loads[1].wait()
    dec_copy(core).start()
    loads[0].wait()
    for f in range(F):
        c2 = dot(perm, cot_ref[f]).astype(BF)
        for h in range(2):
            for hi in range(2):
                at = hi * half + f * 16
                cg[core, h, at:at + 16, :] = c2[h * 32 + hi * 16:h * 32 + hi * 16 + 16]

    @pl.when(core == 1)
    def _():
        cot_copy(core, 0).start()
        cot_copy(core, 1).start()

    @pl.when(jnp.logical_and(core == 0, jnp.logical_not(first)))
    def _():
        cot_copy(core, 1).start()

    pass_on(0)
    for i in (3, 4, 5, 6):
        loads[i].wait()

    W = x_ref.shape[2]

    low_row = lax.rem(iota((16, 128), 1), 16) == iota((16, 128), 0)
    low_col = iota((16, 256), 1) // 16 == iota((16, 256), 0)
    expand = low_col.astype(F32).astype(BF)
    r256, l256 = iota((256, 256), 0), iota((256, 256), 1)
    kept = r256 // 16 == lax.rem(l256, 16)

    def group(hi):
        return slice(hi * half, (hi + 1) * half)

    def decayed(to, slot, run):
        for g in range(F):
            run = run * dg[slot, g:g + 1, :]
            qs[g:g + 1, :] = run
        for hi in range(2):
            m = lax.dot_general(qs[:, hi * 256:(hi + 1) * 256].astype(BF), expand, (((0,), (0,)), ((), ())),
                                preferred_element_type=F32)
            mb[to, hi] = jnp.where(kept, m, 0.0).astype(BF)
        return run

    def diagonal(to, run):
        for hi in range(2):
            dm[to, hi] = jnp.where(r256 == l256, run[:, hi * 256:(hi + 1) * 256], 0.0).astype(BF)

    def take():
        fwd_copy(core).wait_recv()
        fwd_copy(core).start()

    dec_copy(1 - core).wait_recv()

    @pl.when(jnp.logical_not(first))
    def _():
        run = decayed(1, 0, jnp.ones((1, 512), F32))
        run = decayed(2, 1, run)
        cot_copy(1 - core, core).wait_recv()
        for hi in range(2):
            adj[0, hi] = dot(mb[1, hi], cg[0, core, group(hi)]) + dot(mb[2, hi], cg[1, core, group(hi)])

        @pl.when(jnp.logical_not(last))
        def _():
            diagonal(1, run)
            take()
            for hi in range(2):
                adj[0, hi] += dot(dm[1, hi], ab[core, hi])

        ab_out[...] = adj[0].astype(BF)
        adj_copy().start()

    @pl.when(last)
    def _():
        ab[...] = jnp.zeros_like(ab)

    spread = (iota((32, 512), 1) // 16 == iota((32, 512), 0)).astype(F32)
    io = jnp.dot(in_ref[...] * out_ref[...], spread, precision=lax.Precision.HIGHEST, preferred_element_type=F32)
    io = jnp.sum(jnp.where(lax.rem(iota((16, 512), 1), 16) == iota((16, 512), 0), io, 0.0), axis=0, keepdims=True)
    tr, tc = iota((32, 256), 0), iota((32, 256), 1)
    skips = jnp.where(tr == tc // 128 * 16 + lax.rem(tc, 16), 1.0, 0.0)
    skips = jnp.dot(skip_ref[...], skips, precision=lax.Precision.HIGHEST, preferred_element_type=F32)
    tr, tc = iota((512, 256), 0), iota((512, 256), 1)
    tile = (tr // 16 == tc // 128 * 16 + lax.rem(tc, 16)).astype(F32).astype(BF)

    fi = iota((F, 512), 0)
    v = jnp.zeros((F, 512), F32)
    for g in range(F):
        v = jnp.where(fi == g, 1.0, v * dg[core, g:g + 1, :])
        p3[g * F:(g + 1) * F, :] = v
    pe[...] = v * io
    kk = dot((p3[...] * io).astype(BF), tile)
    row16, lane16 = iota((F, 256), 0), lax.rem(iota((F, 256), 1), 128) // 16
    for G in range(2):
        k = jnp.where(row16 == lane16 + 8 * G, skips, 0.0)
        for j in range(8):
            at = (8 * G + j) * F
            k = k + jnp.where(lane16 == j, kk[at:at + F], 0.0)
        k4[G * F:(G + 1) * F, :] = k
    for hi in range(2):
        for f in range(F):
            for G in range(2):
                row = jnp.broadcast_to(k4[G * F + f:G * F + f + 1, hi * 128:(hi + 1) * 128], (16, 128))
                kb[hi, f * 16:(f + 1) * 16, G * 128:(G + 1) * 128] = jnp.where(low_row, row, 0.0).astype(BF)
            row = jnp.broadcast_to(pe[f:f + 1, hi * 256:(hi + 1) * 256], (16, 256))
            nb[hi, f * 16:(f + 1) * 16, :] = jnp.where(low_col, row, 0.0).astype(BF)

    def cells(slot, hi):
        return jnp.concatenate([cg[slot, 0, group(hi)], cg[slot, 1, group(hi)]], axis=1)

    for hi in range(2):
        d = dot(kb[hi], cells(core, hi))
        own_d[0, hi] = d[:, 0:128]
        own_d[1, hi] = d[:, 128:256]

    @pl.when(core == 0)
    def _():
        diagonal(0, decayed(0, 1, jnp.ones((1, 512), F32)))
        pl.when(first)(cot_copy(1, 0).wait_recv)
        cot_copy(1, 1).wait_recv()
        for hi in range(2):
            a = dot(mb[0, hi], cells(1, hi))
            adj[0, hi] = a[:, 0:128]
            adj[1, hi] = a[:, 128:256]

    kk, ll = iota((288, 384), 0), iota((288, 384), 1)
    for r in range(2):
        tap = lax.rem(ll, 128) // 32 - r
        pick = jnp.logical_and(kk == (tap * 3 + ll // 128) * 32 + lax.rem(ll, 32),
                               jnp.logical_and(tap >= 0, tap <= 2))
        aw[r * 32:(r + 1) * 32, :] = dot(w_ref[...], pick.astype(F32).astype(BF)).astype(BF)
    mm, kk = iota((64, 288), 0), iota((64, 288), 1)
    for k in range(3):
        for row in range(4):
            tap = lax.rem(mm, 2) + 2 - row
            pick = jnp.logical_and(kk == (tap * 3 + k) * 32 + mm // 2,
                                   jnp.logical_and(tap >= 0, tap <= 2))
            at = k * 128 + row * 32
            bw[:, at:at + 32] = dot_nt(pick.astype(F32).astype(BF), w_ref[...])

    dup = remote(dr.at[:, 64:96], dr.at[:, 0:32], dhalo_s.at[1], dhalo_r.at[1], sky=nxt)
    ddown = remote(dr.at[:, 32:64], dr.at[:, 96:128], dhalo_s.at[0], dhalo_r.at[0], sky=prv)

    def mix(h):
        @pl.when(core == 0)
        def _():
            for hi in range(2):
                adj_bf[h, hi] = (adj[h, hi] + dot(dm[0, hi], ab[h, hi])).astype(BF)

        @pl.when(core == 1)
        def _():
            adj_bf[h] = ab[h]

        for hi in range(2):
            d = (own_d[h, hi] + dot(nb[hi], adj_bf[h, hi])).astype(BF)
            at = pl.multiple_of(32 + 32 * h + 16 * hi, 16)
            for f in range(F):
                dr[f, pl.ds(at, 16), :] = d[f * 16:(f + 1) * 16]

    for stage in range(1, stages):
        pl.semaphore_wait(relay.at[stage - 1], 2)
        pass_on(stage)

    pl.when(first)(take)
    mix(core)
    pl.when(core == 0)(ddown.start)
    pl.when(core == 1)(dup.start)
    pl.when(jnp.logical_not(last))(fwd_copy(1 - core).wait_recv)
    mix(1 - core)
    up.wait_recv()
    down.wait_recv()
    for f in range(F):
        x = xr[f]
        full = jnp.concatenate([pltpu.roll(x, 1, 1), x, pltpu.roll(x, W - 1, 1)], axis=0)
        got = dot(aw[...], full).astype(BF)
        for r in range(2):
            for hi in range(2):
                inp[hi, f * 16:(f + 1) * 16, r * 128:(r + 1) * 128] = got[r * 32 + hi * 16:r * 32 + hi * 16 + 16]

    same = lax.rem(r256, 16) == lax.rem(l256, 16)
    widen = (lax.rem(r256, 16) == l256 // 16).astype(F32).astype(BF)
    now = r256 // 16 == lax.rem(r256, 16)
    block_of = l256[0:16] // 16
    sums = []
    for hi in range(2):
        gram = jnp.where(same, dot_nt(inp[hi], cells(core, hi)), 0.0).astype(BF)
        rows_f = dot(expand, gram)
        stack = jnp.concatenate([jnp.where(block_of == g, rows_f, 0.0) for g in range(F)], axis=0).astype(BF)
        pairs = dot(stack, widen)
        sums.append(jnp.sum((pairs * p3[:, hi * 256:(hi + 1) * 256]).reshape(F * F // 8, 8, 256), axis=0))
        skip = jnp.sum(jnp.where(now, pairs, 0.0), axis=0, keepdims=True)
        for k in range(2):
            pay[100 + 2 * hi + k:101 + 2 * hi + k, :] = skip[:, k * 128:(k + 1) * 128]
    for hi in range(2):
        gram = dot_nt(inp[hi], jnp.concatenate([adj_bf[0, hi], adj_bf[1, hi]], axis=1))
        total = sums[hi]
        for f in range(F):
            rows_f = jnp.where(low_col, gram[f * 16:(f + 1) * 16], 0.0)
            at = (F - 1) * F + f
            total = total + (rows_f[0:8] + rows_f[8:16]) * p3[at:at + 1, hi * 256:(hi + 1) * 256]
        t = jnp.sum(total, axis=0, keepdims=True)
        for k in range(2):
            pay[96 + 2 * hi + k:97 + 2 * hi + k, :] = t[:, k * 128:(k + 1) * 128]

    grad = jnp.zeros((192, 128), F32)
    for f in range(F):
        mid = dr[f, 32:96, :]
        full = jnp.concatenate([pltpu.roll(mid, W - 1, 1), mid, pltpu.roll(mid, 1, 1)], axis=0)
        grad = grad + dot_nt(full, xr[f])
    for k in range(3):
        top = grad[k * 64:k * 64 + 32, 0:96]
        low = grad[k * 64 + 32:k * 64 + 64, 32:128]
        pay[k * 32:(k + 1) * 32, 0:96] = top + low
        pay[k * 32:(k + 1) * 32, 96:128] = jnp.zeros((32, 32), F32)

    def part(ref, i):
        return ref.at[pl.ds(pl.multiple_of(i * rows, 16), rows)]

    def each_owner(do):
        def step(d, carry):
            i = lax.rem(owner + d, owners)

            @pl.when(jnp.logical_not(jnp.logical_and(owns, i == owner)))
            def _():
                do(remote(part(pay_bf, i), rs.at[here], rs_s.at[0], rs_r.at[0],
                          sky=i // chips, freq=lax.rem(i, chips) * 2 + 1))

            return carry

        lax.fori_loop(0, owners, step, 0, unroll=owners <= 8)

    def each_other(do):
        def step(d, carry):
            other = lax.rem(here + d, nf * ns)
            do(remote(part(pay_out, owner), part(pay_out, owner), ag_s.at[0], ag_r.at[0],
                      sky=other // nf, freq=lax.rem(other, nf)))
            return carry

        lax.fori_loop(1, nf * ns, step, 0, unroll=nf * ns <= 16)

    pay_bf[0:96, :] = pay[0:96, :].astype(BF)
    small = pay[96:104, :]
    high = small.astype(BF).astype(F32)
    pay_bf[96:112, :] = jnp.concatenate([high, small - high], axis=0).astype(BF)
    pay_bf[112:128, :] = jnp.zeros((16, 128), BF)
    pl.semaphore_wait(relay.at[stages - 1], 2)
    each_owner(lambda one: one.start())
    pl.when(core == 0)(dup.start)
    pl.when(core == 1)(ddown.start)
    @pl.when(owns)
    def _():
        at = pl.ds(pl.multiple_of(owner * rows, 16), rows)
        rs[here] = pay_bf[at, :]
        some = rs.at[0:nf * ns - 1]
        pltpu.make_async_copy(some, some, rs_r.at[0]).wait()
        total = jnp.sum(rs[...].astype(F32), axis=0)
        small = total[0:8] + total[8:16]
        high = small.astype(BF).astype(F32)
        pair = jnp.concatenate([high, small - high], axis=0)
        pay_out[at, :] = jnp.where(owner * rows == 96, pair, total).astype(BF)
        each_other(lambda one: one.start())

    dup.wait_recv()
    ddown.wait_recv()
    b = bw[...].astype(BF)
    for f in range(F):
        x = dr[f]
        full = jnp.concatenate([pltpu.roll(x, W - 1, 1), x, pltpu.roll(x, 1, 1)], axis=0)
        dl_ref[f] = dot(b, full).astype(BF)

    up.wait_send()
    down.wait_send()
    dup.wait_send()
    ddown.wait_send()
    dec_copy(core).wait_send()

    @pl.when(core == 1)
    def _():
        cot_copy(core, 0).wait_send()
        cot_copy(core, 1).wait_send()

    @pl.when(jnp.logical_and(core == 0, jnp.logical_not(first)))
    def _():
        cot_copy(core, 1).wait_send()

    pl.when(jnp.logical_not(first))(adj_copy().wait_send)
    pl.when(jnp.logical_not(last))(fwd_copy(core).wait_send)

    @pl.when(owns)
    def _():
        sent = pay_bf.at[0:128 - rows]
        pltpu.make_async_copy(sent, sent, rs_s.at[0]).wait()

    @pl.when(jnp.logical_not(owns))
    def _():
        pltpu.make_async_copy(pay_bf, pay_bf, rs_s.at[0]).wait()

    @pl.when(owns)
    def _():
        rest = pay_out.at[0:128 - rows]
        pltpu.make_async_copy(rest, rest, ag_r.at[0]).wait()

    @pl.when(jnp.logical_not(owns))
    def _():
        pltpu.make_async_copy(pay_out, pay_out, ag_r.at[0]).wait()

    @pl.when(owns)
    def _():
        sent = rs.at[0:nf * ns - 1]
        pltpu.make_async_copy(sent, sent, ag_s.at[0]).wait()


def finish(scale, dl_ref, pay_ref, in_ref, out_ref, dl_hbm, conv_hbm, din_hbm, dout_hbm, skip_hbm,
           conv_out, din_out, dout_out, skip_out, pay, sems):
    copies = [
        pltpu.make_async_copy(src, dst, sems.at[i])
        for i, (src, dst) in enumerate((
            (dl_ref, dl_hbm), (conv_out, conv_hbm), (din_out, din_hbm), (dout_out, dout_hbm), (skip_out, skip_hbm)))
    ]
    copies[0].start()
    pay[...] = pay_ref[...].astype(F32)
    pay[96:104, :] += pay[104:112, :]
    for dr in range(3):
        for k in range(3):
            at = (dr * 3 + k) * 32
            conv_out[:, at:at + 32] = pay[k * 32:(k + 1) * 32, dr * 32:(dr + 1) * 32] * scale
    copies[1].start()
    t = jnp.concatenate([pay[96 + k:97 + k, :] for k in range(4)], axis=1) * scale
    t = jnp.where(lax.rem(iota((16, 512), 1), 16) == iota((16, 512), 0), t, 0.0)
    join = (iota((512, 32), 0) // 16 == iota((512, 32), 1)).astype(F32)
    t = jnp.dot(t, join, precision=lax.Precision.HIGHEST, preferred_element_type=F32)
    din_out[...] = t * out_ref[...]
    dout_out[...] = t * in_ref[...]
    s = jnp.concatenate([pay[100 + k:101 + k, :] for k in range(4)], axis=1) * scale
    s = jnp.where(lax.rem(iota((1, 512), 1), 16) == 0, s, 0.0)
    skip_out[...] = jnp.dot(s, join, precision=lax.Precision.HIGHEST, preferred_element_type=F32)
    for one in copies[2:]:
        one.start()
    for one in copies:
        one.wait()


def in_hbm(x):
    return pltpu.with_memory_space_constraint(x, pltpu.MemorySpace.HBM)


def per_device(lightcone, cotangent, conv_weight, in_proj, out_proj, skip_gain, decay):
    F, C, R, W = lightcone.shape
    N = in_proj.shape[1]
    nf, ns = lax.axis_size("freq"), lax.axis_size("sky")
    scale = 1.0 / float(F * nf * R * ns * W) ** 0.5
    owners = min(nf // 2 * ns, 8)
    dma = pltpu.SemaphoreType.DMA
    vm = pl.BlockSpec(memory_space=pltpu.VMEM)
    hbm = pl.BlockSpec(memory_space=pltpu.MemorySpace.HBM)
    dl, pay = pl.pallas_call(
        functools.partial(kernel, nf, ns),
        out_shape=(
            jax.ShapeDtypeStruct((F, C * R, W), BF),
            jax.ShapeDtypeStruct((128, 128), BF),
        ),
        in_specs=[hbm] * 7,
        out_specs=(vm, vm),
        scratch_shapes=[
            pltpu.VMEM((F, 4 * C, W), BF),
            pltpu.VMEM((2, R, F * C, W), BF),
            pltpu.VMEM((2, F, C * N), F32),
            pltpu.VMEM((2, F * 16, R * W), BF),
            pltpu.VMEM((F * F, C * N), F32),
            pltpu.VMEM((2 * F, 256), F32),
            pltpu.VMEM((F, C * N), F32),
            pltpu.VMEM((F, C * N), F32),
            pltpu.VMEM((2, F * 16, F * 16), BF),
            pltpu.VMEM((2, F * 16, 16 * N), BF),
            pltpu.VMEM((3, 2, 16 * N, F * 16), BF),
            pltpu.VMEM((2, 2, 16 * N, 16 * N), BF),
            pltpu.VMEM((R, 2, F * 16, W), F32),
            pltpu.VMEM((R, 2, 16 * N, W), F32),
            pltpu.VMEM((R, 2, 16 * N, W), BF),
            pltpu.VMEM((R, 2, 16 * N, W), BF),
            pltpu.VMEM((2, 16 * N, W), BF),
            pltpu.VMEM((F, 4 * C, W), BF),
            pltpu.VMEM((128, 128), F32),
            pltpu.VMEM((128, 128), BF),
            pltpu.VMEM((nf * ns, 128 // owners, 128), BF),
            pltpu.VMEM((2 * C, 12 * C), BF),
            pltpu.VMEM((2 * C, 12 * C), F32),
            dma((2,)), dma((2,)), dma((2,)), dma((2,)),
            dma((1,)), dma((1,)), dma((2,)), dma((2,)), dma((2,)), dma((2,)),
            dma((1,)), dma((1,)), dma((1,)), dma((1,)),
            pltpu.SemaphoreType.REGULAR((ns // 2,)),
            pltpu.VMEM((F, C * R, W), BF),
            pltpu.VMEM((F, C * R, W), BF),
            pltpu.VMEM((C, 9 * C), BF),
            pltpu.VMEM((N, C), F32),
            pltpu.VMEM((N, C), F32),
            pltpu.VMEM((1, C), F32),
            dma((7,)),
        ],
        compiler_params=pltpu.CompilerParams(
            collective_id=0, has_side_effects=True, vmem_limit_bytes=16 << 20),
    )(*map(in_hbm, (lightcone.reshape(F, C * R, W), cotangent.reshape(F, C * R, W), conv_weight,
                    in_proj.T, out_proj.T, skip_gain.reshape(1, C), decay)))
    dl, grad, din, dout, d_skip = pl.pallas_call(
        functools.partial(finish, scale),
        out_shape=(
            jax.ShapeDtypeStruct((F, C * R, W), BF),
            jax.ShapeDtypeStruct((C, 9 * C), F32),
            jax.ShapeDtypeStruct((N, C), F32),
            jax.ShapeDtypeStruct((N, C), F32),
            jax.ShapeDtypeStruct((1, C), F32),
        ),
        in_specs=[vm] * 4,
        out_specs=(hbm,) * 5,
        scratch_shapes=[
            pltpu.VMEM((C, 9 * C), F32), pltpu.VMEM((N, C), F32), pltpu.VMEM((N, C), F32),
            pltpu.VMEM((1, C), F32), pltpu.VMEM((128, 128), F32), dma((5,))],
        compiler_params=pltpu.CompilerParams(vmem_limit_bytes=8 << 20),
    )(dl, pay, in_proj.T, out_proj.T)
    return dl.reshape(F, C, R, W), grad, din.T, dout.T, d_skip.reshape(C)


def solution(mesh):
    return jax.shard_map(
        per_device,
        mesh=mesh,
        in_specs=(
            P(("replica", "freq"), None, "sky", None),
            P(("replica", "freq"), None, "sky", None),
            P(),
            P(),
            P(),
            P(),
            P("freq", None),
        ),
        out_specs=(
            P(("replica", "freq"), None, "sky", None),
            P("replica", None),
            P("replica", None),
            P("replica", None),
            P("replica"),
        ),
        check_vma=False,
    )
```

```python
import functools

import jax
import jax.numpy as jnp
from jax import lax
from jax.experimental import pallas as pl
from jax.experimental.pallas import tpu as pltpu
from jax.sharding import PartitionSpec as P

MESH = pl.DeviceIdType.MESH
BF = jnp.bfloat16
F32 = jnp.float32


def dot(a, b):
    return jnp.dot(a, b, preferred_element_type=F32)


def dot_nt(a, b):
    return lax.dot_general(a, b, (((1,), (1,)), ((), ())), preferred_element_type=F32)


def iota(shape, dim):
    return lax.broadcasted_iota(jnp.int32, shape, dim)


def kernel(nf, ns, x_hbm, cot_hbm, w_hbm, in_hbm, out_hbm, skip_hbm, dec_hbm,
           dl_ref, pay_out,
           xr, cg, dg, inp, p3, k4, pe, qs, kb, nb, mb, dm, own_d, adj, adj_bf, ab, ab_out, dr, pay, pay_bf, rs, aw, own_in, bw,
           halo_s, halo_r, dhalo_s, dhalo_r, dec_s, dec_r, cot_s, cot_r, ab_s, ab_r,
           rs_s, rs_r, ag_s, ag_r, relay,
           x_ref, cot_ref, w_ref, in_ref, out_ref, skip_ref, load):
    F = x_ref.shape[0]
    half = F * 16
    me = lax.axis_index("freq")
    sky = lax.axis_index("sky")
    core = lax.rem(me, 2)
    chip = me // 2
    chips = nf // 2
    sibling = me + 1 - 2 * core
    nxt = lax.rem(sky + 1, ns)
    prv = lax.rem(sky + ns - 1, ns)
    rows = rs.shape[1]
    owners = pay_bf.shape[0] // rows
    here = sky * nf + me
    owner = sky * chips + chip
    owns = jnp.logical_and(core == 1, owner < owners)

    loads = [
        pltpu.make_async_copy(src, dst, load.at[i])
        for i, (src, dst) in enumerate((
            (cot_hbm, cot_ref), (dec_hbm, dg.at[core]), (x_hbm, x_ref), (w_hbm, w_ref),
            (in_hbm, in_ref), (out_hbm, out_ref), (skip_hbm, skip_ref)))
    ]
    for i in (2, 1, 0, 3, 4, 5, 6):
        loads[i].start()
    barrier = pltpu.get_barrier_semaphore()
    for d in range(1, nf):
        pl.semaphore_signal(barrier, inc=1, device_id={"freq": lax.rem(me + d, nf)}, device_id_type=MESH)
    for to in (nxt, prv):
        pl.semaphore_signal(barrier, inc=1, device_id={"sky": to}, device_id_type=MESH)

    def pass_on(stage):
        for to in (nxt, prv):
            pl.semaphore_signal(relay.at[stage], inc=1, device_id={"sky": to}, device_id_type=MESH)

    stages = ns // 2

    pr, pc = iota((64, 64), 0), iota((64, 64), 1)
    perm = (pc == 2 * lax.rem(pr, 32) + pr // 32).astype(F32).astype(BF)
    loads[2].wait()
    for f in range(F):
        xr[f, 32:96, :] = dot(perm, x_ref[f]).astype(BF)
    pl.semaphore_wait(barrier, nf - 1 + 2)

    def remote(src, dst, s, r, **where):
        return pltpu.make_async_remote_copy(
            src_ref=src, dst_ref=dst, send_sem=s, recv_sem=r, device_id=dict(where), device_id_type=MESH)

    first, last = chip == 0, chip == chips - 1

    def dec_copy(slot):
        return remote(dg.at[slot], dg.at[slot], dec_s.at[0], dec_r.at[0], freq=sibling)

    def cot_copy(slot, h):
        return remote(cg.at[slot, h], cg.at[slot, h], cot_s.at[h], cot_r.at[h], freq=sibling)

    def adj_copy():
        return remote(ab_out, ab.at[core], ab_s.at[0], ab_r.at[core], freq=jnp.maximum(me - 2, 0))

    def fwd_copy(slot):
        return remote(ab.at[slot], ab.at[slot], ab_s.at[1], ab_r.at[slot], freq=sibling)

    up = remote(xr.at[:, 64:96], xr.at[:, 0:32], halo_s.at[0], halo_r.at[0], sky=nxt)
    down = remote(xr.at[:, 32:64], xr.at[:, 96:128], halo_s.at[1], halo_r.at[1], sky=prv)
    up.start()
    down.start()
    loads[1].wait()
    dec_copy(core).start()
    loads[0].wait()
    for f in range(F):
        c2 = dot(perm, cot_ref[f]).astype(BF)
        for h in range(2):
            for hi in range(2):
                at = hi * half + f * 16
                cg[core, h, at:at + 16, :] = c2[h * 32 + hi * 16:h * 32 + hi * 16 + 16]

    @pl.when(core == 1)
    def _():
        cot_copy(core, 0).start()
        cot_copy(core, 1).start()

    @pl.when(jnp.logical_and(core == 0, jnp.logical_not(first)))
    def _():
        cot_copy(core, 1).start()

    pass_on(0)
    for i in (3, 4, 5, 6):
        loads[i].wait()

    W = x_ref.shape[2]

    low_row = lax.rem(iota((16, 128), 1), 16) == iota((16, 128), 0)
    low_col = iota((16, 256), 1) // 16 == iota((16, 256), 0)
    expand = low_col.astype(F32).astype(BF)
    r256, l256 = iota((256, 256), 0), iota((256, 256), 1)
    kept = r256 // 16 == lax.rem(l256, 16)

    def group(hi):
        return slice(hi * half, (hi + 1) * half)

    def decayed(to, slot, run):
        for g in range(F):
            run = run * dg[slot, g:g + 1, :]
            qs[g:g + 1, :] = run
        for hi in range(2):
            m = lax.dot_general(qs[:, hi * 256:(hi + 1) * 256].astype(BF), expand, (((0,), (0,)), ((), ())),
                                preferred_element_type=F32)
            mb[to, hi] = jnp.where(kept, m, 0.0).astype(BF)
        return run

    def diagonal(to, run):
        for hi in range(2):
            dm[to, hi] = jnp.where(r256 == l256, run[:, hi * 256:(hi + 1) * 256], 0.0).astype(BF)

    def take():
        fwd_copy(core).wait_recv()
        fwd_copy(core).start()

    dec_copy(1 - core).wait_recv()

    @pl.when(jnp.logical_not(first))
    def _():
        run = decayed(1, 0, jnp.ones((1, 512), F32))
        run = decayed(2, 1, run)
        cot_copy(1 - core, core).wait_recv()
        for hi in range(2):
            adj[0, hi] = dot(mb[1, hi], cg[0, core, group(hi)]) + dot(mb[2, hi], cg[1, core, group(hi)])

        @pl.when(jnp.logical_not(last))
        def _():
            diagonal(1, run)
            take()
            for hi in range(2):
                adj[0, hi] += dot(dm[1, hi], ab[core, hi])

        ab_out[...] = adj[0].astype(BF)
        adj_copy().start()

    @pl.when(last)
    def _():
        ab[...] = jnp.zeros_like(ab)

    spread = (iota((32, 512), 1) // 16 == iota((32, 512), 0)).astype(F32)
    io = jnp.dot(in_ref[...] * out_ref[...], spread, precision=lax.Precision.HIGHEST, preferred_element_type=F32)
    io = jnp.sum(jnp.where(lax.rem(iota((16, 512), 1), 16) == iota((16, 512), 0), io, 0.0), axis=0, keepdims=True)
    tr, tc = iota((32, 256), 0), iota((32, 256), 1)
    skips = jnp.where(tr == tc // 128 * 16 + lax.rem(tc, 16), 1.0, 0.0)
    skips = jnp.dot(skip_ref[...], skips, precision=lax.Precision.HIGHEST, preferred_element_type=F32)
    tr, tc = iota((512, 256), 0), iota((512, 256), 1)
    tile = (tr // 16 == tc // 128 * 16 + lax.rem(tc, 16)).astype(F32).astype(BF)

    fi = iota((F, 512), 0)
    v = jnp.zeros((F, 512), F32)
    for g in range(F):
        v = jnp.where(fi == g, 1.0, v * dg[core, g:g + 1, :])
        p3[g * F:(g + 1) * F, :] = v
    pe[...] = v * io
    kk = dot((p3[...] * io).astype(BF), tile)
    row16, lane16 = iota((F, 256), 0), lax.rem(iota((F, 256), 1), 128) // 16
    for G in range(2):
        k = jnp.where(row16 == lane16 + 8 * G, skips, 0.0)
        for j in range(8):
            at = (8 * G + j) * F
            k = k + jnp.where(lane16 == j, kk[at:at + F], 0.0)
        k4[G * F:(G + 1) * F, :] = k
    for hi in range(2):
        for f in range(F):
            for G in range(2):
                row = jnp.broadcast_to(k4[G * F + f:G * F + f + 1, hi * 128:(hi + 1) * 128], (16, 128))
                kb[hi, f * 16:(f + 1) * 16, G * 128:(G + 1) * 128] = jnp.where(low_row, row, 0.0).astype(BF)
            row = jnp.broadcast_to(pe[f:f + 1, hi * 256:(hi + 1) * 256], (16, 256))
            nb[hi, f * 16:(f + 1) * 16, :] = jnp.where(low_col, row, 0.0).astype(BF)

    def cells(slot, hi):
        return jnp.concatenate([cg[slot, 0, group(hi)], cg[slot, 1, group(hi)]], axis=1)

    for hi in range(2):
        d = dot(kb[hi], cells(core, hi))
        own_d[0, hi] = d[:, 0:128]
        own_d[1, hi] = d[:, 128:256]

    @pl.when(core == 0)
    def _():
        diagonal(0, decayed(0, 1, jnp.ones((1, 512), F32)))
        pl.when(first)(cot_copy(1, 0).wait_recv)
        cot_copy(1, 1).wait_recv()
        for hi in range(2):
            a = dot(mb[0, hi], cells(1, hi))
            adj[0, hi] = a[:, 0:128]
            adj[1, hi] = a[:, 128:256]

    kk, ll = iota((288, 192), 0), iota((288, 192), 1)
    for part in range(2):
        pos = lax.rem(ll, 64) // 32
        pos = 3 * pos if part else 1 + pos
        for r in range(2):
            tap = pos - r
            pick = jnp.logical_and(kk == (tap * 3 + ll // 64) * 32 + lax.rem(ll, 32),
                                   jnp.logical_and(tap >= 0, tap <= 2))
            aw[part, r * 32:(r + 1) * 32, :] = dot(w_ref[...], pick.astype(F32).astype(BF)).astype(BF)
    mm, kk = iota((64, 288), 0), iota((64, 288), 1)
    for k in range(3):
        for row in range(4):
            tap = lax.rem(mm, 2) + 2 - row
            pick = jnp.logical_and(kk == (tap * 3 + k) * 32 + mm // 2,
                                   jnp.logical_and(tap >= 0, tap <= 2))
            at = k * 128 + row * 32
            bw[:, at:at + 32] = dot_nt(pick.astype(F32).astype(BF), w_ref[...])

    dup = remote(dr.at[:, 64:96], dr.at[:, 0:32], dhalo_s.at[1], dhalo_r.at[1], sky=nxt)
    ddown = remote(dr.at[:, 32:64], dr.at[:, 96:128], dhalo_s.at[0], dhalo_r.at[0], sky=prv)

    def mix(h):
        @pl.when(core == 0)
        def _():
            for hi in range(2):
                adj_bf[h, hi] = (adj[h, hi] + dot(dm[0, hi], ab[h, hi])).astype(BF)

        @pl.when(core == 1)
        def _():
            adj_bf[h] = ab[h]

        for hi in range(2):
            d = (own_d[h, hi] + dot(nb[hi], adj_bf[h, hi])).astype(BF)
            at = pl.multiple_of(32 + 32 * h + 16 * hi, 16)
            for f in range(F):
                dr[f, pl.ds(at, 16), :] = d[f * 16:(f + 1) * 16]

    for f in range(F):
        x = xr[f, 32:96]
        full = jnp.concatenate([pltpu.roll(x, 1, 1), x, pltpu.roll(x, W - 1, 1)], axis=0)
        own_in[f] = dot(aw[0], full)

    for stage in range(1, stages):
        pl.semaphore_wait(relay.at[stage - 1], 2)
        pass_on(stage)

    pl.when(first)(take)
    mix(core)
    pl.when(core == 0)(ddown.start)
    pl.when(core == 1)(dup.start)
    pl.when(jnp.logical_not(last))(fwd_copy(1 - core).wait_recv)
    mix(1 - core)
    up.wait_recv()
    down.wait_recv()
    for f in range(F):
        x = jnp.concatenate([xr[f, 0:32], xr[f, 96:128]], axis=0)
        full = jnp.concatenate([pltpu.roll(x, 1, 1), x, pltpu.roll(x, W - 1, 1)], axis=0)
        got = (own_in[f] + dot(aw[1], full)).astype(BF)
        for r in range(2):
            for hi in range(2):
                inp[hi, f * 16:(f + 1) * 16, r * 128:(r + 1) * 128] = got[r * 32 + hi * 16:r * 32 + hi * 16 + 16]

    same = lax.rem(r256, 16) == lax.rem(l256, 16)
    widen = (lax.rem(r256, 16) == l256 // 16).astype(F32).astype(BF)
    now = r256 // 16 == lax.rem(r256, 16)
    block_of = l256[0:16] // 16
    sums = []
    for hi in range(2):
        gram = jnp.where(same, dot_nt(inp[hi], cells(core, hi)), 0.0).astype(BF)
        rows_f = dot(expand, gram)
        stack = jnp.concatenate([jnp.where(block_of == g, rows_f, 0.0) for g in range(F)], axis=0).astype(BF)
        pairs = dot(stack, widen)
        sums.append(jnp.sum((pairs * p3[:, hi * 256:(hi + 1) * 256]).reshape(F * F // 8, 8, 256), axis=0))
        skip = jnp.sum(jnp.where(now, pairs, 0.0), axis=0, keepdims=True)
        for k in range(2):
            pay[100 + 2 * hi + k:101 + 2 * hi + k, :] = skip[:, k * 128:(k + 1) * 128]
    for hi in range(2):
        gram = dot_nt(inp[hi], jnp.concatenate([adj_bf[0, hi], adj_bf[1, hi]], axis=1))
        total = sums[hi]
        for f in range(F):
            rows_f = jnp.where(low_col, gram[f * 16:(f + 1) * 16], 0.0)
            at = (F - 1) * F + f
            total = total + (rows_f[0:8] + rows_f[8:16]) * p3[at:at + 1, hi * 256:(hi + 1) * 256]
        t = jnp.sum(total, axis=0, keepdims=True)
        for k in range(2):
            pay[96 + 2 * hi + k:97 + 2 * hi + k, :] = t[:, k * 128:(k + 1) * 128]

    grad = jnp.zeros((192, 128), F32)
    for f in range(F):
        mid = dr[f, 32:96, :]
        full = jnp.concatenate([pltpu.roll(mid, W - 1, 1), mid, pltpu.roll(mid, 1, 1)], axis=0)
        grad = grad + dot_nt(full, xr[f])
    for k in range(3):
        top = grad[k * 64:k * 64 + 32, 0:96]
        low = grad[k * 64 + 32:k * 64 + 64, 32:128]
        pay[k * 32:(k + 1) * 32, 0:96] = top + low
        pay[k * 32:(k + 1) * 32, 96:128] = jnp.zeros((32, 32), F32)

    def part(ref, i):
        return ref.at[pl.ds(pl.multiple_of(i * rows, 16), rows)]

    def each_owner(do):
        def step(d, carry):
            i = lax.rem(owner + d, owners)

            @pl.when(jnp.logical_not(jnp.logical_and(owns, i == owner)))
            def _():
                do(remote(part(pay_bf, i), rs.at[here], rs_s.at[0], rs_r.at[0],
                          sky=i // chips, freq=lax.rem(i, chips) * 2 + 1))

            return carry

        lax.fori_loop(0, owners, step, 0, unroll=owners <= 8)

    def each_other(do):
        def step(d, carry):
            other = lax.rem(here + d, nf * ns)
            do(remote(part(pay_out, owner), part(pay_out, owner), ag_s.at[0], ag_r.at[0],
                      sky=other // nf, freq=lax.rem(other, nf)))
            return carry

        lax.fori_loop(1, nf * ns, step, 0, unroll=nf * ns <= 16)

    pay_bf[0:96, :] = pay[0:96, :].astype(BF)
    small = pay[96:104, :]
    high = small.astype(BF).astype(F32)
    pay_bf[96:112, :] = jnp.concatenate([high, small - high], axis=0).astype(BF)
    pl.semaphore_wait(relay.at[stages - 1], 2)
    each_owner(lambda one: one.start())
    pl.when(core == 0)(dup.start)
    pl.when(core == 1)(ddown.start)
    @pl.when(owns)
    def _():
        at = pl.ds(pl.multiple_of(owner * rows, 16), rows)
        rs[here] = pay_bf[at, :]
        some = rs.at[0:nf * ns - 1]
        pltpu.make_async_copy(some, some, rs_r.at[0]).wait()
        total = jnp.sum(rs[...].astype(F32), axis=0)
        small = total[0:8] + total[8:16]
        high = small.astype(BF).astype(F32)
        pair = jnp.concatenate([high, small - high], axis=0)
        pay_out[at, :] = jnp.where(owner * rows == 96, pair, total).astype(BF)
        each_other(lambda one: one.start())

    dup.wait_recv()
    ddown.wait_recv()
    b = bw[...].astype(BF)
    for f in range(F):
        x = dr[f]
        full = jnp.concatenate([pltpu.roll(x, W - 1, 1), x, pltpu.roll(x, 1, 1)], axis=0)
        dl_ref[f] = dot(b, full).astype(BF)

    up.wait_send()
    down.wait_send()
    dup.wait_send()
    ddown.wait_send()
    dec_copy(core).wait_send()

    @pl.when(core == 1)
    def _():
        cot_copy(core, 0).wait_send()
        cot_copy(core, 1).wait_send()

    @pl.when(jnp.logical_and(core == 0, jnp.logical_not(first)))
    def _():
        cot_copy(core, 1).wait_send()

    pl.when(jnp.logical_not(first))(adj_copy().wait_send)
    pl.when(jnp.logical_not(last))(fwd_copy(core).wait_send)

    @pl.when(owns)
    def _():
        sent = pay_bf.at[0:pay_bf.shape[0] - rows]
        pltpu.make_async_copy(sent, sent, rs_s.at[0]).wait()

    @pl.when(jnp.logical_not(owns))
    def _():
        pltpu.make_async_copy(pay_bf, pay_bf, rs_s.at[0]).wait()

    @pl.when(owns)
    def _():
        rest = pay_out.at[0:pay_out.shape[0] - rows]
        pltpu.make_async_copy(rest, rest, ag_r.at[0]).wait()

    @pl.when(jnp.logical_not(owns))
    def _():
        pltpu.make_async_copy(pay_out, pay_out, ag_r.at[0]).wait()

    @pl.when(owns)
    def _():
        sent = rs.at[0:nf * ns - 1]
        pltpu.make_async_copy(sent, sent, ag_s.at[0]).wait()


def finish(scale, dl_ref, pay_ref, in_ref, out_ref, dl_hbm, conv_hbm, din_hbm, dout_hbm, skip_hbm,
           conv_out, din_out, dout_out, skip_out, pay, sems):
    copies = [
        pltpu.make_async_copy(src, dst, sems.at[i])
        for i, (src, dst) in enumerate((
            (dl_ref, dl_hbm), (conv_out, conv_hbm), (din_out, din_hbm), (dout_out, dout_hbm), (skip_out, skip_hbm)))
    ]
    copies[0].start()
    pay[...] = pay_ref[...].astype(F32)
    pay[96:104, :] += pay[104:112, :]
    for dr in range(3):
        for k in range(3):
            at = (dr * 3 + k) * 32
            conv_out[:, at:at + 32] = pay[k * 32:(k + 1) * 32, dr * 32:(dr + 1) * 32] * scale
    copies[1].start()
    t = jnp.concatenate([pay[96 + k:97 + k, :] for k in range(4)], axis=1) * scale
    t = jnp.where(lax.rem(iota((16, 512), 1), 16) == iota((16, 512), 0), t, 0.0)
    join = (iota((512, 32), 0) // 16 == iota((512, 32), 1)).astype(F32)
    t = jnp.dot(t, join, precision=lax.Precision.HIGHEST, preferred_element_type=F32)
    din_out[...] = t * out_ref[...]
    dout_out[...] = t * in_ref[...]
    s = jnp.concatenate([pay[100 + k:101 + k, :] for k in range(4)], axis=1) * scale
    s = jnp.where(lax.rem(iota((1, 512), 1), 16) == 0, s, 0.0)
    skip_out[...] = jnp.dot(s, join, precision=lax.Precision.HIGHEST, preferred_element_type=F32)
    for one in copies[2:]:
        one.start()
    for one in copies:
        one.wait()


def in_hbm(x):
    return pltpu.with_memory_space_constraint(x, pltpu.MemorySpace.HBM)


def per_device(lightcone, cotangent, conv_weight, in_proj, out_proj, skip_gain, decay):
    F, C, R, W = lightcone.shape
    N = in_proj.shape[1]
    nf, ns = lax.axis_size("freq"), lax.axis_size("sky")
    scale = 1.0 / float(F * nf * R * ns * W) ** 0.5
    owners = min(nf // 2 * ns, 7)
    dma = pltpu.SemaphoreType.DMA
    vm = pl.BlockSpec(memory_space=pltpu.VMEM)
    hbm = pl.BlockSpec(memory_space=pltpu.MemorySpace.HBM)
    dl, pay = pl.pallas_call(
        functools.partial(kernel, nf, ns),
        out_shape=(
            jax.ShapeDtypeStruct((F, C * R, W), BF),
            jax.ShapeDtypeStruct((112, 128), BF),
        ),
        in_specs=[hbm] * 7,
        out_specs=(vm, vm),
        scratch_shapes=[
            pltpu.VMEM((F, 4 * C, W), BF),
            pltpu.VMEM((2, R, F * C, W), BF),
            pltpu.VMEM((2, F, C * N), F32),
            pltpu.VMEM((2, F * 16, R * W), BF),
            pltpu.VMEM((F * F, C * N), F32),
            pltpu.VMEM((2 * F, 256), F32),
            pltpu.VMEM((F, C * N), F32),
            pltpu.VMEM((F, C * N), F32),
            pltpu.VMEM((2, F * 16, F * 16), BF),
            pltpu.VMEM((2, F * 16, 16 * N), BF),
            pltpu.VMEM((3, 2, 16 * N, F * 16), BF),
            pltpu.VMEM((2, 2, 16 * N, 16 * N), BF),
            pltpu.VMEM((R, 2, F * 16, W), F32),
            pltpu.VMEM((R, 2, 16 * N, W), F32),
            pltpu.VMEM((R, 2, 16 * N, W), BF),
            pltpu.VMEM((R, 2, 16 * N, W), BF),
            pltpu.VMEM((2, 16 * N, W), BF),
            pltpu.VMEM((F, 4 * C, W), BF),
            pltpu.VMEM((128, 128), F32),
            pltpu.VMEM((112, 128), BF),
            pltpu.VMEM((nf * ns, 112 // owners, 128), BF),
            pltpu.VMEM((2, 2 * C, 6 * C), BF),
            pltpu.VMEM((F, 2 * C, W), F32),
            pltpu.VMEM((2 * C, 12 * C), F32),
            dma((2,)), dma((2,)), dma((2,)), dma((2,)),
            dma((1,)), dma((1,)), dma((2,)), dma((2,)), dma((2,)), dma((2,)),
            dma((1,)), dma((1,)), dma((1,)), dma((1,)),
            pltpu.SemaphoreType.REGULAR((ns // 2,)),
            pltpu.VMEM((F, C * R, W), BF),
            pltpu.VMEM((F, C * R, W), BF),
            pltpu.VMEM((C, 9 * C), BF),
            pltpu.VMEM((N, C), F32),
            pltpu.VMEM((N, C), F32),
            pltpu.VMEM((1, C), F32),
            dma((7,)),
        ],
        compiler_params=pltpu.CompilerParams(
            collective_id=0, has_side_effects=True, vmem_limit_bytes=16 << 20),
    )(*map(in_hbm, (lightcone.reshape(F, C * R, W), cotangent.reshape(F, C * R, W), conv_weight,
                    in_proj.T, out_proj.T, skip_gain.reshape(1, C), decay)))
    dl, grad, din, dout, d_skip = pl.pallas_call(
        functools.partial(finish, scale),
        out_shape=(
            jax.ShapeDtypeStruct((F, C * R, W), BF),
            jax.ShapeDtypeStruct((C, 9 * C), F32),
            jax.ShapeDtypeStruct((N, C), F32),
            jax.ShapeDtypeStruct((N, C), F32),
            jax.ShapeDtypeStruct((1, C), F32),
        ),
        in_specs=[vm] * 4,
        out_specs=(hbm,) * 5,
        scratch_shapes=[
            pltpu.VMEM((C, 9 * C), F32), pltpu.VMEM((N, C), F32), pltpu.VMEM((N, C), F32),
            pltpu.VMEM((1, C), F32), pltpu.VMEM((112, 128), F32), dma((5,))],
        compiler_params=pltpu.CompilerParams(vmem_limit_bytes=8 << 20),
    )(dl, pay, in_proj.T, out_proj.T)
    return dl.reshape(F, C, R, W), grad, din.T, dout.T, d_skip.reshape(C)


def solution(mesh):
    return jax.shard_map(
        per_device,
        mesh=mesh,
        in_specs=(
            P(("replica", "freq"), None, "sky", None),
            P(("replica", "freq"), None, "sky", None),
            P(),
            P(),
            P(),
            P(),
            P("freq", None),
        ),
        out_specs=(
            P(("replica", "freq"), None, "sky", None),
            P("replica", None),
            P("replica", None),
            P("replica", None),
            P("replica"),
        ),
        check_vma=False,
    )
```

```python
import functools

import jax
import jax.numpy as jnp
from jax import lax
from jax.experimental import pallas as pl
from jax.experimental.pallas import tpu as pltpu
from jax.sharding import PartitionSpec as P

MESH = pl.DeviceIdType.MESH
BF = jnp.bfloat16
F32 = jnp.float32


def dot(a, b):
    return jnp.dot(a, b, preferred_element_type=F32)


def dot_nt(a, b):
    return lax.dot_general(a, b, (((1,), (1,)), ((), ())), preferred_element_type=F32)


def iota(shape, dim):
    return lax.broadcasted_iota(jnp.int32, shape, dim)


def kernel(nf, ns, x_hbm, cot_hbm, w_hbm, in_hbm, out_hbm, skip_hbm, dec_hbm,
           dl_ref, pay_out,
           xr, cg, dg, inp, p3, k4, pe, qs, kb, nb, mb, dm, own_d, adj, adj_bf, ab, ab_out, dr, pay, pay_bf, rs, aw, own_in, bw,
           halo_s, halo_r, dhalo_s, dhalo_r, dec_s, dec_r, cot_s, cot_r, ab_s, ab_r,
           rs_s, rs_r, ag_s, ag_r, relay,
           x_ref, cot_ref, w_ref, in_ref, out_ref, skip_ref, load):
    F = x_ref.shape[0]
    half = F * 16
    me = lax.axis_index("freq")
    sky = lax.axis_index("sky")
    core = lax.rem(me, 2)
    chip = me // 2
    chips = nf // 2
    sibling = me + 1 - 2 * core
    nxt = lax.rem(sky + 1, ns)
    prv = lax.rem(sky + ns - 1, ns)
    rows = rs.shape[1]
    owners = pay_bf.shape[0] // rows
    here = sky * nf + me
    owner = sky * chips + chip
    owns = jnp.logical_and(core == 1, owner < owners)

    loads = [
        pltpu.make_async_copy(src, dst, load.at[i])
        for i, (src, dst) in enumerate((
            (cot_hbm, cot_ref), (dec_hbm, dg.at[core]), (x_hbm, x_ref), (w_hbm, w_ref),
            (in_hbm, in_ref), (out_hbm, out_ref), (skip_hbm, skip_ref)))
    ]
    for i in (2, 1, 0, 3, 4, 5, 6):
        loads[i].start()
    barrier = pltpu.get_barrier_semaphore()
    for d in range(1, nf):
        pl.semaphore_signal(barrier, inc=1, device_id={"freq": lax.rem(me + d, nf)}, device_id_type=MESH)
    for to in (nxt, prv):
        pl.semaphore_signal(barrier, inc=1, device_id={"sky": to}, device_id_type=MESH)

    def pass_on(stage):
        for to in (nxt, prv):
            pl.semaphore_signal(relay.at[stage], inc=1, device_id={"sky": to}, device_id_type=MESH)

    stages = ns // 2

    pr, pc = iota((64, 64), 0), iota((64, 64), 1)
    perm = (pc == 2 * lax.rem(pr, 32) + pr // 32).astype(F32).astype(BF)
    loads[2].wait()
    for f in range(F):
        xr[f, 32:96, :] = dot(perm, x_ref[f]).astype(BF)
    pl.semaphore_wait(barrier, nf - 1 + 2)

    def remote(src, dst, s, r, **where):
        return pltpu.make_async_remote_copy(
            src_ref=src, dst_ref=dst, send_sem=s, recv_sem=r, device_id=dict(where), device_id_type=MESH)

    first, last = chip == 0, chip == chips - 1

    def dec_copy(slot):
        return remote(dg.at[slot], dg.at[slot], dec_s.at[0], dec_r.at[0], freq=sibling)

    def cot_copy(slot, h):
        return remote(cg.at[slot, h], cg.at[slot, h], cot_s.at[h], cot_r.at[h], freq=sibling)

    def adj_copy():
        return remote(ab_out, ab.at[core], ab_s.at[0], ab_r.at[core], freq=jnp.maximum(me - 2, 0))

    def fwd_copy(slot):
        return remote(ab.at[slot], ab.at[slot], ab_s.at[1], ab_r.at[slot], freq=sibling)

    up = remote(xr.at[:, 64:96], xr.at[:, 0:32], halo_s.at[0], halo_r.at[0], sky=nxt)
    down = remote(xr.at[:, 32:64], xr.at[:, 96:128], halo_s.at[1], halo_r.at[1], sky=prv)
    up.start()
    down.start()
    loads[1].wait()
    dec_copy(core).start()
    loads[0].wait()
    for f in range(F):
        c2 = dot(perm, cot_ref[f]).astype(BF)
        for h in range(2):
            for hi in range(2):
                at = hi * half + f * 16
                cg[core, h, at:at + 16, :] = c2[h * 32 + hi * 16:h * 32 + hi * 16 + 16]

    @pl.when(core == 1)
    def _():
        cot_copy(core, 0).start()
        cot_copy(core, 1).start()

    @pl.when(jnp.logical_and(core == 0, jnp.logical_not(first)))
    def _():
        cot_copy(core, 1).start()

    pass_on(0)
    for i in (3, 4, 5, 6):
        loads[i].wait()

    W = x_ref.shape[2]

    low_row = lax.rem(iota((16, 128), 1), 16) == iota((16, 128), 0)
    low_col = iota((16, 256), 1) // 16 == iota((16, 256), 0)
    expand = low_col.astype(F32).astype(BF)
    r256, l256 = iota((256, 256), 0), iota((256, 256), 1)
    kept = r256 // 16 == lax.rem(l256, 16)

    def group(hi):
        return slice(hi * half, (hi + 1) * half)

    def decayed(to, slot, run):
        for g in range(F):
            run = run * dg[slot, g:g + 1, :]
            qs[g:g + 1, :] = run
        for hi in range(2):
            m = lax.dot_general(qs[:, hi * 256:(hi + 1) * 256].astype(BF), expand, (((0,), (0,)), ((), ())),
                                preferred_element_type=F32)
            mb[to, hi] = jnp.where(kept, m, 0.0).astype(BF)
        return run

    def diagonal(to, run):
        for hi in range(2):
            dm[to, hi] = jnp.where(r256 == l256, run[:, hi * 256:(hi + 1) * 256], 0.0).astype(BF)

    def take():
        fwd_copy(core).wait_recv()
        fwd_copy(core).start()

    dec_copy(1 - core).wait_recv()

    @pl.when(jnp.logical_not(first))
    def _():
        run = decayed(1, 0, jnp.ones((1, 512), F32))
        run = decayed(2, 1, run)
        cot_copy(1 - core, core).wait_recv()
        for hi in range(2):
            adj[0, hi] = dot(mb[1, hi], cg[0, core, group(hi)]) + dot(mb[2, hi], cg[1, core, group(hi)])

        @pl.when(jnp.logical_not(last))
        def _():
            diagonal(1, run)
            take()
            for hi in range(2):
                adj[0, hi] += dot(dm[1, hi], ab[core, hi])

        ab_out[...] = adj[0].astype(BF)
        adj_copy().start()

    @pl.when(last)
    def _():
        ab[...] = jnp.zeros_like(ab)

    spread = (iota((32, 512), 1) // 16 == iota((32, 512), 0)).astype(F32)
    io = jnp.dot(in_ref[...] * out_ref[...], spread, precision=lax.Precision.HIGHEST, preferred_element_type=F32)
    io = jnp.sum(jnp.where(lax.rem(iota((16, 512), 1), 16) == iota((16, 512), 0), io, 0.0), axis=0, keepdims=True)
    tr, tc = iota((32, 256), 0), iota((32, 256), 1)
    skips = jnp.where(tr == tc // 128 * 16 + lax.rem(tc, 16), 1.0, 0.0)
    skips = jnp.dot(skip_ref[...], skips, precision=lax.Precision.HIGHEST, preferred_element_type=F32)
    tr, tc = iota((512, 256), 0), iota((512, 256), 1)
    tile = (tr // 16 == tc // 128 * 16 + lax.rem(tc, 16)).astype(F32).astype(BF)

    fi = iota((F, 512), 0)
    v = jnp.zeros((F, 512), F32)
    for g in range(F):
        v = jnp.where(fi == g, 1.0, v * dg[core, g:g + 1, :])
        p3[g * F:(g + 1) * F, :] = v
    pe[...] = v * io
    kk = dot((p3[...] * io).astype(BF), tile)
    row16, lane16 = iota((F, 256), 0), lax.rem(iota((F, 256), 1), 128) // 16
    for G in range(2):
        k = jnp.where(row16 == lane16 + 8 * G, skips, 0.0)
        for j in range(8):
            at = (8 * G + j) * F
            k = k + jnp.where(lane16 == j, kk[at:at + F], 0.0)
        k4[G * F:(G + 1) * F, :] = k
    for hi in range(2):
        for f in range(F):
            for G in range(2):
                row = jnp.broadcast_to(k4[G * F + f:G * F + f + 1, hi * 128:(hi + 1) * 128], (16, 128))
                kb[hi, f * 16:(f + 1) * 16, G * 128:(G + 1) * 128] = jnp.where(low_row, row, 0.0).astype(BF)
            row = jnp.broadcast_to(pe[f:f + 1, hi * 256:(hi + 1) * 256], (16, 256))
            nb[hi, f * 16:(f + 1) * 16, :] = jnp.where(low_col, row, 0.0).astype(BF)

    def cells(slot, hi):
        return jnp.concatenate([cg[slot, 0, group(hi)], cg[slot, 1, group(hi)]], axis=1)

    for hi in range(2):
        d = dot(kb[hi], cells(core, hi))
        own_d[0, hi] = d[:, 0:128]
        own_d[1, hi] = d[:, 128:256]

    @pl.when(core == 0)
    def _():
        diagonal(0, decayed(0, 1, jnp.ones((1, 512), F32)))
        pl.when(first)(cot_copy(1, 0).wait_recv)
        cot_copy(1, 1).wait_recv()
        for hi in range(2):
            a = dot(mb[0, hi], cells(1, hi))
            adj[0, hi] = a[:, 0:128]
            adj[1, hi] = a[:, 128:256]

    kk, ll = iota((288, 192), 0), iota((288, 192), 1)
    for part in range(2):
        pos = lax.rem(ll, 64) // 32
        pos = 3 * pos if part else 1 + pos
        for r in range(2):
            tap = pos - r
            pick = jnp.logical_and(kk == (tap * 3 + ll // 64) * 32 + lax.rem(ll, 32),
                                   jnp.logical_and(tap >= 0, tap <= 2))
            aw[part, r * 32:(r + 1) * 32, :] = dot(w_ref[...], pick.astype(F32).astype(BF)).astype(BF)
    mm, kk = iota((64, 288), 0), iota((64, 288), 1)
    for k in range(3):
        for row in range(4):
            tap = lax.rem(mm, 2) + 2 - row
            pick = jnp.logical_and(kk == (tap * 3 + k) * 32 + mm // 2,
                                   jnp.logical_and(tap >= 0, tap <= 2))
            at = k * 128 + row * 32
            bw[:, at:at + 32] = dot_nt(pick.astype(F32).astype(BF), w_ref[...])

    dup = remote(dr.at[:, 64:96], dr.at[:, 0:32], dhalo_s.at[1], dhalo_r.at[1], sky=nxt)
    ddown = remote(dr.at[:, 32:64], dr.at[:, 96:128], dhalo_s.at[0], dhalo_r.at[0], sky=prv)

    def mix(h):
        @pl.when(core == 0)
        def _():
            for hi in range(2):
                adj_bf[h, hi] = (adj[h, hi] + dot(dm[0, hi], ab[h, hi])).astype(BF)

        @pl.when(core == 1)
        def _():
            adj_bf[h] = ab[h]

        for hi in range(2):
            d = (own_d[h, hi] + dot(nb[hi], adj_bf[h, hi])).astype(BF)
            at = pl.multiple_of(32 + 32 * h + 16 * hi, 16)
            for f in range(F):
                dr[f, pl.ds(at, 16), :] = d[f * 16:(f + 1) * 16]

    for stage in range(1, stages):
        pl.semaphore_wait(relay.at[stage - 1], 2)
        pass_on(stage)

    pl.when(first)(take)
    mix(core)
    pl.when(core == 0)(ddown.start)
    pl.when(core == 1)(dup.start)
    for f in range(F):
        x = xr[f, 32:96]
        full = jnp.concatenate([pltpu.roll(x, 1, 1), x, pltpu.roll(x, W - 1, 1)], axis=0)
        own_in[f] = dot(aw[0], full)
    pl.when(jnp.logical_not(last))(fwd_copy(1 - core).wait_recv)
    mix(1 - core)
    up.wait_recv()
    down.wait_recv()
    for f in range(F):
        x = jnp.concatenate([xr[f, 0:32], xr[f, 96:128]], axis=0)
        full = jnp.concatenate([pltpu.roll(x, 1, 1), x, pltpu.roll(x, W - 1, 1)], axis=0)
        got = (own_in[f] + dot(aw[1], full)).astype(BF)
        for r in range(2):
            for hi in range(2):
                inp[hi, f * 16:(f + 1) * 16, r * 128:(r + 1) * 128] = got[r * 32 + hi * 16:r * 32 + hi * 16 + 16]

    same = lax.rem(r256, 16) == lax.rem(l256, 16)
    widen = (lax.rem(r256, 16) == l256 // 16).astype(F32).astype(BF)
    now = r256 // 16 == lax.rem(r256, 16)
    block_of = l256[0:16] // 16
    sums = []
    for hi in range(2):
        gram = jnp.where(same, dot_nt(inp[hi], cells(core, hi)), 0.0).astype(BF)
        rows_f = dot(expand, gram)
        stack = jnp.concatenate([jnp.where(block_of == g, rows_f, 0.0) for g in range(F)], axis=0).astype(BF)
        pairs = dot(stack, widen)
        sums.append(jnp.sum((pairs * p3[:, hi * 256:(hi + 1) * 256]).reshape(F * F // 8, 8, 256), axis=0))
        skip = jnp.sum(jnp.where(now, pairs, 0.0), axis=0, keepdims=True)
        for k in range(2):
            pay[100 + 2 * hi + k:101 + 2 * hi + k, :] = skip[:, k * 128:(k + 1) * 128]
    for hi in range(2):
        gram = dot_nt(inp[hi], jnp.concatenate([adj_bf[0, hi], adj_bf[1, hi]], axis=1))
        total = sums[hi]
        for f in range(F):
            rows_f = jnp.where(low_col, gram[f * 16:(f + 1) * 16], 0.0)
            at = (F - 1) * F + f
            total = total + (rows_f[0:8] + rows_f[8:16]) * p3[at:at + 1, hi * 256:(hi + 1) * 256]
        t = jnp.sum(total, axis=0, keepdims=True)
        for k in range(2):
            pay[96 + 2 * hi + k:97 + 2 * hi + k, :] = t[:, k * 128:(k + 1) * 128]

    grad = jnp.zeros((192, 128), F32)
    for f in range(F):
        mid = dr[f, 32:96, :]
        full = jnp.concatenate([pltpu.roll(mid, W - 1, 1), mid, pltpu.roll(mid, 1, 1)], axis=0)
        grad = grad + dot_nt(full, xr[f])
    for k in range(3):
        top = grad[k * 64:k * 64 + 32, 0:96]
        low = grad[k * 64 + 32:k * 64 + 64, 32:128]
        pay[k * 32:(k + 1) * 32, 0:96] = top + low
        pay[k * 32:(k + 1) * 32, 96:128] = jnp.zeros((32, 32), F32)

    def part(ref, i):
        return ref.at[pl.ds(pl.multiple_of(i * rows, 16), rows)]

    def each_owner(do):
        def step(d, carry):
            i = lax.rem(owner + d, owners)

            @pl.when(jnp.logical_not(jnp.logical_and(owns, i == owner)))
            def _():
                do(remote(part(pay_bf, i), rs.at[here], rs_s.at[0], rs_r.at[0],
                          sky=i // chips, freq=lax.rem(i, chips) * 2 + 1))

            return carry

        lax.fori_loop(0, owners, step, 0, unroll=owners <= 8)

    def each_other(do):
        def step(d, carry):
            other = lax.rem(here + d, nf * ns)
            do(remote(part(pay_out, owner), part(pay_out, owner), ag_s.at[0], ag_r.at[0],
                      sky=other // nf, freq=lax.rem(other, nf)))
            return carry

        lax.fori_loop(1, nf * ns, step, 0, unroll=nf * ns <= 16)

    pay_bf[0:96, :] = pay[0:96, :].astype(BF)
    small = pay[96:104, :]
    high = small.astype(BF).astype(F32)
    pay_bf[96:112, :] = jnp.concatenate([high, small - high], axis=0).astype(BF)
    pl.semaphore_wait(relay.at[stages - 1], 2)
    each_owner(lambda one: one.start())
    pl.when(core == 0)(dup.start)
    pl.when(core == 1)(ddown.start)
    @pl.when(owns)
    def _():
        at = pl.ds(pl.multiple_of(owner * rows, 16), rows)
        rs[here] = pay_bf[at, :]
        some = rs.at[0:nf * ns - 1]
        pltpu.make_async_copy(some, some, rs_r.at[0]).wait()
        total = jnp.sum(rs[...].astype(F32), axis=0)
        small = total[0:8] + total[8:16]
        high = small.astype(BF).astype(F32)
        pair = jnp.concatenate([high, small - high], axis=0)
        pay_out[at, :] = jnp.where(owner * rows == 96, pair, total).astype(BF)
        each_other(lambda one: one.start())

    dup.wait_recv()
    ddown.wait_recv()
    b = bw[...].astype(BF)
    for f in range(F):
        x = dr[f]
        full = jnp.concatenate([pltpu.roll(x, W - 1, 1), x, pltpu.roll(x, 1, 1)], axis=0)
        dl_ref[f] = dot(b, full).astype(BF)

    up.wait_send()
    down.wait_send()
    dup.wait_send()
    ddown.wait_send()
    dec_copy(core).wait_send()

    @pl.when(core == 1)
    def _():
        cot_copy(core, 0).wait_send()
        cot_copy(core, 1).wait_send()

    @pl.when(jnp.logical_and(core == 0, jnp.logical_not(first)))
    def _():
        cot_copy(core, 1).wait_send()

    pl.when(jnp.logical_not(first))(adj_copy().wait_send)
    pl.when(jnp.logical_not(last))(fwd_copy(core).wait_send)

    @pl.when(owns)
    def _():
        sent = pay_bf.at[0:pay_bf.shape[0] - rows]
        pltpu.make_async_copy(sent, sent, rs_s.at[0]).wait()

    @pl.when(jnp.logical_not(owns))
    def _():
        pltpu.make_async_copy(pay_bf, pay_bf, rs_s.at[0]).wait()

    @pl.when(owns)
    def _():
        rest = pay_out.at[0:pay_out.shape[0] - rows]
        pltpu.make_async_copy(rest, rest, ag_r.at[0]).wait()

    @pl.when(jnp.logical_not(owns))
    def _():
        pltpu.make_async_copy(pay_out, pay_out, ag_r.at[0]).wait()

    @pl.when(owns)
    def _():
        sent = rs.at[0:nf * ns - 1]
        pltpu.make_async_copy(sent, sent, ag_s.at[0]).wait()


def finish(scale, dl_ref, pay_ref, in_ref, out_ref, dl_hbm, conv_hbm, din_hbm, dout_hbm, skip_hbm,
           conv_out, din_out, dout_out, skip_out, pay, sems):
    copies = [
        pltpu.make_async_copy(src, dst, sems.at[i])
        for i, (src, dst) in enumerate((
            (dl_ref, dl_hbm), (conv_out, conv_hbm), (din_out, din_hbm), (dout_out, dout_hbm), (skip_out, skip_hbm)))
    ]
    copies[0].start()
    pay[...] = pay_ref[...].astype(F32)
    pay[96:104, :] += pay[104:112, :]
    for dr in range(3):
        for k in range(3):
            at = (dr * 3 + k) * 32
            conv_out[:, at:at + 32] = pay[k * 32:(k + 1) * 32, dr * 32:(dr + 1) * 32] * scale
    copies[1].start()
    t = jnp.concatenate([pay[96 + k:97 + k, :] for k in range(4)], axis=1) * scale
    t = jnp.where(lax.rem(iota((16, 512), 1), 16) == iota((16, 512), 0), t, 0.0)
    join = (iota((512, 32), 0) // 16 == iota((512, 32), 1)).astype(F32)
    t = jnp.dot(t, join, precision=lax.Precision.HIGHEST, preferred_element_type=F32)
    din_out[...] = t * out_ref[...]
    dout_out[...] = t * in_ref[...]
    s = jnp.concatenate([pay[100 + k:101 + k, :] for k in range(4)], axis=1) * scale
    s = jnp.where(lax.rem(iota((1, 512), 1), 16) == 0, s, 0.0)
    skip_out[...] = jnp.dot(s, join, precision=lax.Precision.HIGHEST, preferred_element_type=F32)
    for one in copies[2:]:
        one.start()
    for one in copies:
        one.wait()


def in_hbm(x):
    return pltpu.with_memory_space_constraint(x, pltpu.MemorySpace.HBM)


def per_device(lightcone, cotangent, conv_weight, in_proj, out_proj, skip_gain, decay):
    F, C, R, W = lightcone.shape
    N = in_proj.shape[1]
    nf, ns = lax.axis_size("freq"), lax.axis_size("sky")
    scale = 1.0 / float(F * nf * R * ns * W) ** 0.5
    owners = min(nf // 2 * ns, 7)
    dma = pltpu.SemaphoreType.DMA
    vm = pl.BlockSpec(memory_space=pltpu.VMEM)
    hbm = pl.BlockSpec(memory_space=pltpu.MemorySpace.HBM)
    dl, pay = pl.pallas_call(
        functools.partial(kernel, nf, ns),
        out_shape=(
            jax.ShapeDtypeStruct((F, C * R, W), BF),
            jax.ShapeDtypeStruct((112, 128), BF),
        ),
        in_specs=[hbm] * 7,
        out_specs=(vm, vm),
        scratch_shapes=[
            pltpu.VMEM((F, 4 * C, W), BF),
            pltpu.VMEM((2, R, F * C, W), BF),
            pltpu.VMEM((2, F, C * N), F32),
            pltpu.VMEM((2, F * 16, R * W), BF),
            pltpu.VMEM((F * F, C * N), F32),
            pltpu.VMEM((2 * F, 256), F32),
            pltpu.VMEM((F, C * N), F32),
            pltpu.VMEM((F, C * N), F32),
            pltpu.VMEM((2, F * 16, F * 16), BF),
            pltpu.VMEM((2, F * 16, 16 * N), BF),
            pltpu.VMEM((3, 2, 16 * N, F * 16), BF),
            pltpu.VMEM((2, 2, 16 * N, 16 * N), BF),
            pltpu.VMEM((R, 2, F * 16, W), F32),
            pltpu.VMEM((R, 2, 16 * N, W), F32),
            pltpu.VMEM((R, 2, 16 * N, W), BF),
            pltpu.VMEM((R, 2, 16 * N, W), BF),
            pltpu.VMEM((2, 16 * N, W), BF),
            pltpu.VMEM((F, 4 * C, W), BF),
            pltpu.VMEM((128, 128), F32),
            pltpu.VMEM((112, 128), BF),
            pltpu.VMEM((nf * ns, 112 // owners, 128), BF),
            pltpu.VMEM((2, 2 * C, 6 * C), BF),
            pltpu.VMEM((F, 2 * C, W), F32),
            pltpu.VMEM((2 * C, 12 * C), F32),
            dma((2,)), dma((2,)), dma((2,)), dma((2,)),
            dma((1,)), dma((1,)), dma((2,)), dma((2,)), dma((2,)), dma((2,)),
            dma((1,)), dma((1,)), dma((1,)), dma((1,)),
            pltpu.SemaphoreType.REGULAR((ns // 2,)),
            pltpu.VMEM((F, C * R, W), BF),
            pltpu.VMEM((F, C * R, W), BF),
            pltpu.VMEM((C, 9 * C), BF),
            pltpu.VMEM((N, C), F32),
            pltpu.VMEM((N, C), F32),
            pltpu.VMEM((1, C), F32),
            dma((7,)),
        ],
        compiler_params=pltpu.CompilerParams(
            collective_id=0, has_side_effects=True, vmem_limit_bytes=16 << 20),
    )(*map(in_hbm, (lightcone.reshape(F, C * R, W), cotangent.reshape(F, C * R, W), conv_weight,
                    in_proj.T, out_proj.T, skip_gain.reshape(1, C), decay)))
    dl, grad, din, dout, d_skip = pl.pallas_call(
        functools.partial(finish, scale),
        out_shape=(
            jax.ShapeDtypeStruct((F, C * R, W), BF),
            jax.ShapeDtypeStruct((C, 9 * C), F32),
            jax.ShapeDtypeStruct((N, C), F32),
            jax.ShapeDtypeStruct((N, C), F32),
            jax.ShapeDtypeStruct((1, C), F32),
        ),
        in_specs=[vm] * 4,
        out_specs=(hbm,) * 5,
        scratch_shapes=[
            pltpu.VMEM((C, 9 * C), F32), pltpu.VMEM((N, C), F32), pltpu.VMEM((N, C), F32),
            pltpu.VMEM((1, C), F32), pltpu.VMEM((112, 128), F32), dma((5,))],
        compiler_params=pltpu.CompilerParams(vmem_limit_bytes=8 << 20),
    )(dl, pay, in_proj.T, out_proj.T)
    return dl.reshape(F, C, R, W), grad, din.T, dout.T, d_skip.reshape(C)


def solution(mesh):
    return jax.shard_map(
        per_device,
        mesh=mesh,
        in_specs=(
            P(("replica", "freq"), None, "sky", None),
            P(("replica", "freq"), None, "sky", None),
            P(),
            P(),
            P(),
            P(),
            P("freq", None),
        ),
        out_specs=(
            P(("replica", "freq"), None, "sky", None),
            P("replica", None),
            P("replica", None),
            P("replica", None),
            P("replica"),
        ),
        check_vma=False,
    )
```
